128 devices in a mesh: sample: 8 (over x, y_hi), gz: 16 (over z, y_lo, core).
Axes of the slice: x: 4, y: 4 (y_hi: 2, y_lo: 2; y = y_hi * 2 + y_lo), z: 4, core: 2. Of those that a mesh axis runs over, the one named last changes fastest.
Arguments:
- cubes: bfloat16 [16, 64, 32, 1024], P('sample', 'gz'), may hold values from -6 to 6
- weight_a: bfloat16 [27, 2048], replicated, may hold values from -0.21875 to 0.21875
- weight_b: bfloat16 [27, 8192], replicated, may hold values from -0.15625 to 0.15625
- cotangent: bfloat16 [16, 16, 8, 1024], P('sample', 'gz'), may hold values from -6 to 6
Outputs:
- input_grad: bfloat16 [16, 64, 32, 1024], P('sample', 'gz')
- weight_grad_a: float32 [27, 2048], replicated
- weight_grad_b: float32 [27, 8192], replicated
The draws below stay inside these ranges and needn't reach their ends.
All inputs are finite; a program needn't handle non-finite values.
Results may differ from the reference program's by a relative error of at most 0.012.
Values may be sent and summed in bfloat16 or wider, within the bound.
A program may use at most 192 MiB of HBM per device.

```python
import jax
import jax.numpy as jnp
from jax import lax

C1 = 32
C2 = 64
C3 = 128
SIDE = 32
BATCH = 16
ZTOT = 64


def shard_levels(stream_key, shape, split, least, top_value):
    gain, own = 1.0, jax.random.fold_in(stream_key, 6)
    for dim, shards_of in split:
        draws = jnp.exp(jax.random.uniform(jax.random.fold_in(own, dim), (shards_of,), jnp.float32, least / len(split), top_value / len(split)))
        gain = gain * jnp.repeat(draws, shape[dim] // shards_of).reshape([-1 if axis == dim else 1 for axis in range(len(shape))])
    return gain


def scatter_about(own_key, shape, scale, most, split=(), kind=jnp.bfloat16):
    factor_of = shard_levels(own_key, shape, split, -0.22, 0.18) if split else 1.0
    drawn = jax.random.normal(own_key, shape, jnp.float32) * scale * factor_of
    return jnp.minimum(jnp.maximum(drawn, -most), most).astype(kind)


def setup_inputs(seed: int = 0) -> dict:
    splits = jax.random.split(jax.random.key(seed), 5)
    cubes = scatter_about(splits[0], (BATCH, ZTOT, SIDE, SIDE * C1), 1.0, 6.0, ((0, 8), (1, 16)))
    weight_a = scatter_about(splits[1], (27, C1 * C2), (27 * C1) ** -0.5, 0.21875)
    weight_b = scatter_about(splits[2], (27, C2 * C3), (27 * C2) ** -0.5, 0.15625)
    cotangent = scatter_about(splits[3], (BATCH, ZTOT // 4, SIDE // 4, SIDE // 4 * C3), 1.0, 6.0, ((0, 8), (1, 16)))
    return {"cubes": cubes, "weight_a": weight_a, "weight_b": weight_b, "cotangent": cotangent}


def activate(values):
    return values * jax.nn.sigmoid(values)


def slope(values):
    squash = jax.nn.sigmoid(values)
    return squash + values * squash * (1.0 - squash)


def rounded(values):
    return lax.optimization_barrier(values.astype(jnp.bfloat16)).astype(jnp.float32)


def correlate(volume, kernel):
    return lax.conv_general_dilated(volume[None], kernel, (1, 1, 1), ((1, 1), (1, 1), (1, 1)),
                                    dimension_numbers=("NDHWC", "DHWIO", "NDHWC"),
                                    precision=lax.Precision.HIGHEST)[0]


def shrink(values):
    planes, extent_y, extent_x, channels = values.shape
    return values.reshape(planes // 2, 2, extent_y // 2, 2, extent_x // 2, 2, channels).mean(axis=(1, 3, 5))


def spread(values):
    planes, extent_y, extent_x, channels = values.shape
    widened = jnp.broadcast_to(values[:, None, :, None, :, None, :], (planes, 2, extent_y, 2, extent_x, 2, channels))
    return widened.reshape(planes * 2, extent_y * 2, extent_x * 2, channels) * 0.125


def kernel_terms(volume, gradient):
    planes, extent_y, extent_x, channels = volume.shape
    padded = jnp.pad(volume, ((1, 1), (1, 1), (1, 1), (0, 0)))
    flat_grad = gradient.reshape(-1, gradient.shape[-1])
    partials = []
    for offset in range(27):
        shift_z, shift_y, shift_x = offset // 9, (offset // 3) % 3, offset % 3
        window = padded[shift_z:shift_z + planes, shift_y:shift_y + extent_y, shift_x:shift_x + extent_x]
        partials.append(lax.dot_general(window.reshape(-1, channels), flat_grad, (((0,), (0,)), ((), ())),
                                        precision=lax.Precision.HIGHEST))
    return jnp.stack(partials).reshape(27, -1)


def reference(cubes, weight_a, weight_b, cotangent):
    kernel_a = weight_a.astype(jnp.float32).reshape(3, 3, 3, C1, C2)
    kernel_b = weight_b.astype(jnp.float32).reshape(3, 3, 3, C2, C3)
    back_a = jnp.transpose(kernel_a[::-1, ::-1, ::-1], (0, 1, 2, 4, 3))
    back_b = jnp.transpose(kernel_b[::-1, ::-1, ::-1], (0, 1, 2, 4, 3))

    def one_cube(pair):
        sample_cube, upstream = pair
        volume = sample_cube.astype(jnp.float32).reshape(ZTOT, SIDE, SIDE, C1)
        pre_a = correlate(volume, kernel_a)
        pooled_a = rounded(shrink(activate(pre_a)))
        pre_b = correlate(pooled_a, kernel_b)
        coarse = upstream.astype(jnp.float32).reshape(ZTOT // 4, SIDE // 4, SIDE // 4, C3)
        grad_pre_b = rounded(spread(coarse) * slope(pre_b))
        term_b = kernel_terms(pooled_a, grad_pre_b)
        grad_pooled_a = correlate(grad_pre_b, back_b)
        grad_pre_a = rounded(spread(grad_pooled_a) * slope(pre_a))
        term_a = kernel_terms(volume, grad_pre_a)
        input_grad = correlate(grad_pre_a, back_a).astype(jnp.bfloat16).reshape(ZTOT, SIDE, SIDE * C1)
        return input_grad, term_a, term_b

    input_grad, terms_a, terms_b = lax.map(one_cube, (cubes, cotangent))
    weight_grad_a = jnp.sum(terms_a, axis=0) / BATCH
    weight_grad_b = jnp.sum(terms_b, axis=0) / BATCH
    return input_grad, weight_grad_a, weight_grad_b
```

```python
import functools

import jax
import jax.numpy as jnp
from jax import lax
from jax.experimental import pallas as pl
from jax.experimental.pallas import tpu as pltpu
from jax.sharding import PartitionSpec as P

C1, C2, C3 = 32, 64, 128
SIDE = 32
ZD = 4
CUBES = 2
BLOCKS = 9
F32, BF16 = jnp.float32, jnp.bfloat16
MESH = pl.DeviceIdType.MESH
ROWS_B = 1792
ROWS_A = 512


def iota(shape, dim):
    return lax.broadcasted_iota(jnp.int32, shape, dim)


def dot(a, b):
    return lax.dot_general(a, b, (((1,), (0,)), ((), ())), preferred_element_type=F32)


def dot_nt(a, b):
    return lax.dot_general(a, b, (((1,), (1,)), ((), ())), preferred_element_type=F32)


def rows_before(v):
    return jnp.where(iota(v.shape, 0) % 16 == 0, 0.0, pltpu.roll(v, 1, 0))


def rows_after(v):
    return jnp.where(iota(v.shape, 0) % 16 == 15, 0.0, pltpu.roll(v, v.shape[0] - 1, 0))


def lanes(start, size):
    return pl.ds(pl.multiple_of(start, 128), size)


def kernel(
    n_s, n_gz, x_ref, wa_ref, wb_ref, cot_ref, dx_ref, ga_ref, gb_ref,
    xa, ta, tb, tad, tbd, ds_a, pb, hb, ga, ht, gt, cs, da,
    xh, ph, hh, gh, sb, rb, eb, fb, sa, ra, ea, fa,
    halo_s, halo_r, rs_s, rs_r, ex_s, ex_r, ag_s, ag_r,
):
    me_s = lax.axis_index("sample")
    me_z = lax.axis_index("gz")
    low = lax.rem(me_z + n_gz - 1, n_gz)
    high = lax.rem(me_z + 1, n_gz)
    keep_low = (me_z > 0).astype(F32)
    keep_high = (me_z < n_gz - 1).astype(F32)

    barrier = pltpu.get_barrier_semaphore()

    @pl.loop(1, n_gz)
    def _(d):
        pl.semaphore_signal(barrier, inc=1, device_id=(me_s, lax.rem(me_z + d, n_gz)), device_id_type=MESH)

    @pl.loop(1, n_s)
    def _(d):
        pl.semaphore_signal(barrier, inc=1, device_id=(lax.rem(me_s + d, n_s), me_z), device_id_type=MESH)

    pl.semaphore_wait(barrier, n_gz + n_s - 2)

    def halo(stage, low_plane, high_plane, landing):
        pair = []
        for way, (src, peer) in enumerate(((high_plane, high), (low_plane, low))):
            copy = pltpu.make_async_remote_copy(
                src_ref=src, dst_ref=landing.at[way],
                send_sem=halo_s.at[stage, way], recv_sem=halo_r.at[stage, way],
                device_id=(me_s, peer), device_id_type=MESH,
            )
            copy.start()
            pair.append(copy)
        return pair

    halo_x = halo(0, x_ref.at[:, 0], x_ref.at[:, ZD - 1], xh)

    zero_a = jnp.zeros((C1, 128), BF16)
    zero_b = jnp.zeros((C2, 128), BF16)
    left = iota((C1, 128), 1) < C2

    def tap_a(zy, dx):
        if dx < -1 or dx > 1:
            return None
        return wa_ref[pl.ds(pl.multiple_of((zy * 3 + dx + 1) * C1, C1), C1), :]

    def tap_b(zy, dx):
        if dx < -1 or dx > 1:
            return zero_b
        return wb_ref[pl.ds(pl.multiple_of((zy * 3 + dx + 1) * C2, C2), C2), :]

    def two(zy, dx0, dx1):
        first, second = tap_a(zy, dx0), tap_a(zy, dx1)
        if first is None and second is None:
            return zero_a
        return jnp.where(left, zero_a if first is None else first, zero_a if second is None else second)

    @pl.loop(0, 9)
    def _(zy):
        base = zy * 256
        for p in range(8):
            for par in range(2):
                ta[pl.ds(pl.multiple_of(base + 32 * p, 32), 32), 128 * par:128 * par + 128] = two(zy, p - 2 - par, p - 4 - par)

    @pl.loop(0, 9)
    def _(zy):
        base = zy * 256
        for p in range(4):
            for q in range(2):
                tb[pl.ds(pl.multiple_of(base + 64 * p, 64), 64), 128 * q:128 * q + 128] = tap_b(zy, p - 1 - q)

    @pl.loop(0, 9)
    def _(s):
        for r in range(4):
            for p in range(6):
                tbd[64 * r:64 * r + 64, lanes(s * 768 + 128 * p, 128)] = tap_b(8 - s, r + 1 - p)

    @pl.loop(0, 9)
    def _(s):
        for r in range(8):
            for kk in range(3):
                for par in range(2):
                    dx = r + 2 - 4 * kk - par
                    tad[32 * r:32 * r + 32, lanes(s * 768 + 256 * kk + 128 * par, 128)] = two(8 - s, dx, dx - 2)

    spread_rows = (iota((64, SIDE), 1) == 2 * (iota((64, SIDE), 0) % 16) + iota((64, SIDE), 0) // 16 - 1).astype(BF16)
    spread_cot = (iota((16, 8), 0) // 2 == iota((16, 8), 1)).astype(BF16)
    natural = (iota((SIDE, SIDE), 1) == (iota((SIDE, SIDE), 0) % 2) * 16 + iota((SIDE, SIDE), 0) // 2).astype(BF16)
    edge = jnp.zeros((CUBES, ZD + 2, 64, 128), BF16)
    xa[:, :, :, 0:128] = edge
    xa[:, :, :, 1152:1280] = edge
    hb[:, :, :, :, 0:256] = jnp.zeros((CUBES, 4, 3, 16, 256), BF16)
    hb[:, :, :, :, 2304:2816] = jnp.zeros((CUBES, 4, 3, 16, 512), BF16)
    for b in range(CUBES):
        cs[b] = dot(spread_cot, cot_ref[b, 0]) * 0.125
        for z in range(ZD):
            xa[b, z + 1, :, 128:1152] = dot(spread_rows, x_ref[b, z]).astype(BF16)
    for copy in halo_x:
        copy.wait()
    for b in range(CUBES):
        xa[b, 0, :, 128:1152] = (dot(spread_rows, xh[0, b]) * keep_low).astype(BF16)
        xa[b, ZD + 1, :, 128:1152] = (dot(spread_rows, xh[1, b]) * keep_high).astype(BF16)

    @pl.loop(0, BLOCKS)
    def _(kk):
        window = [
            xa[:, dz:dz + ZD, 16 * dy:16 * dy + 32, lanes(128 * kk, 256)].reshape(256, 256)
            for dz in range(3) for dy in range(3)
        ]
        pre = dot(jnp.concatenate(window, axis=1), ta[...])
        place = 2 * kk - 1 + (iota((1, 128), 1) // C2)
        inside = ((place >= 0) & (place < SIDE // 2)).astype(F32) * 0.125
        s = 0.5 * jnp.tanh(0.5 * pre) + 0.5
        act = pre * s
        slope = s + act * (1.0 - s)
        ds_a[kk] = slope * jnp.concatenate([inside, inside], axis=1)
        act = (act[:, :128] + act[:, 128:]).reshape(CUBES, 2, 2, 2, 16, 128)
        pooled = (act[:, :, 0, 0] + act[:, :, 0, 1] + act[:, :, 1, 0] + act[:, :, 1, 1]).reshape(64, 128) * inside
        for dy, v in enumerate((rows_before(pooled), pooled, rows_after(pooled))):
            pb[:, 1:3, dy, :, lanes(128 * kk, 128)] = v.astype(BF16).reshape(CUBES, 2, 16, 128)

    halo_p = halo(1, pb.at[:, 1, 1], pb.at[:, 2, 1], ph)
    for copy in halo_p:
        copy.wait()
    for plane, way, keep in ((0, 0, keep_low), (3, 1, keep_high)):
        v = ph[way].astype(F32).reshape(32, 1152) * keep
        for dy, v in enumerate((rows_before(v), v, rows_after(v))):
            pb[:, plane, dy] = v.astype(BF16).reshape(CUBES, 16, 1152)

    @pl.loop(0, 2)
    def _(kc):
        stacks = []
        for i in range(4):
            stacks.append(jnp.concatenate([
                pb[:, dz:dz + 2, dy, :, lanes(512 * kc + 128 * i, 256)].reshape(64, 256)
                for dz in range(3) for dy in range(3)
            ], axis=1))
        pre = dot(jnp.concatenate(stacks, axis=0), tb[...])
        s = 0.5 * jnp.tanh(0.5 * pre) + 0.5
        slope = s + pre * s * (1.0 - s)
        grads = []
        for i in range(4):
            up = cs[:, :, lanes(512 * kc + 128 * i, 128)]
            up = jnp.concatenate([up, up], axis=2).reshape(CUBES, 1, 16, 256)
            h = (slope[64 * i:64 * i + 64].reshape(CUBES, 2, 16, 256) * up).reshape(64, 256)
            grads.append(h)
            for dy, v in enumerate((rows_before(h), h, rows_after(h))):
                hb[:, 1:3, dy, :, lanes(256 + 1024 * kc + 256 * i, 256)] = v.astype(BF16).reshape(CUBES, 2, 16, 256)
        ht[:, lanes(256 * kc, 256)] = jnp.concatenate(grads, axis=0).T.astype(BF16)

    halo_h = halo(2, hb.at[:, 1, 1, :, 256:2304], hb.at[:, 2, 1, :, 256:2304], hh)

    @pl.loop(0, 9)
    def _(zy):
        dz, dy = zy // 3, zy % 3
        window = jnp.concatenate([
            pb[:, pl.ds(dz, 2), dy, :, 128 * k:128 * k + 256].reshape(64, 256) for k in range(8)
        ], axis=0)
        full = dot(ht[...], window)
        diag = full[:128] + pltpu.roll(full[128:], 192, 1)
        sb[pl.ds(pl.multiple_of(zy * 192, 64), 192), :] = diag.T[:192].astype(BF16)

    sb[1728:ROWS_B, :] = jnp.zeros((ROWS_B - 1728, 128), BF16)

    def shard(ref, n, index):
        rows = ref.shape[0] // n
        return ref.at[pl.ds(pl.multiple_of(index * rows, 16), rows), :]

    def scatter_copy(which, send, land, d):
        peer = lax.rem(me_z + d, n_gz)
        return pltpu.make_async_remote_copy(
            src_ref=shard(send, n_gz, peer), dst_ref=land.at[me_z],
            send_sem=rs_s.at[which, d], recv_sem=rs_r.at[which, d],
            device_id=(me_s, peer), device_id_type=MESH,
        )

    def sample_copy(which, land, d):
        peer = lax.rem(me_s + d, n_s)
        return pltpu.make_async_remote_copy(
            src_ref=land.at[me_s], dst_ref=land.at[me_s],
            send_sem=ex_s.at[which, d], recv_sem=ex_r.at[which, d],
            device_id=(peer, me_z), device_id_type=MESH,
        )

    def gather_copy(which, full, d):
        peer = lax.rem(me_z + d, n_gz)
        return pltpu.make_async_remote_copy(
            src_ref=shard(full, n_gz, me_z), dst_ref=shard(full, n_gz, me_z),
            send_sem=ag_s.at[which, d], recv_sem=ag_r.at[which, d],
            device_id=(me_s, peer), device_id_type=MESH,
        )

    def start_all(make, n):
        @pl.loop(1, n)
        def _(d):
            make(d).start()

    def wait_all(make, n):
        @pl.loop(1, n)
        def _(d):
            make(d).wait()

    def scatter_start(which, send, land):
        start_all(functools.partial(scatter_copy, which, send, land), n_gz)

    def scatter_end(which, send, land, exchange):
        wait_all(functools.partial(scatter_copy, which, send, land), n_gz)
        rows = send.shape[0] // n_gz
        own = send[pl.ds(pl.multiple_of(me_z * rows, 16), rows), :]
        land[me_z] = own
        total = land[0].astype(F32)
        for t in range(1, n_gz):
            total = total + land[t].astype(F32)
        exchange[me_s] = total.astype(BF16)
        start_all(functools.partial(sample_copy, which, exchange), n_s)

    def exchange_end(which, exchange, full):
        wait_all(functools.partial(sample_copy, which, exchange), n_s)
        total = exchange[0].astype(F32)
        for t in range(1, n_s):
            total = total + exchange[t].astype(F32)
        rows = full.shape[0] // n_gz
        full[pl.ds(pl.multiple_of(me_z * rows, 16), rows), :] = (total * (1.0 / (CUBES * n_s))).astype(BF16)
        start_all(functools.partial(gather_copy, which, full), n_gz)

    scatter_start(0, sb, rb)

    for copy in halo_h:
        copy.wait()
    for plane, way, keep in ((0, 0, keep_low), (3, 1, keep_high)):
        v = hh[way].astype(F32).reshape(32, 2048) * keep
        for dy, v in enumerate((rows_before(v), v, rows_after(v))):
            hb[:, plane, dy, :, 256:2304] = v.astype(BF16).reshape(CUBES, 16, 2048)

    @pl.loop(0, 5)
    def _(j):
        gp = jnp.zeros((64, 256), F32)
        for sz in range(3):
            part = jnp.concatenate([
                hb[:, sz:sz + 2, sy, :, lanes(512 * j, 768)].reshape(64, 768) for sy in range(3)
            ], axis=1)
            gp = gp + dot_nt(part, tbd[:, 2304 * sz:2304 * sz + 2304])
        for half in range(2):
            @pl.when(2 * j + half < BLOCKS)
            def _():
                kk = 2 * j + half
                up = gp[:, 128 * half:128 * half + 128]
                up = jnp.concatenate([up, up], axis=1).reshape(CUBES, 2, 1, 1, 16, 256)
                g = ds_a[kk].reshape(CUBES, 2, 2, 2, 16, 256) * up
                gt[:, lanes(256 * kk, 256)] = g.reshape(256, 256).T.astype(BF16)
                g = g.reshape(CUBES, ZD, 2, 16, 256)
                even = g[:, :, 0].reshape(128, 256)
                odd = g[:, :, 1].reshape(128, 256)
                for group, v in enumerate((rows_before(odd), even, odd, rows_after(even))):
                    ga[:, 1:1 + ZD, 16 * group:16 * group + 16, lanes(256 * kk, 256)] = v.astype(BF16).reshape(CUBES, ZD, 16, 256)

    halo_g = halo(3, ga.at[:, 1, 16:48], ga.at[:, ZD, 16:48], gh)
    scatter_end(0, sb, rb, eb)

    @pl.loop(0, 9)
    def _(zy):
        dz, dy = zy // 3, zy % 3
        window = jnp.concatenate([
            xa[:, pl.ds(dz, ZD), pl.ds(pl.multiple_of(16 * dy, 16), 32), 128 * kk:128 * kk + 256].reshape(256, 256)
            for kk in range(BLOCKS)
        ], axis=0)
        full = dot(gt[...], window)
        total = jnp.zeros((64, 256), F32)
        for par in range(2):
            for pair in range(2):
                t = 2 * pair + par
                at = 128 * par + 64 * pair
                total = total + pltpu.roll(full[at:at + 64], 256 - 32 * (t + 1), 1)
        da[zy] = total[:, :128]

    da[9] = jnp.zeros((64, 128), F32)
    for i in range(5):
        both = jnp.concatenate([da[i], da[i + 5]], axis=0)
        sa[96 * i:96 * i + 96, :] = both.T[:96].astype(BF16)
    sa[480:ROWS_A, :] = jnp.zeros((ROWS_A - 480, 128), BF16)
    scatter_start(1, sa, ra)
    exchange_end(0, eb, fb)

    for copy in halo_g:
        copy.wait()
    for plane, way, keep in ((0, 0, keep_low), (ZD + 1, 1, keep_high)):
        even = gh[way, :, 0:16].astype(F32).reshape(32, 2304) * keep
        odd = gh[way, :, 16:32].astype(F32).reshape(32, 2304) * keep
        for group, v in enumerate((rows_before(odd), even, odd, rows_after(even))):
            ga[:, plane, 16 * group:16 * group + 16] = v.astype(BF16).reshape(CUBES, 16, 2304)

    def cubes_grad(j):
        total = jnp.zeros((256, 256), F32)
        for sz in range(3):
            part = jnp.concatenate([
                ga[:, sz:sz + ZD, 16 * sy:16 * sy + 32, lanes(512 * j, 768)].reshape(256, 768) for sy in range(3)
            ], axis=1)
            total = total + dot_nt(part, tad[:, 2304 * sz:2304 * sz + 2304])
        total = total.astype(BF16)
        for b in range(CUBES):
            for z in range(ZD):
                at = 32 * (ZD * b + z)
                dx_ref[b, z, :, lanes(256 * j, 256)] = dot(natural, total[at:at + 32]).astype(BF16)

    @pl.loop(0, 2)
    def _(j):
        cubes_grad(j)

    scatter_end(1, sa, ra, ea)

    @pl.loop(2, 4)
    def _(j):
        cubes_grad(j)

    exchange_end(1, ea, fa)
    wait_all(functools.partial(gather_copy, 0, fb), n_gz)
    gb_ref[...] = fb[0:1728].astype(F32)
    wait_all(functools.partial(gather_copy, 1, fa), n_gz)
    ga_ref[...] = fa[0:480].astype(F32)


def shards(n_s, n_gz, cubes, weight_a, weight_b, cotangent):
    wa = weight_a.reshape(27 * C1, C2)
    wa = jnp.concatenate([wa, wa], axis=1)
    wb = weight_b.reshape(27 * C2, C3)
    dma = pltpu.SemaphoreType.DMA
    vmem = pl.BlockSpec(memory_space=pltpu.VMEM)
    grad_x, grad_a, grad_b = pl.pallas_call(
        functools.partial(kernel, n_s, n_gz),
        out_shape=(
            jax.ShapeDtypeStruct((CUBES, ZD, SIDE, SIDE * C1), BF16),
            jax.ShapeDtypeStruct((480, 128), F32),
            jax.ShapeDtypeStruct((27 * C2, 128), F32),
        ),
        in_specs=[vmem] * 4,
        out_specs=(vmem,) * 3,
        scratch_shapes=[
            pltpu.VMEM((CUBES, ZD + 2, 64, 1280), BF16),
            pltpu.VMEM((2304, 256), BF16),
            pltpu.VMEM((2304, 256), BF16),
            pltpu.VMEM((256, 6912), BF16),
            pltpu.VMEM((256, 6912), BF16),
            pltpu.VMEM((BLOCKS, 256, 256), F32),
            pltpu.VMEM((CUBES, 4, 3, 16, 1152), BF16),
            pltpu.VMEM((CUBES, 4, 3, 16, 2816), BF16),
            pltpu.VMEM((CUBES, ZD + 2, 64, 2304), BF16),
            pltpu.VMEM((256, 512), BF16),
            pltpu.VMEM((256, 2304), BF16),
            pltpu.VMEM((CUBES, 16, 1024), F32),
            pltpu.VMEM((10, 64, 128), F32),
            pltpu.VMEM((2, CUBES, SIDE, 1024), BF16),
            pltpu.VMEM((2, CUBES, 16, 1152), BF16),
            pltpu.VMEM((2, CUBES, 16, 2048), BF16),
            pltpu.VMEM((2, CUBES, 32, 2304), BF16),
            pltpu.VMEM((ROWS_B, 128), BF16),
            pltpu.VMEM((n_gz, ROWS_B // n_gz, 128), BF16),
            pltpu.VMEM((n_s, ROWS_B // n_gz, 128), BF16),
            pltpu.VMEM((ROWS_B, 128), BF16),
            pltpu.VMEM((ROWS_A, 128), BF16),
            pltpu.VMEM((n_gz, ROWS_A // n_gz, 128), BF16),
            pltpu.VMEM((n_s, ROWS_A // n_gz, 128), BF16),
            pltpu.VMEM((ROWS_A, 128), BF16),
            dma((4, 2)), dma((4, 2)),
            dma((2, n_gz)), dma((2, n_gz)),
            dma((2, n_s)), dma((2, n_s)),
            dma((2, n_gz)), dma((2, n_gz)),
        ],
        compiler_params=pltpu.CompilerParams(
            collective_id=0, has_side_effects=True, vmem_limit_bytes=60 * 1024 * 1024
        ),
    )(cubes, wa, wb, cotangent)
    grad_a = jnp.concatenate([grad_a[:, :C2], grad_a[:384, C2:]], axis=0)
    return grad_x, grad_a.reshape(27, C1 * C2), grad_b.reshape(27, C2 * C3)


def solution(mesh):
    in_specs = (P("sample", "gz", None, None), P(), P(), P("sample", "gz", None, None))
    out_specs = (P("sample", "gz", None, None), P(), P())
    body = functools.partial(shards, mesh.shape["sample"], mesh.shape["gz"])
    return jax.shard_map(body, mesh=mesh, in_specs=in_specs, out_specs=out_specs, check_vma=False)
```

```python
import functools

import jax
import jax.numpy as jnp
from jax import lax
from jax.experimental import pallas as pl
from jax.experimental.pallas import tpu as pltpu
from jax.sharding import PartitionSpec as P

C1, C2, C3 = 32, 64, 128
SIDE = 32
ZD = 4
CUBES = 2
BLOCKS = 9
F32, BF16 = jnp.float32, jnp.bfloat16
MESH = pl.DeviceIdType.MESH
ROWS_B = 1792
ROWS_A = 512


def iota(shape, dim):
    return lax.broadcasted_iota(jnp.int32, shape, dim)


def dot(a, b):
    return lax.dot_general(a, b, (((1,), (0,)), ((), ())), preferred_element_type=F32)


def dot_nt(a, b):
    return lax.dot_general(a, b, (((1,), (1,)), ((), ())), preferred_element_type=F32)


def rows_before(v):
    return jnp.where(iota(v.shape, 0) % 16 == 0, 0.0, pltpu.roll(v, 1, 0))


def rows_after(v):
    return jnp.where(iota(v.shape, 0) % 16 == 15, 0.0, pltpu.roll(v, v.shape[0] - 1, 0))


def lanes(start, size):
    return pl.ds(pl.multiple_of(start, 128), size)


def kernel(
    n_s, n_gz, x_hbm, wa_hbm, wb_hbm, cot_hbm, dx_hbm, ga_hbm, gb_hbm,
    x_ref, wa_ref, wb_ref, cot_ref, dx_ref, ga_ref, gb_ref,
    wa32, wb32, xa, ta, tb, tad, tbd, ds_a, pre_s, gp_s, pb, hb, ga, ht, gt, cs, da,
    xh, ph, hh, gh, sb, rb, eb, fb, sa, ra, ea, fa,
    load_s, store_s, halo_s, halo_r, rs_s, rs_r, ex_s, ex_r, ag_s, ag_r,
):
    me_s = lax.axis_index("sample")
    me_z = lax.axis_index("gz")
    low = lax.rem(me_z + n_gz - 1, n_gz)
    high = lax.rem(me_z + 1, n_gz)
    keep_low = (me_z > 0).astype(F32)
    keep_high = (me_z < n_gz - 1).astype(F32)

    barrier = pltpu.get_barrier_semaphore()

    @pl.loop(1, n_gz)
    def _(d):
        pl.semaphore_signal(barrier, inc=1, device_id=(me_s, lax.rem(me_z + d, n_gz)), device_id_type=MESH)

    @pl.loop(1, n_s)
    def _(d):
        pl.semaphore_signal(barrier, inc=1, device_id=(lax.rem(me_s + d, n_s), me_z), device_id_type=MESH)

    loads = [
        pltpu.make_async_copy(src, dst, load_s.at[i])
        for i, (src, dst) in enumerate(((wa_hbm, wa_ref), (wb_hbm, wb_ref), (x_hbm, x_ref), (cot_hbm, cot_ref)))
    ]
    for load in loads:
        load.start()

    def halo(stage, low_plane, high_plane, landing):
        pair = []
        for way, (src, peer) in enumerate(((high_plane, high), (low_plane, low))):
            copy = pltpu.make_async_remote_copy(
                src_ref=src, dst_ref=landing.at[way],
                send_sem=halo_s.at[stage, way], recv_sem=halo_r.at[stage, way],
                device_id=(me_s, peer), device_id_type=MESH,
            )
            copy.start()
            pair.append(copy)
        return pair

    half = iota((27, 128), 1) < C2
    loads[0].wait()

    @pl.loop(0, C1 // 2)
    def _(m):
        v = wa_ref[:, lanes(128 * m, 128)].astype(F32)
        w = pltpu.roll(v, C2, 1)
        wa32[pl.ds(2 * m, 27, stride=C1), :] = jnp.where(half, v, w)
        wa32[pl.ds(2 * m + 1, 27, stride=C1), :] = jnp.where(half, w, v)

    loads[1].wait()

    @pl.loop(0, C2)
    def _(i):
        wb32[pl.ds(i, 27, stride=C2), :] = wb_ref[:, lanes(128 * i, 128)].astype(F32)

    pl.semaphore_wait(barrier, n_gz + n_s - 2)
    halo_x = halo(0, x_hbm.at[:, 0], x_hbm.at[:, ZD - 1], xh)

    zero_a = jnp.zeros((C1, 128), BF16)
    zero_b = jnp.zeros((C2, 128), BF16)
    left = iota((C1, 128), 1) < C2

    def taps_a(zy):
        at = pl.multiple_of(zy * 3 * C1, C1)
        full = wa32[pl.ds(at, 3 * C1), :].astype(BF16)
        taps = [full[C1 * i:C1 * i + C1] for i in range(3)]

        def two(dx0, dx1):
            first = taps[dx0 + 1] if -1 <= dx0 <= 1 else zero_a
            second = taps[dx1 + 1] if -1 <= dx1 <= 1 else zero_a
            if first is second:
                return zero_a
            return jnp.where(left, first, second)

        return two

    def taps_b(zy):
        at = pl.multiple_of(zy * 3 * C2, C2)
        full = wb32[pl.ds(at, 3 * C2), :].astype(BF16)
        taps = [full[C2 * i:C2 * i + C2] for i in range(3)]
        return lambda dx: taps[dx + 1] if -1 <= dx <= 1 else zero_b

    @pl.loop(0, 9)
    def _(zy):
        dz = zy // 3
        base = (jnp.where(dz == 2, 2, 1 - dz) * 3 + zy % 3) * 256
        two = taps_a(zy)
        for p in range(8):
            for par in range(2):
                ta[pl.ds(pl.multiple_of(base + 32 * p, 32), 32), 128 * par:128 * par + 128] = two(p - 2 - par, p - 4 - par)

    spread_rows = (iota((64, SIDE), 1) == 2 * (iota((64, SIDE), 0) % 16) + iota((64, SIDE), 0) // 16 - 1).astype(BF16)
    spread_cot = (iota((16, 8), 0) // 2 == iota((16, 8), 1)).astype(BF16)
    natural = (iota((SIDE, SIDE), 1) == (iota((SIDE, SIDE), 0) % 2) * 16 + iota((SIDE, SIDE), 0) // 2).astype(BF16)
    edge = jnp.zeros((CUBES, ZD + 2, 64, 128), BF16)
    xa[:, :, :, 0:128] = edge
    xa[:, :, :, 1152:1280] = edge
    loads[2].wait()
    for b in range(CUBES):
        for z in range(ZD):
            xa[b, z + 1, :, 128:1152] = dot(spread_rows, x_ref[b, z]).astype(BF16)

    def x_windows(kt, planes):
        return jnp.concatenate([jnp.concatenate([
            xa[:, dz:dz + ZD, 16 * dy:16 * dy + 32, lanes(384 * kt + 128 * i, 256)].reshape(256, 256)
            for dz in planes for dy in range(3)
        ], axis=1) for i in range(3)], axis=0)

    @pl.loop(0, 3)
    def _(kt):
        part = dot(x_windows(kt, (1,)), ta[0:768])
        for i in range(3):
            ds_a[3 * kt + i] = part[256 * i:256 * i + 256]

    loads[3].wait()
    for b in range(CUBES):
        cs[b] = dot(spread_cot, cot_ref[b, 0]) * 0.125
    hb[:, :, :, :, 0:256] = jnp.zeros((CUBES, 4, 3, 16, 256), BF16)
    hb[:, :, :, :, 2304:2816] = jnp.zeros((CUBES, 4, 3, 16, 512), BF16)
    for copy in halo_x:
        copy.wait()
    for b in range(CUBES):
        xa[b, 0, :, 128:1152] = (dot(spread_rows, xh[0, b]) * keep_low).astype(BF16)
        xa[b, ZD + 1, :, 128:1152] = (dot(spread_rows, xh[1, b]) * keep_high).astype(BF16)

    @pl.loop(0, 3)
    def _(kt):
        part = dot(x_windows(kt, (0, 2)), ta[768:2304])
        for i in range(3):
            kk = 3 * kt + i
            pre = part[256 * i:256 * i + 256] + ds_a[kk]
            place = 2 * kk - 1 + (iota((1, 128), 1) // C2)
            inside = ((place >= 0) & (place < SIDE // 2)).astype(F32) * 0.125
            s = 0.5 * jnp.tanh(0.5 * pre) + 0.5
            act = pre * s
            slope = s + act * (1.0 - s)
            ds_a[kk] = slope * jnp.concatenate([inside, inside], axis=1)
            act = (act[:, :128] + act[:, 128:]).reshape(CUBES, 2, 2, 2, 16, 128)
            pooled = (act[:, :, 0, 0] + act[:, :, 0, 1] + act[:, :, 1, 0] + act[:, :, 1, 1]).reshape(64, 128) * inside
            for dy, v in enumerate((rows_before(pooled), pooled, rows_after(pooled))):
                pb[:, 1:3, dy, :, lanes(128 * kk, 128)] = v.astype(BF16).reshape(CUBES, 2, 16, 128)

    halo_p = halo(1, pb.at[:, 1, 1], pb.at[:, 2, 1], ph)

    @pl.loop(0, 9)
    def _(zy):
        base = zy * 256
        tap = taps_b(zy)
        for p in range(4):
            for q in range(2):
                tb[pl.ds(pl.multiple_of(base + 64 * p, 64), 64), 128 * q:128 * q + 128] = tap(p - 1 - q)

    def p_windows(planes):
        return jnp.concatenate([jnp.concatenate([
            pb[:, z, dy, :, 128 * k:128 * k + 256].reshape(32, 256) for z in planes for dy in range(3)
        ], axis=1) for k in range(8)], axis=0)

    window = p_windows((1, 2))
    pre_s[0] = dot(window, tb[768:2304])
    pre_s[1] = dot(window, tb[0:1536])

    @pl.loop(0, 9)
    def _(s):
        tap = taps_b(8 - s)
        for r in range(4):
            for p in range(6):
                tbd[64 * r:64 * r + 64, lanes(s * 768 + 128 * p, 128)] = tap(r + 1 - p)

    @pl.loop(0, 9)
    def _(s):
        two = taps_a(8 - s)
        for r in range(8):
            for kk in range(3):
                for par in range(2):
                    dx = r + 2 - 4 * kk - par
                    tad[32 * r:32 * r + 32, lanes(s * 768 + 256 * kk + 128 * par, 128)] = two(dx, dx - 2)

    for copy in halo_p:
        copy.wait()
    for plane, way, keep in ((0, 0, keep_low), (3, 1, keep_high)):
        v = ph[way].astype(F32).reshape(32, 1152) * keep
        for dy, v in enumerate((rows_before(v), v, rows_after(v))):
            pb[:, plane, dy] = v.astype(BF16).reshape(CUBES, 16, 1152)

    for zp in range(2):
        pre = pre_s[zp] + dot(p_windows((3 * zp,)), tb[1536 * zp:1536 * zp + 768])
        s = 0.5 * jnp.tanh(0.5 * pre) + 0.5
        slope = s + pre * s * (1.0 - s)
        grads = []
        for k in range(8):
            up = cs[:, :, 128 * k:128 * k + 128].reshape(32, 128)
            h = slope[32 * k:32 * k + 32] * jnp.concatenate([up, up], axis=1)
            grads.append(h)
            for dy, v in enumerate((rows_before(h), h, rows_after(h))):
                hb[:, 1 + zp, dy, :, 256 + 256 * k:512 + 256 * k] = v.astype(BF16).reshape(CUBES, 16, 256)
        ht[:, 256 * zp:256 * zp + 256] = jnp.concatenate(grads, axis=0).T.astype(BF16)

    halo_h = halo(2, hb.at[:, 1, 1, :, 256:2304], hb.at[:, 2, 1, :, 256:2304], hh)

    @pl.loop(0, 3)
    def _(dz):
        window = jnp.concatenate([jnp.concatenate([
            pb[:, dz + zp, dy, :, 128 * k:128 * k + 256].reshape(32, 256) for zp in range(2) for k in range(8)
        ], axis=0) for dy in range(3)], axis=1)
        all_dy = dot(ht[...], window)
        for dy in range(3):
            full = all_dy[:, 256 * dy:256 * dy + 256]
            diag = full[:128] + pltpu.roll(full[128:], 192, 1)
            sb[pl.ds(pl.multiple_of(dz * 576 + dy * 192, 64), 192), :] = diag.T[:192].astype(BF16)

    sb[1728:ROWS_B, :] = jnp.zeros((ROWS_B - 1728, 128), BF16)

    def shard(ref, n, index):
        rows = ref.shape[0] // n
        return ref.at[pl.ds(pl.multiple_of(index * rows, 16), rows), :]

    def scatter_copy(which, send, land, d):
        peer = lax.rem(me_z + d, n_gz)
        return pltpu.make_async_remote_copy(
            src_ref=shard(send, n_gz, peer), dst_ref=land.at[me_z],
            send_sem=rs_s.at[which, d], recv_sem=rs_r.at[which, d],
            device_id=(me_s, peer), device_id_type=MESH,
        )

    def sample_copy(which, land, d):
        peer = lax.rem(me_s + d, n_s)
        return pltpu.make_async_remote_copy(
            src_ref=land.at[me_s], dst_ref=land.at[me_s],
            send_sem=ex_s.at[which, d], recv_sem=ex_r.at[which, d],
            device_id=(peer, me_z), device_id_type=MESH,
        )

    def gather_copy(which, full, d):
        peer = lax.rem(me_z + d, n_gz)
        return pltpu.make_async_remote_copy(
            src_ref=shard(full, n_gz, me_z), dst_ref=shard(full, n_gz, me_z),
            send_sem=ag_s.at[which, d], recv_sem=ag_r.at[which, d],
            device_id=(me_s, peer), device_id_type=MESH,
        )

    def start_all(make, n):
        @pl.loop(1, n)
        def _(d):
            make(d).start()

    def wait_all(make, n):
        @pl.loop(1, n)
        def _(d):
            make(d).wait()

    def scatter_start(which, send, land):
        start_all(functools.partial(scatter_copy, which, send, land), n_gz)

    def scatter_end(which, send, land, exchange):
        wait_all(functools.partial(scatter_copy, which, send, land), n_gz)
        rows = send.shape[0] // n_gz
        own = send[pl.ds(pl.multiple_of(me_z * rows, 16), rows), :]
        land[me_z] = own
        total = land[0].astype(F32)
        for t in range(1, n_gz):
            total = total + land[t].astype(F32)
        exchange[me_s] = total.astype(BF16)
        start_all(functools.partial(sample_copy, which, exchange), n_s)

    def exchange_end(which, exchange, full):
        wait_all(functools.partial(sample_copy, which, exchange), n_s)
        total = exchange[0].astype(F32)
        for t in range(1, n_s):
            total = total + exchange[t].astype(F32)
        rows = full.shape[0] // n_gz
        full[pl.ds(pl.multiple_of(me_z * rows, 16), rows), :] = (total * (1.0 / (CUBES * n_s))).astype(BF16)
        start_all(functools.partial(gather_copy, which, full), n_gz)

    scatter_start(0, sb, rb)

    def h_windows(planes):
        return jnp.concatenate([jnp.concatenate([
            hb[:, z, sy, :, 512 * j:512 * j + 768].reshape(32, 768) for z in planes for sy in range(3)
        ], axis=1) for j in range(5)], axis=0)

    window = h_windows((1, 2))
    gp_s[0] = dot_nt(window, tbd[:, 2304:6912])
    gp_s[1] = dot_nt(window, tbd[:, 0:4608])

    for copy in halo_h:
        copy.wait()
    for plane, way, keep in ((0, 0, keep_low), (3, 1, keep_high)):
        v = hh[way].astype(F32).reshape(32, 2048) * keep
        for dy, v in enumerate((rows_before(v), v, rows_after(v))):
            hb[:, plane, dy, :, 256:2304] = v.astype(BF16).reshape(CUBES, 16, 2048)

    for zp in range(2):
        gp_s[zp] = gp_s[zp] + dot_nt(h_windows((3 * zp,)), tbd[:, 4608 * zp:4608 * zp + 2304])

    @pl.loop(0, BLOCKS)
    def _(kk):
        up = gp_s[:, pl.ds(pl.multiple_of((kk // 2) * 32, 32), 32), lanes(128 * (kk % 2), 128)]
        up = jnp.concatenate([up, up], axis=2).reshape(2, CUBES, 16, 256)
        g = []
        for b in range(CUBES):
            for zp in range(2):
                g.append((ds_a[kk, 128 * b + 64 * zp:128 * b + 64 * zp + 64].reshape(4, 16, 256) * up[zp, b][None]).reshape(64, 256))
        g = jnp.concatenate(g, axis=0)
        gt[:, lanes(256 * kk, 256)] = g.T.astype(BF16)
        g = g.reshape(CUBES, ZD, 2, 16, 256)
        even = g[:, :, 0].reshape(128, 256)
        odd = g[:, :, 1].reshape(128, 256)
        for group, v in enumerate((rows_before(odd), even, odd, rows_after(even))):
            ga[:, 1:1 + ZD, 16 * group:16 * group + 16, lanes(256 * kk, 256)] = v.astype(BF16).reshape(CUBES, ZD, 16, 256)

    halo_g = halo(3, ga.at[:, 1, 16:48], ga.at[:, ZD, 16:48], gh)

    def terms_a(dz):
        window = jnp.concatenate([jnp.concatenate([
            xa[:, pl.ds(dz, ZD), 16 * dy:16 * dy + 32, 128 * kk:128 * kk + 256].reshape(256, 256)
            for kk in range(BLOCKS)
        ], axis=0) for dy in range(3)], axis=1)
        all_dy = dot(gt[...], window)
        for dy in range(3):
            full = all_dy[:, 256 * dy:256 * dy + 256]
            total = jnp.zeros((64, 256), F32)
            for par in range(2):
                for pair in range(2):
                    t = 2 * pair + par
                    at = 128 * par + 64 * pair
                    total = total + pltpu.roll(full[at:at + 64], 256 - 32 * (t + 1), 1)
            total = total[:, :128]
            da[pl.ds(pl.multiple_of(dz * 288 + dy * 96, 32), 96), :] = jnp.concatenate([total, total], axis=0).T[:96]

    @pl.loop(0, 2)
    def _(dz):
        terms_a(dz)

    scatter_end(0, sb, rb, eb)
    terms_a(2)
    half = iota((ROWS_A, 128), 1) < C2
    da[864:1024, :] = jnp.zeros((160, 128), F32)
    sa[...] = jnp.where(half, da[0:512], da[512:1024]).astype(BF16)
    scatter_start(1, sa, ra)

    for copy in halo_g:
        copy.wait()
    for plane, way, keep in ((0, 0, keep_low), (ZD + 1, 1, keep_high)):
        even = gh[way, :, 0:16].astype(F32).reshape(32, 2304) * keep
        odd = gh[way, :, 16:32].astype(F32).reshape(32, 2304) * keep
        for group, v in enumerate((rows_before(odd), even, odd, rows_after(even))):
            ga[:, plane, 16 * group:16 * group + 16] = v.astype(BF16).reshape(CUBES, 16, 2304)

    exchange_end(0, eb, fb)

    stores = []

    def store(src, dst):
        copy = pltpu.make_async_copy(src, dst, store_s.at[len(stores)])
        copy.start()
        stores.append(copy)

    def cubes_grad(jj):
        part = jnp.concatenate([jnp.concatenate([
            ga[:, sz:sz + ZD, 16 * sy:16 * sy + 32, 1024 * jj + 512 * i:1024 * jj + 512 * i + 768].reshape(256, 768)
            for sz in range(3) for sy in range(3)
        ], axis=1) for i in range(2)], axis=0)
        total = dot_nt(part, tad[...]).astype(BF16)
        for i in range(2):
            for b in range(CUBES):
                for z in range(ZD):
                    at = 256 * i + 32 * (ZD * b + z)
                    dx_ref[b, z, :, 512 * jj + 256 * i:512 * jj + 256 * i + 256] = dot(natural, total[at:at + 32]).astype(BF16)

    cubes_grad(0)
    scatter_end(1, sa, ra, ea)
    cubes_grad(1)
    store(dx_ref, dx_hbm)
    exchange_end(1, ea, fa)

    wait_all(functools.partial(gather_copy, 0, fb), n_gz)
    wb32[...] = fb[0:1728].astype(F32)

    @pl.loop(0, C2)
    def _(i):
        gb_ref[:, lanes(128 * i, 128)] = wb32[pl.ds(i, 27, stride=C2), :]

    store(gb_ref, gb_hbm)
    wait_all(functools.partial(gather_copy, 1, fa), n_gz)
    wa32[0:ROWS_A] = fa[...].astype(F32)
    first = iota((16, 128), 1) < C2

    @pl.loop(0, C1 // 2)
    def _(m):
        v = wa32[pl.ds(2 * m, 16, stride=C1), :]
        w = wa32[pl.ds(2 * m + 1, 16, stride=C1), :]
        ga_ref[0:16, lanes(128 * m, 128)] = jnp.where(first, v, pltpu.roll(w, C2, 1))
        ga_ref[16:27, lanes(128 * m, 128)] = jnp.where(first, pltpu.roll(v, C2, 1), w)[:11]

    store(ga_ref, ga_hbm)
    for copy in stores:
        copy.wait()


def shards(n_s, n_gz, cubes, weight_a, weight_b, cotangent):
    dma = pltpu.SemaphoreType.DMA
    anywhere = pl.BlockSpec(memory_space=pl.ANY)
    ins = (cubes, weight_a, weight_b, cotangent)
    outs = (
        jax.ShapeDtypeStruct((CUBES, ZD, SIDE, SIDE * C1), BF16),
        jax.ShapeDtypeStruct((27, C1 * C2), F32),
        jax.ShapeDtypeStruct((27, C2 * C3), F32),
    )
    return pl.pallas_call(
        functools.partial(kernel, n_s, n_gz),
        out_shape=outs,
        in_specs=[anywhere] * 4,
        out_specs=(anywhere,) * 3,
        scratch_shapes=[pltpu.VMEM(v.shape, v.dtype) for v in ins + outs] + [
            pltpu.VMEM((27 * C1, 128), F32),
            pltpu.VMEM((27 * C2, 128), F32),
            pltpu.VMEM((CUBES, ZD + 2, 64, 1280), BF16),
            pltpu.VMEM((2304, 256), BF16),
            pltpu.VMEM((2304, 256), BF16),
            pltpu.VMEM((256, 6912), BF16),
            pltpu.VMEM((256, 6912), BF16),
            pltpu.VMEM((BLOCKS, 256, 256), F32),
            pltpu.VMEM((2, 256, 256), F32),
            pltpu.VMEM((2, 160, 256), F32),
            pltpu.VMEM((CUBES, 4, 3, 16, 1152), BF16),
            pltpu.VMEM((CUBES, 4, 3, 16, 2816), BF16),
            pltpu.VMEM((CUBES, ZD + 2, 64, 2304), BF16),
            pltpu.VMEM((256, 512), BF16),
            pltpu.VMEM((256, 2304), BF16),
            pltpu.VMEM((CUBES, 16, 1024), F32),
            pltpu.VMEM((1024, 128), F32),
            pltpu.VMEM((2, CUBES, SIDE, 1024), BF16),
            pltpu.VMEM((2, CUBES, 16, 1152), BF16),
            pltpu.VMEM((2, CUBES, 16, 2048), BF16),
            pltpu.VMEM((2, CUBES, 32, 2304), BF16),
            pltpu.VMEM((ROWS_B, 128), BF16),
            pltpu.VMEM((n_gz, ROWS_B // n_gz, 128), BF16),
            pltpu.VMEM((n_s, ROWS_B // n_gz, 128), BF16),
            pltpu.VMEM((ROWS_B, 128), BF16),
            pltpu.VMEM((ROWS_A, 128), BF16),
            pltpu.VMEM((n_gz, ROWS_A // n_gz, 128), BF16),
            pltpu.VMEM((n_s, ROWS_A // n_gz, 128), BF16),
            pltpu.VMEM((ROWS_A, 128), BF16),
            dma((4,)), dma((3,)),
            dma((4, 2)), dma((4, 2)),
            dma((2, n_gz)), dma((2, n_gz)),
            dma((2, n_s)), dma((2, n_s)),
            dma((2, n_gz)), dma((2, n_gz)),
        ],
        compiler_params=pltpu.CompilerParams(
            collective_id=0, has_side_effects=True, vmem_limit_bytes=60 * 1024 * 1024
        ),
    )(*ins)


def solution(mesh):
    in_specs = (P("sample", "gz", None, None), P(), P(), P("sample", "gz", None, None))
    out_specs = (P("sample", "gz", None, None), P(), P())
    body = functools.partial(shards, mesh.shape["sample"], mesh.shape["gz"])
    return jax.shard_map(body, mesh=mesh, in_specs=in_specs, out_specs=out_specs, check_vma=False)
```

```python
import functools

import jax
import jax.numpy as jnp
from jax import lax
from jax.experimental import pallas as pl
from jax.experimental.pallas import tpu as pltpu
from jax.sharding import PartitionSpec as P

C1, C2, C3 = 32, 64, 128
SIDE = 32
ZD = 4
CUBES = 2
BLOCKS = 9
F32, BF16 = jnp.float32, jnp.bfloat16
MESH = pl.DeviceIdType.MESH
ROWS_B = 1792
HALF_B = 896
WIDE_B = 1024
ROWS_A = 512


def iota(shape, dim):
    return lax.broadcasted_iota(jnp.int32, shape, dim)


def dot(a, b):
    return lax.dot_general(a, b, (((1,), (0,)), ((), ())), preferred_element_type=F32)


def dot_nt(a, b):
    return lax.dot_general(a, b, (((1,), (1,)), ((), ())), preferred_element_type=F32)


def rows_before(v):
    return jnp.where(iota(v.shape, 0) % 16 == 0, 0.0, pltpu.roll(v, 1, 0))


def rows_after(v):
    return jnp.where(iota(v.shape, 0) % 16 == 15, 0.0, pltpu.roll(v, v.shape[0] - 1, 0))


def lanes(start, size):
    return pl.ds(pl.multiple_of(start, 128), size)


def kernel(
    n_s, n_gz, x_hbm, wa_hbm, wb_hbm, cot_hbm, dx_hbm, ga_hbm, gb_hbm,
    x_ref, wa_ref, wb_ref, cot_ref, dx_ref, ga_ref, gb_ref,
    wa32, wb32, xa, ta, tb, tad, tbd, ds_a, pre_s, gp_s, pb, hb, ga, ht, gt, cs, da,
    xh, ph, hh, gh, sb, cb, hs, rb, eb, fh, fo, sa, ra, ea, fa,
    load_s, store_s, halo_s, halo_r, core_s, core_r, rs_s, rs_r, ex_s, ex_r, ag_s, ag_r,
):
    me_s = lax.axis_index("sample")
    me_z = lax.axis_index("gz")
    low = lax.rem(me_z + n_gz - 1, n_gz)
    high = lax.rem(me_z + 1, n_gz)
    keep_low = (me_z > 0).astype(F32)
    keep_high = (me_z < n_gz - 1).astype(F32)

    core, y_lo, at_z = me_z % 2, (me_z // 2) % 2, me_z // 4
    at_x, y_hi = me_s // 2, me_s % 2
    n_e = n_s // 2
    mine = (core * at_x + (1 - core) * at_z) * 4 + y_hi * 2 + y_lo
    last = core * at_z + (1 - core) * at_x

    def in_group(t):
        a, y = t // 4, t % 4
        to_x = core * a + (1 - core) * at_x
        to_z = (1 - core) * a + core * at_z
        return (to_x * 2 + y // 2, to_z * 4 + (y % 2) * 2 + core)

    def in_line(e):
        to_x = core * at_x + (1 - core) * e
        to_z = (1 - core) * at_z + core * e
        return (to_x * 2 + y_hi, to_z * 4 + y_lo * 2 + core)

    barrier = pltpu.get_barrier_semaphore()

    @pl.loop(1, n_gz)
    def _(d):
        pl.semaphore_signal(barrier, inc=1, device_id=in_group(lax.rem(mine + d, n_gz)), device_id_type=MESH)

    @pl.loop(1, n_gz)
    def _(d):
        pl.semaphore_signal(barrier, inc=1, device_id=(me_s, lax.rem(me_z + d, n_gz)), device_id_type=MESH)

    @pl.loop(1, n_s)
    def _(d):
        pl.semaphore_signal(barrier, inc=1, device_id=(lax.rem(me_s + d, n_s), me_z), device_id_type=MESH)

    loads = [
        pltpu.make_async_copy(src, dst, load_s.at[i])
        for i, (src, dst) in enumerate(((wa_hbm, wa_ref), (wb_hbm, wb_ref), (x_hbm, x_ref), (cot_hbm, cot_ref)))
    ]
    for load in loads:
        load.start()

    def halo(stage, low_plane, high_plane, landing):
        pair = []
        for way, (src, peer) in enumerate(((high_plane, high), (low_plane, low))):
            copy = pltpu.make_async_remote_copy(
                src_ref=src, dst_ref=landing.at[way],
                send_sem=halo_s.at[stage, way], recv_sem=halo_r.at[stage, way],
                device_id=(me_s, peer), device_id_type=MESH,
            )
            copy.start()
            pair.append(copy)
        return pair

    half = iota((27, 128), 1) < C2
    loads[0].wait()

    @pl.loop(0, C1 // 2)
    def _(m):
        v = wa_ref[:, lanes(128 * m, 128)].astype(F32)
        w = pltpu.roll(v, C2, 1)
        wa32[pl.ds(2 * m, 27, stride=C1), :] = jnp.where(half, v, w)
        wa32[pl.ds(2 * m + 1, 27, stride=C1), :] = jnp.where(half, w, v)

    loads[1].wait()

    @pl.loop(0, C2)
    def _(i):
        wb32[pl.ds(i, 27, stride=C2), :] = wb_ref[:, lanes(128 * i, 128)].astype(F32)

    pl.semaphore_wait(barrier, 2 * n_gz + n_s - 3)
    halo_x = halo(0, x_hbm.at[:, 0], x_hbm.at[:, ZD - 1], xh)

    zero_a = jnp.zeros((C1, 128), BF16)
    zero_b = jnp.zeros((C2, 128), BF16)
    left = iota((C1, 128), 1) < C2

    def taps_a(zy):
        at = pl.multiple_of(zy * 3 * C1, C1)
        full = wa32[pl.ds(at, 3 * C1), :].astype(BF16)
        taps = [full[C1 * i:C1 * i + C1] for i in range(3)]

        def two(dx0, dx1):
            first = taps[dx0 + 1] if -1 <= dx0 <= 1 else zero_a
            second = taps[dx1 + 1] if -1 <= dx1 <= 1 else zero_a
            if first is second:
                return zero_a
            return jnp.where(left, first, second)

        return two

    def taps_b(zy):
        at = pl.multiple_of(zy * 3 * C2, C2)
        full = wb32[pl.ds(at, 3 * C2), :].astype(BF16)
        taps = [full[C2 * i:C2 * i + C2] for i in range(3)]
        return lambda dx: taps[dx + 1] if -1 <= dx <= 1 else zero_b

    @pl.loop(0, 9)
    def _(zy):
        dz = zy // 3
        base = (jnp.where(dz == 2, 2, 1 - dz) * 3 + zy % 3) * 256
        two = taps_a(zy)
        for p in range(8):
            for par in range(2):
                ta[pl.ds(pl.multiple_of(base + 32 * p, 32), 32), 128 * par:128 * par + 128] = two(p - 2 - par, p - 4 - par)

    spread_rows = (iota((64, SIDE), 1) == 2 * (iota((64, SIDE), 0) % 16) + iota((64, SIDE), 0) // 16 - 1).astype(BF16)
    spread_cot = (iota((16, 8), 0) // 2 == iota((16, 8), 1)).astype(BF16)
    natural = (iota((SIDE, SIDE), 1) == (iota((SIDE, SIDE), 0) % 2) * 16 + iota((SIDE, SIDE), 0) // 2).astype(BF16)
    edge = jnp.zeros((CUBES, ZD + 2, 64, 128), BF16)
    xa[:, :, :, 0:128] = edge
    xa[:, :, :, 1152:1280] = edge
    loads[2].wait()
    for b in range(CUBES):
        for z in range(ZD):
            xa[b, z + 1, :, 128:1152] = dot(spread_rows, x_ref[b, z]).astype(BF16)

    def x_windows(kt, planes):
        return jnp.concatenate([jnp.concatenate([
            xa[:, dz:dz + ZD, 16 * dy:16 * dy + 32, lanes(384 * kt + 128 * i, 256)].reshape(256, 256)
            for dz in planes for dy in range(3)
        ], axis=1) for i in range(3)], axis=0)

    @pl.loop(0, 3)
    def _(kt):
        part = dot(x_windows(kt, (1,)), ta[0:768])
        for i in range(3):
            ds_a[3 * kt + i] = part[256 * i:256 * i + 256]

    loads[3].wait()
    for b in range(CUBES):
        cs[b] = dot(spread_cot, cot_ref[b, 0]) * 0.125
    hb[:, :, :, :, 0:256] = jnp.zeros((CUBES, 4, 3, 16, 256), BF16)
    hb[:, :, :, :, 2304:2816] = jnp.zeros((CUBES, 4, 3, 16, 512), BF16)
    for copy in halo_x:
        copy.wait()
    for b in range(CUBES):
        xa[b, 0, :, 128:1152] = (dot(spread_rows, xh[0, b]) * keep_low).astype(BF16)
        xa[b, ZD + 1, :, 128:1152] = (dot(spread_rows, xh[1, b]) * keep_high).astype(BF16)

    @pl.loop(0, 3)
    def _(kt):
        part = dot(x_windows(kt, (0, 2)), ta[768:2304])
        for i in range(3):
            kk = 3 * kt + i
            pre = part[256 * i:256 * i + 256] + ds_a[kk]
            place = 2 * kk - 1 + (iota((1, 128), 1) // C2)
            inside = ((place >= 0) & (place < SIDE // 2)).astype(F32) * 0.125
            s = 0.5 * jnp.tanh(0.5 * pre) + 0.5
            act = pre * s
            slope = s + act * (1.0 - s)
            ds_a[kk] = slope * jnp.concatenate([inside, inside], axis=1)
            act = (act[:, :128] + act[:, 128:]).reshape(CUBES, 2, 2, 2, 16, 128)
            pooled = (act[:, :, 0, 0] + act[:, :, 0, 1] + act[:, :, 1, 0] + act[:, :, 1, 1]).reshape(64, 128) * inside
            for dy, v in enumerate((rows_before(pooled), pooled, rows_after(pooled))):
                pb[:, 1:3, dy, :, lanes(128 * kk, 128)] = v.astype(BF16).reshape(CUBES, 2, 16, 128)

    halo_p = halo(1, pb.at[:, 1, 1], pb.at[:, 2, 1], ph)

    @pl.loop(0, 9)
    def _(zy):
        base = zy * 256
        tap = taps_b(zy)
        for p in range(4):
            for q in range(2):
                tb[pl.ds(pl.multiple_of(base + 64 * p, 64), 64), 128 * q:128 * q + 128] = tap(p - 1 - q)

    def p_windows(planes):
        return jnp.concatenate([jnp.concatenate([
            pb[:, z, dy, :, 128 * k:128 * k + 256].reshape(32, 256) for z in planes for dy in range(3)
        ], axis=1) for k in range(8)], axis=0)

    window = p_windows((1, 2))
    pre_s[0] = dot(window, tb[768:2304])
    pre_s[1] = dot(window, tb[0:1536])

    @pl.loop(0, 9)
    def _(s):
        tap = taps_b(8 - s)
        for r in range(4):
            for p in range(6):
                tbd[64 * r:64 * r + 64, lanes(s * 768 + 128 * p, 128)] = tap(r + 1 - p)

    @pl.loop(0, 9)
    def _(s):
        two = taps_a(8 - s)
        for r in range(8):
            for kk in range(3):
                for par in range(2):
                    dx = r + 2 - 4 * kk - par
                    tad[32 * r:32 * r + 32, lanes(s * 768 + 256 * kk + 128 * par, 128)] = two(dx, dx - 2)

    for copy in halo_p:
        copy.wait()
    for plane, way, keep in ((0, 0, keep_low), (3, 1, keep_high)):
        v = ph[way].astype(F32).reshape(32, 1152) * keep
        for dy, v in enumerate((rows_before(v), v, rows_after(v))):
            pb[:, plane, dy] = v.astype(BF16).reshape(CUBES, 16, 1152)

    for zp in range(2):
        pre = pre_s[zp] + dot(p_windows((3 * zp,)), tb[1536 * zp:1536 * zp + 768])
        s = 0.5 * jnp.tanh(0.5 * pre) + 0.5
        slope = s + pre * s * (1.0 - s)
        grads = []
        for k in range(8):
            up = cs[:, :, 128 * k:128 * k + 128].reshape(32, 128)
            h = slope[32 * k:32 * k + 32] * jnp.concatenate([up, up], axis=1)
            grads.append(h)
            for dy, v in enumerate((rows_before(h), h, rows_after(h))):
                hb[:, 1 + zp, dy, :, 256 + 256 * k:512 + 256 * k] = v.astype(BF16).reshape(CUBES, 16, 256)
        ht[:, 256 * zp:256 * zp + 256] = jnp.concatenate(grads, axis=0).T.astype(BF16)

    halo_h = halo(2, hb.at[:, 1, 1, :, 256:2304], hb.at[:, 2, 1, :, 256:2304], hh)

    @pl.loop(0, 3)
    def _(dz):
        window = jnp.concatenate([jnp.concatenate([
            pb[:, dz + zp, dy, :, 128 * k:128 * k + 256].reshape(32, 256) for zp in range(2) for k in range(8)
        ], axis=0) for dy in range(3)], axis=1)
        all_dy = dot(ht[...], window)
        for dy in range(3):
            full = all_dy[:, 256 * dy:256 * dy + 256]
            diag = full[:128] + pltpu.roll(full[128:], 192, 1)
            sb[pl.ds(pl.multiple_of(dz * 576 + dy * 192, 64), 192), :] = diag.T[:192].astype(BF16)

    sb[1728:ROWS_B, :] = jnp.zeros((ROWS_B - 1728, 128), BF16)
    hs[HALF_B:, :] = jnp.zeros((WIDE_B - HALF_B, 128), BF16)

    def shard(ref, n, index):
        rows = ref.shape[0] // n
        return ref.at[pl.ds(pl.multiple_of(index * rows, 16), rows), :]

    def scatter_copy(which, send, land, d):
        peer = lax.rem(me_z + d, n_gz)
        return pltpu.make_async_remote_copy(
            src_ref=shard(send, n_gz, peer), dst_ref=land.at[me_z],
            send_sem=rs_s.at[which, d], recv_sem=rs_r.at[which, d],
            device_id=(me_s, peer), device_id_type=MESH,
        )

    def sample_copy(which, land, d):
        peer = lax.rem(me_s + d, n_s)
        return pltpu.make_async_remote_copy(
            src_ref=land.at[me_s], dst_ref=land.at[me_s],
            send_sem=ex_s.at[which, d], recv_sem=ex_r.at[which, d],
            device_id=(peer, me_z), device_id_type=MESH,
        )

    def gather_copy(which, full, d):
        peer = lax.rem(me_z + d, n_gz)
        return pltpu.make_async_remote_copy(
            src_ref=shard(full, n_gz, me_z), dst_ref=shard(full, n_gz, me_z),
            send_sem=ag_s.at[which, d], recv_sem=ag_r.at[which, d],
            device_id=(me_s, peer), device_id_type=MESH,
        )

    def start_all(make, n):
        @pl.loop(1, n)
        def _(d):
            make(d).start()

    def wait_all(make, n):
        @pl.loop(1, n)
        def _(d):
            make(d).wait()

    def scatter_start(which, send, land):
        start_all(functools.partial(scatter_copy, which, send, land), n_gz)

    def scatter_end(which, send, land, exchange):
        wait_all(functools.partial(scatter_copy, which, send, land), n_gz)
        rows = send.shape[0] // n_gz
        own = send[pl.ds(pl.multiple_of(me_z * rows, 16), rows), :]
        land[me_z] = own
        total = land[0].astype(F32)
        for t in range(1, n_gz):
            total = total + land[t].astype(F32)
        exchange[me_s] = total.astype(BF16)
        start_all(functools.partial(sample_copy, which, exchange), n_s)

    def exchange_end(which, exchange, full):
        wait_all(functools.partial(sample_copy, which, exchange), n_s)
        total = exchange[0].astype(F32)
        for t in range(1, n_s):
            total = total + exchange[t].astype(F32)
        rows = full.shape[0] // n_gz
        full[pl.ds(pl.multiple_of(me_z * rows, 16), rows), :] = (total * (1.0 / (CUBES * n_s))).astype(BF16)
        start_all(functools.partial(gather_copy, which, full), n_gz)

    def half_of(ref, which):
        return ref.at[pl.ds(pl.multiple_of(which * HALF_B, 128), HALF_B), :]

    part = WIDE_B // n_gz

    def part_of(ref, t):
        return ref.at[pl.ds(pl.multiple_of(t * part, 64), part), :]

    def core_copy(stage, src, dst):
        return pltpu.make_async_remote_copy(
            src_ref=src, dst_ref=dst, send_sem=core_s.at[stage], recv_sem=core_r.at[stage],
            device_id=(me_s, me_z + 1 - 2 * core), device_id_type=MESH,
        )

    def group_copy(d):
        peer = lax.rem(mine + d, n_gz)
        return pltpu.make_async_remote_copy(
            src_ref=part_of(hs, peer), dst_ref=rb.at[mine], send_sem=rs_s.at[0, d], recv_sem=rs_r.at[0, d],
            device_id=in_group(peer), device_id_type=MESH,
        )

    def line_copy(d):
        return pltpu.make_async_remote_copy(
            src_ref=eb.at[last], dst_ref=eb.at[last], send_sem=ex_s.at[0, d], recv_sem=ex_r.at[0, d],
            device_id=in_line(lax.rem(last + d, n_e)), device_id_type=MESH,
        )

    def back_copy(d):
        return pltpu.make_async_remote_copy(
            src_ref=part_of(fh, mine), dst_ref=part_of(fh, mine), send_sem=ag_s.at[0, d], recv_sem=ag_r.at[0, d],
            device_id=in_group(lax.rem(mine + d, n_gz)), device_id_type=MESH,
        )

    def reduce_b0():
        swap = core_copy(0, half_of(sb, 1 - core), cb)
        swap.start()
        return swap

    def reduce_b1(swap):
        swap.wait()
        own = sb[pl.ds(pl.multiple_of(core * HALF_B, 128), HALF_B), :]
        hs[0:HALF_B] = (own.astype(F32) + cb[...].astype(F32)).astype(BF16)
        start_all(group_copy, n_gz)

    def reduce_b2():
        wait_all(group_copy, n_gz)
        rb[mine] = hs[pl.ds(pl.multiple_of(mine * part, 64), part), :]
        total = rb[0].astype(F32)
        for t in range(1, n_gz):
            total = total + rb[t].astype(F32)
        eb[last] = total.astype(BF16)
        start_all(line_copy, n_e)

    def reduce_b3():
        wait_all(line_copy, n_e)
        total = eb[0].astype(F32)
        for t in range(1, n_e):
            total = total + eb[t].astype(F32)
        fh[pl.ds(pl.multiple_of(mine * part, 64), part), :] = (total * (1.0 / (CUBES * n_s))).astype(BF16)
        start_all(back_copy, n_gz)

    def reduce_b4():
        wait_all(back_copy, n_gz)
        swap = core_copy(1, fh.at[0:HALF_B], fo)
        swap.start()
        wb32[pl.ds(pl.multiple_of(core * HALF_B, 128), HALF_B), :] = fh[0:HALF_B].astype(F32)
        return swap

    def reduce_b5(swap):
        swap.wait()
        wb32[pl.ds(pl.multiple_of((1 - core) * HALF_B, 128), HALF_B), :] = fo[...].astype(F32)

    swap = reduce_b0()

    def h_windows(planes):
        return jnp.concatenate([jnp.concatenate([
            hb[:, z, sy, :, 512 * j:512 * j + 768].reshape(32, 768) for z in planes for sy in range(3)
        ], axis=1) for j in range(5)], axis=0)

    window = h_windows((1, 2))
    gp_s[0] = dot_nt(window, tbd[:, 2304:6912])
    gp_s[1] = dot_nt(window, tbd[:, 0:4608])

    reduce_b1(swap)
    for copy in halo_h:
        copy.wait()
    for plane, way, keep in ((0, 0, keep_low), (3, 1, keep_high)):
        v = hh[way].astype(F32).reshape(32, 2048) * keep
        for dy, v in enumerate((rows_before(v), v, rows_after(v))):
            hb[:, plane, dy, :, 256:2304] = v.astype(BF16).reshape(CUBES, 16, 2048)

    for zp in range(2):
        gp_s[zp] = gp_s[zp] + dot_nt(h_windows((3 * zp,)), tbd[:, 4608 * zp:4608 * zp + 2304])

    @pl.loop(0, BLOCKS)
    def _(kk):
        up = gp_s[:, pl.ds(pl.multiple_of((kk // 2) * 32, 32), 32), lanes(128 * (kk % 2), 128)]
        up = jnp.concatenate([up, up], axis=2).reshape(2, CUBES, 16, 256)
        g = []
        for b in range(CUBES):
            for zp in range(2):
                g.append((ds_a[kk, 128 * b + 64 * zp:128 * b + 64 * zp + 64].reshape(4, 16, 256) * up[zp, b][None]).reshape(64, 256))
        g = jnp.concatenate(g, axis=0)
        gt[:, lanes(256 * kk, 256)] = g.T.astype(BF16)
        g = g.reshape(CUBES, ZD, 2, 16, 256)
        even = g[:, :, 0].reshape(128, 256)
        odd = g[:, :, 1].reshape(128, 256)
        for group, v in enumerate((rows_before(odd), even, odd, rows_after(even))):
            ga[:, 1:1 + ZD, 16 * group:16 * group + 16, lanes(256 * kk, 256)] = v.astype(BF16).reshape(CUBES, ZD, 16, 256)

    halo_g = halo(3, ga.at[:, 1, 16:48], ga.at[:, ZD, 16:48], gh)

    def terms_a(dz):
        window = jnp.concatenate([jnp.concatenate([
            xa[:, pl.ds(dz, ZD), 16 * dy:16 * dy + 32, 128 * kk:128 * kk + 256].reshape(256, 256)
            for kk in range(BLOCKS)
        ], axis=0) for dy in range(3)], axis=1)
        all_dy = dot(gt[...], window)
        for dy in range(3):
            full = all_dy[:, 256 * dy:256 * dy + 256]
            total = jnp.zeros((64, 256), F32)
            for par in range(2):
                for pair in range(2):
                    t = 2 * pair + par
                    at = 128 * par + 64 * pair
                    total = total + pltpu.roll(full[at:at + 64], 256 - 32 * (t + 1), 1)
            total = total[:, :128]
            da[pl.ds(pl.multiple_of(dz * 288 + dy * 96, 32), 96), :] = jnp.concatenate([total, total], axis=0).T[:96]

    @pl.loop(0, 3)
    def _(dz):
        terms_a(dz)

    half = iota((ROWS_A, 128), 1) < C2
    da[864:1024, :] = jnp.zeros((160, 128), F32)
    sa[...] = jnp.where(half, da[0:512], da[512:1024]).astype(BF16)
    scatter_start(1, sa, ra)
    reduce_b2()

    for copy in halo_g:
        copy.wait()
    for plane, way, keep in ((0, 0, keep_low), (ZD + 1, 1, keep_high)):
        even = gh[way, :, 0:16].astype(F32).reshape(32, 2304) * keep
        odd = gh[way, :, 16:32].astype(F32).reshape(32, 2304) * keep
        for group, v in enumerate((rows_before(odd), even, odd, rows_after(even))):
            ga[:, plane, 16 * group:16 * group + 16] = v.astype(BF16).reshape(CUBES, 16, 2304)


    stores = []

    def store(src, dst):
        copy = pltpu.make_async_copy(src, dst, store_s.at[len(stores)])
        copy.start()
        stores.append(copy)

    def cubes_grad(jj):
        part = jnp.concatenate([jnp.concatenate([
            ga[:, sz:sz + ZD, 16 * sy:16 * sy + 32, 1024 * jj + 512 * i:1024 * jj + 512 * i + 768].reshape(256, 768)
            for sz in range(3) for sy in range(3)
        ], axis=1) for i in range(2)], axis=0)
        total = dot_nt(part, tad[...]).astype(BF16)
        for i in range(2):
            for b in range(CUBES):
                for z in range(ZD):
                    at = 256 * i + 32 * (ZD * b + z)
                    dx_ref[b, z, :, 512 * jj + 256 * i:512 * jj + 256 * i + 256] = dot(natural, total[at:at + 32]).astype(BF16)

    cubes_grad(0)
    reduce_b3()
    scatter_end(1, sa, ra, ea)
    cubes_grad(1)
    store(dx_ref, dx_hbm)
    exchange_end(1, ea, fa)

    reduce_b5(reduce_b4())

    @pl.loop(0, C2)
    def _(i):
        gb_ref[:, lanes(128 * i, 128)] = wb32[pl.ds(i, 27, stride=C2), :]

    store(gb_ref, gb_hbm)
    wait_all(functools.partial(gather_copy, 1, fa), n_gz)
    wa32[0:ROWS_A] = fa[...].astype(F32)
    first = iota((16, 128), 1) < C2

    @pl.loop(0, C1 // 2)
    def _(m):
        v = wa32[pl.ds(2 * m, 16, stride=C1), :]
        w = wa32[pl.ds(2 * m + 1, 16, stride=C1), :]
        ga_ref[0:16, lanes(128 * m, 128)] = jnp.where(first, v, pltpu.roll(w, C2, 1))
        ga_ref[16:27, lanes(128 * m, 128)] = jnp.where(first, pltpu.roll(v, C2, 1), w)[:11]

    store(ga_ref, ga_hbm)
    for copy in stores:
        copy.wait()


def pass_on(dx_in, ga_in, gb_in, dx_out, ga_out, gb_out, dx_ref, ga_ref, gb_ref, in_s, out_s):
    near, far = pl.ds(0, 4096), pl.ds(4096, 4096)
    pieces = [(dx_in.at[b], dx_ref.at[b], dx_out.at[b]) for b in range(CUBES)]
    pieces += [(gb_in.at[:, w], gb_ref.at[:, w], gb_out.at[:, w]) for w in (near, far)]
    pieces.append((ga_in, ga_ref, ga_out))
    taken = [pltpu.make_async_copy(src, via, in_s.at[i]) for i, (src, via, _) in enumerate(pieces)]
    given = [pltpu.make_async_copy(via, dst, out_s.at[i]) for i, (_, via, dst) in enumerate(pieces)]
    for copy in taken:
        copy.start()
    for arrive, leave in zip(taken, given):
        arrive.wait()
        leave.start()
    for copy in given:
        copy.wait()


def shards(n_s, n_gz, cubes, weight_a, weight_b, cotangent):
    dma = pltpu.SemaphoreType.DMA
    anywhere = pl.BlockSpec(memory_space=pl.ANY)
    ins = (cubes, weight_a, weight_b, cotangent)
    outs = (
        jax.ShapeDtypeStruct((CUBES, ZD, SIDE, SIDE * C1), BF16),
        jax.ShapeDtypeStruct((27, C1 * C2), F32),
        jax.ShapeDtypeStruct((27, C2 * C3), F32),
    )
    results = pl.pallas_call(
        functools.partial(kernel, n_s, n_gz),
        out_shape=outs,
        in_specs=[anywhere] * 4,
        out_specs=(anywhere,) * 3,
        scratch_shapes=[pltpu.VMEM(v.shape, v.dtype) for v in ins + outs] + [
            pltpu.VMEM((27 * C1, 128), F32),
            pltpu.VMEM((ROWS_B, 128), F32),
            pltpu.VMEM((CUBES, ZD + 2, 64, 1280), BF16),
            pltpu.VMEM((2304, 256), BF16),
            pltpu.VMEM((2304, 256), BF16),
            pltpu.VMEM((256, 6912), BF16),
            pltpu.VMEM((256, 6912), BF16),
            pltpu.VMEM((BLOCKS, 256, 256), F32),
            pltpu.VMEM((2, 256, 256), F32),
            pltpu.VMEM((2, 160, 256), F32),
            pltpu.VMEM((CUBES, 4, 3, 16, 1152), BF16),
            pltpu.VMEM((CUBES, 4, 3, 16, 2816), BF16),
            pltpu.VMEM((CUBES, ZD + 2, 64, 2304), BF16),
            pltpu.VMEM((256, 512), BF16),
            pltpu.VMEM((256, 2304), BF16),
            pltpu.VMEM((CUBES, 16, 1024), F32),
            pltpu.VMEM((1024, 128), F32),
            pltpu.VMEM((2, CUBES, SIDE, 1024), BF16),
            pltpu.VMEM((2, CUBES, 16, 1152), BF16),
            pltpu.VMEM((2, CUBES, 16, 2048), BF16),
            pltpu.VMEM((2, CUBES, 32, 2304), BF16),
            pltpu.VMEM((ROWS_B, 128), BF16),
            pltpu.VMEM((HALF_B, 128), BF16),
            pltpu.VMEM((WIDE_B, 128), BF16),
            pltpu.VMEM((n_gz, WIDE_B // n_gz, 128), BF16),
            pltpu.VMEM((n_s // 2, WIDE_B // n_gz, 128), BF16),
            pltpu.VMEM((WIDE_B, 128), BF16),
            pltpu.VMEM((HALF_B, 128), BF16),
            pltpu.VMEM((ROWS_A, 128), BF16),
            pltpu.VMEM((n_gz, ROWS_A // n_gz, 128), BF16),
            pltpu.VMEM((n_s, ROWS_A // n_gz, 128), BF16),
            pltpu.VMEM((ROWS_A, 128), BF16),
            dma((4,)), dma((3,)),
            dma((4, 2)), dma((4, 2)), dma((2,)), dma((2,)),
            dma((2, n_gz)), dma((2, n_gz)),
            dma((2, n_s)), dma((2, n_s)),
            dma((2, n_gz)), dma((2, n_gz)),
        ],
        compiler_params=pltpu.CompilerParams(
            collective_id=0, has_side_effects=True, vmem_limit_bytes=60 * 1024 * 1024
        ),
    )(*ins)
    return pl.pallas_call(
        pass_on,
        out_shape=outs,
        in_specs=[anywhere] * 3,
        out_specs=(anywhere,) * 3,
        scratch_shapes=[pltpu.VMEM(v.shape, v.dtype) for v in outs] + [dma((5,)), dma((5,))],
    )(*results)


def solution(mesh):
    in_specs = (P("sample", "gz", None, None), P(), P(), P("sample", "gz", None, None))
    out_specs = (P("sample", "gz", None, None), P(), P())
    body = functools.partial(shards, mesh.shape["sample"], mesh.shape["gz"])
    return jax.shard_map(body, mesh=mesh, in_specs=in_specs, out_specs=out_specs, check_vma=False)
```

```python
import functools

import jax
import jax.numpy as jnp
from jax import lax
from jax.experimental import pallas as pl
from jax.experimental.pallas import tpu as pltpu
from jax.sharding import PartitionSpec as P

C1, C2, C3 = 32, 64, 128
SIDE = 32
ZD = 4
CUBES = 2
BLOCKS = 9
F32, BF16 = jnp.float32, jnp.bfloat16
MESH = pl.DeviceIdType.MESH
ROWS_B = 1792
HALF_B = 896
WIDE_B = 1024
ROWS_A = 512


def iota(shape, dim):
    return lax.broadcasted_iota(jnp.int32, shape, dim)


def dot(a, b):
    return lax.dot_general(a, b, (((1,), (0,)), ((), ())), preferred_element_type=F32)


def dot_nt(a, b):
    return lax.dot_general(a, b, (((1,), (1,)), ((), ())), preferred_element_type=F32)


def rows_before(v):
    return jnp.where(iota(v.shape, 0) % 16 == 0, 0.0, pltpu.roll(v, 1, 0))


def rows_after(v):
    return jnp.where(iota(v.shape, 0) % 16 == 15, 0.0, pltpu.roll(v, v.shape[0] - 1, 0))


def lanes(start, size):
    return pl.ds(pl.multiple_of(start, 128), size)


def kernel(
    n_s, n_gz, x_hbm, wa_hbm, wb_hbm, cot_hbm, dx_hbm, ga_hbm, gb_hbm,
    x_ref, wa_ref, wb_ref, cot_ref, dx_ref, ga_ref, gb_ref,
    wa32, wb32, xa, ta, tb, tad, tbd, ds_a, pre_s, gp_s, pb, hb, ga, ht, gt, cs, da,
    xh, ph, hh, gh, sb, cb, hs, rb, eb, fh, fo, sa, ra, ea, fa,
    load_s, store_s, halo_s, halo_r, core_s, core_r, rs_s, rs_r, ex_s, ex_r, ag_s, ag_r,
):
    me_s = lax.axis_index("sample")
    me_z = lax.axis_index("gz")
    low = lax.rem(me_z + n_gz - 1, n_gz)
    high = lax.rem(me_z + 1, n_gz)
    keep_low = (me_z > 0).astype(F32)
    keep_high = (me_z < n_gz - 1).astype(F32)

    core, y_lo, at_z = me_z % 2, (me_z // 2) % 2, me_z // 4
    at_x, y_hi = me_s // 2, me_s % 2
    n_e = n_s // 2
    mine = (core * at_x + (1 - core) * at_z) * 4 + y_hi * 2 + y_lo
    last = core * at_z + (1 - core) * at_x

    def in_group(t):
        a, y = t // 4, t % 4
        to_x = core * a + (1 - core) * at_x
        to_z = (1 - core) * a + core * at_z
        return (to_x * 2 + y // 2, to_z * 4 + (y % 2) * 2 + core)

    def in_line(e):
        to_x = core * at_x + (1 - core) * e
        to_z = (1 - core) * at_z + core * e
        return (to_x * 2 + y_hi, to_z * 4 + y_lo * 2 + core)

    barrier = pltpu.get_barrier_semaphore()

    @pl.loop(1, n_gz)
    def _(d):
        pl.semaphore_signal(barrier, inc=1, device_id=in_group(lax.rem(mine + d, n_gz)), device_id_type=MESH)

    @pl.loop(1, n_gz)
    def _(d):
        pl.semaphore_signal(barrier, inc=1, device_id=(me_s, lax.rem(me_z + d, n_gz)), device_id_type=MESH)

    @pl.loop(1, n_s)
    def _(d):
        pl.semaphore_signal(barrier, inc=1, device_id=(lax.rem(me_s + d, n_s), me_z), device_id_type=MESH)

    loads = [
        pltpu.make_async_copy(src, dst, load_s.at[i])
        for i, (src, dst) in enumerate(((wa_hbm, wa_ref), (wb_hbm, wb_ref), (x_hbm, x_ref), (cot_hbm, cot_ref)))
    ]
    for load in loads:
        load.start()

    def halo(stage, low_plane, high_plane, landing):
        pair = []
        for way, (src, peer) in enumerate(((high_plane, high), (low_plane, low))):
            copy = pltpu.make_async_remote_copy(
                src_ref=src, dst_ref=landing.at[way],
                send_sem=halo_s.at[stage, way], recv_sem=halo_r.at[stage, way],
                device_id=(me_s, peer), device_id_type=MESH,
            )
            copy.start()
            pair.append(copy)
        return pair

    half = iota((27, 128), 1) < C2
    loads[0].wait()

    @pl.loop(0, C1 // 2)
    def _(m):
        v = wa_ref[:, lanes(128 * m, 128)].astype(F32)
        w = pltpu.roll(v, C2, 1)
        wa32[pl.ds(2 * m, 27, stride=C1), :] = jnp.where(half, v, w)
        wa32[pl.ds(2 * m + 1, 27, stride=C1), :] = jnp.where(half, w, v)

    loads[1].wait()

    @pl.loop(0, C2)
    def _(i):
        wb32[pl.ds(i, 27, stride=C2), :] = wb_ref[:, lanes(128 * i, 128)].astype(F32)

    pl.semaphore_wait(barrier, 2 * n_gz + n_s - 3)
    halo_x = halo(0, x_hbm.at[:, 0], x_hbm.at[:, ZD - 1], xh)

    zero_a = jnp.zeros((C1, 128), BF16)
    zero_b = jnp.zeros((C2, 128), BF16)
    left = iota((C1, 128), 1) < C2

    def taps_a(zy):
        at = pl.multiple_of(zy * 3 * C1, C1)
        full = wa32[pl.ds(at, 3 * C1), :].astype(BF16)
        taps = [full[C1 * i:C1 * i + C1] for i in range(3)]

        def two(dx0, dx1):
            first = taps[dx0 + 1] if -1 <= dx0 <= 1 else zero_a
            second = taps[dx1 + 1] if -1 <= dx1 <= 1 else zero_a
            if first is second:
                return zero_a
            return jnp.where(left, first, second)

        return two

    def taps_b(zy):
        at = pl.multiple_of(zy * 3 * C2, C2)
        full = wb32[pl.ds(at, 3 * C2), :].astype(BF16)
        taps = [full[C2 * i:C2 * i + C2] for i in range(3)]
        return lambda dx: taps[dx + 1] if -1 <= dx <= 1 else zero_b

    @pl.loop(0, 9)
    def _(zy):
        dz = zy // 3
        base = (jnp.where(dz == 2, 2, 1 - dz) * 3 + zy % 3) * 256
        two = taps_a(zy)
        for p in range(8):
            for par in range(2):
                ta[pl.ds(pl.multiple_of(base + 32 * p, 32), 32), 128 * par:128 * par + 128] = two(p - 2 - par, p - 4 - par)

    spread_rows = (iota((64, SIDE), 1) == 2 * (iota((64, SIDE), 0) % 16) + iota((64, SIDE), 0) // 16 - 1).astype(BF16)
    spread_cot = (iota((16, 8), 0) // 2 == iota((16, 8), 1)).astype(BF16)
    natural = (iota((SIDE, SIDE), 1) == (iota((SIDE, SIDE), 0) % 2) * 16 + iota((SIDE, SIDE), 0) // 2).astype(BF16)
    edge = jnp.zeros((CUBES, ZD + 2, 64, 128), BF16)
    xa[:, :, :, 0:128] = edge
    xa[:, :, :, 1152:1280] = edge
    loads[2].wait()
    for b in range(CUBES):
        for z in range(ZD):
            xa[b, z + 1, :, 128:1152] = dot(spread_rows, x_ref[b, z]).astype(BF16)

    def x_windows(kt, planes):
        return jnp.concatenate([jnp.concatenate([
            xa[:, dz:dz + ZD, 16 * dy:16 * dy + 32, lanes(384 * kt + 128 * i, 256)].reshape(256, 256)
            for dz in planes for dy in range(3)
        ], axis=1) for i in range(3)], axis=0)

    @pl.loop(0, 3)
    def _(kt):
        part = dot(x_windows(kt, (1,)), ta[0:768])
        for i in range(3):
            ds_a[3 * kt + i] = part[256 * i:256 * i + 256]

    loads[3].wait()
    for b in range(CUBES):
        cs[b] = dot(spread_cot, cot_ref[b, 0]) * 0.125
    hb[:, :, :, :, 0:256] = jnp.zeros((CUBES, 4, 3, 16, 256), BF16)
    hb[:, :, :, :, 2304:2816] = jnp.zeros((CUBES, 4, 3, 16, 512), BF16)
    for copy in halo_x:
        copy.wait()
    for b in range(CUBES):
        xa[b, 0, :, 128:1152] = (dot(spread_rows, xh[0, b]) * keep_low).astype(BF16)
        xa[b, ZD + 1, :, 128:1152] = (dot(spread_rows, xh[1, b]) * keep_high).astype(BF16)

    @pl.loop(0, 3)
    def _(kt):
        part = dot(x_windows(kt, (0, 2)), ta[768:2304])
        for i in range(3):
            kk = 3 * kt + i
            pre = part[256 * i:256 * i + 256] + ds_a[kk]
            place = 2 * kk - 1 + (iota((1, 128), 1) // C2)
            inside = ((place >= 0) & (place < SIDE // 2)).astype(F32) * 0.125
            s = 0.5 * jnp.tanh(0.5 * pre) + 0.5
            act = pre * s
            slope = s + act * (1.0 - s)
            ds_a[kk] = slope * jnp.concatenate([inside, inside], axis=1)
            act = (act[:, :128] + act[:, 128:]).reshape(CUBES, 2, 2, 2, 16, 128)
            pooled = (act[:, :, 0, 0] + act[:, :, 0, 1] + act[:, :, 1, 0] + act[:, :, 1, 1]).reshape(64, 128) * inside
            for dy, v in enumerate((rows_before(pooled), pooled, rows_after(pooled))):
                pb[:, 1:3, dy, :, lanes(128 * kk, 128)] = v.astype(BF16).reshape(CUBES, 2, 16, 128)

    halo_p = halo(1, pb.at[:, 1, 1], pb.at[:, 2, 1], ph)

    @pl.loop(0, 9)
    def _(zy):
        base = zy * 256
        tap = taps_b(zy)
        for p in range(4):
            for q in range(2):
                tb[pl.ds(pl.multiple_of(base + 64 * p, 64), 64), 128 * q:128 * q + 128] = tap(p - 1 - q)

    def p_windows(planes):
        return jnp.concatenate([jnp.concatenate([
            pb[:, z, dy, :, 128 * k:128 * k + 256].reshape(32, 256) for z in planes for dy in range(3)
        ], axis=1) for k in range(8)], axis=0)

    window = p_windows((1, 2))
    pre_s[0] = dot(window, tb[768:2304])
    pre_s[1] = dot(window, tb[0:1536])

    @pl.loop(0, 9)
    def _(s):
        tap = taps_b(8 - s)
        for r in range(4):
            for p in range(6):
                tbd[64 * r:64 * r + 64, lanes(s * 768 + 128 * p, 128)] = tap(r + 1 - p)

    @pl.loop(0, 9)
    def _(s):
        two = taps_a(8 - s)
        sz = s // 3
        base = (jnp.where(sz == 2, 2, 1 - sz) * 3 + s % 3) * 768
        for r in range(8):
            for kk in range(3):
                for par in range(2):
                    dx = r + 2 - 4 * kk - par
                    tad[32 * r:32 * r + 32, lanes(base + 256 * kk + 128 * par, 128)] = two(dx, dx - 2)

    for copy in halo_p:
        copy.wait()
    for plane, way, keep in ((0, 0, keep_low), (3, 1, keep_high)):
        v = ph[way].astype(F32).reshape(32, 1152) * keep
        for dy, v in enumerate((rows_before(v), v, rows_after(v))):
            pb[:, plane, dy] = v.astype(BF16).reshape(CUBES, 16, 1152)

    for zp in range(2):
        pre = pre_s[zp] + dot(p_windows((3 * zp,)), tb[1536 * zp:1536 * zp + 768])
        s = 0.5 * jnp.tanh(0.5 * pre) + 0.5
        slope = s + pre * s * (1.0 - s)
        grads = []
        for k in range(8):
            up = cs[:, :, 128 * k:128 * k + 128].reshape(32, 128)
            h = slope[32 * k:32 * k + 32] * jnp.concatenate([up, up], axis=1)
            grads.append(h)
            for dy, v in enumerate((rows_before(h), h, rows_after(h))):
                hb[:, 1 + zp, dy, :, 256 + 256 * k:512 + 256 * k] = v.astype(BF16).reshape(CUBES, 16, 256)
        ht[:, 256 * zp:256 * zp + 256] = jnp.concatenate(grads, axis=0).astype(BF16).T

    halo_h = halo(2, hb.at[:, 1, 1, :, 256:2304], hb.at[:, 2, 1, :, 256:2304], hh)

    @pl.loop(0, 3)
    def _(dz):
        window = jnp.concatenate([jnp.concatenate([
            pb[:, dz + zp, dy, :, 128 * k:128 * k + 256].reshape(32, 256) for zp in range(2) for k in range(8)
        ], axis=0) for dy in range(3)], axis=1)
        all_dy = dot(ht[...], window)
        for dy in range(3):
            full = all_dy[:, 256 * dy:256 * dy + 256]
            diag = full[:128] + pltpu.roll(full[128:], 192, 1)
            sb[pl.ds(pl.multiple_of(dz * 576 + dy * 192, 64), 192), :] = diag.astype(BF16).T[:192]

    sb[1728:ROWS_B, :] = jnp.zeros((ROWS_B - 1728, 128), BF16)
    hs[HALF_B:, :] = jnp.zeros((WIDE_B - HALF_B, 128), BF16)

    def shard(ref, n, index):
        rows = ref.shape[0] // n
        return ref.at[pl.ds(pl.multiple_of(index * rows, 16), rows), :]

    def scatter_copy(which, send, land, d):
        peer = lax.rem(me_z + d, n_gz)
        return pltpu.make_async_remote_copy(
            src_ref=shard(send, n_gz, peer), dst_ref=land.at[me_z],
            send_sem=rs_s.at[which, d], recv_sem=rs_r.at[which, d],
            device_id=(me_s, peer), device_id_type=MESH,
        )

    def sample_copy(which, land, d):
        peer = lax.rem(me_s + d, n_s)
        return pltpu.make_async_remote_copy(
            src_ref=land.at[me_s], dst_ref=land.at[me_s],
            send_sem=ex_s.at[which, d], recv_sem=ex_r.at[which, d],
            device_id=(peer, me_z), device_id_type=MESH,
        )

    def gather_copy(which, full, d):
        peer = lax.rem(me_z + d, n_gz)
        return pltpu.make_async_remote_copy(
            src_ref=shard(full, n_gz, me_z), dst_ref=shard(full, n_gz, me_z),
            send_sem=ag_s.at[which, d], recv_sem=ag_r.at[which, d],
            device_id=(me_s, peer), device_id_type=MESH,
        )

    def start_all(make, n):
        @pl.loop(1, n)
        def _(d):
            make(d).start()

    def wait_all(make, n):
        @pl.loop(1, n)
        def _(d):
            make(d).wait()

    def scatter_start(which, send, land):
        start_all(functools.partial(scatter_copy, which, send, land), n_gz)

    def scatter_end(which, send, land, exchange):
        wait_all(functools.partial(scatter_copy, which, send, land), n_gz)
        rows = send.shape[0] // n_gz
        own = send[pl.ds(pl.multiple_of(me_z * rows, 16), rows), :]
        land[me_z] = own
        total = land[0].astype(F32)
        for t in range(1, n_gz):
            total = total + land[t].astype(F32)
        exchange[me_s] = total.astype(BF16)
        start_all(functools.partial(sample_copy, which, exchange), n_s)

    def exchange_end(which, exchange, full):
        wait_all(functools.partial(sample_copy, which, exchange), n_s)
        total = exchange[0].astype(F32)
        for t in range(1, n_s):
            total = total + exchange[t].astype(F32)
        rows = full.shape[0] // n_gz
        full[pl.ds(pl.multiple_of(me_z * rows, 16), rows), :] = (total * (1.0 / (CUBES * n_s))).astype(BF16)
        start_all(functools.partial(gather_copy, which, full), n_gz)

    def half_of(ref, which):
        return ref.at[pl.ds(pl.multiple_of(which * HALF_B, 128), HALF_B), :]

    part = WIDE_B // n_gz

    def part_of(ref, t):
        return ref.at[pl.ds(pl.multiple_of(t * part, 64), part), :]

    def core_copy(stage, src, dst):
        return pltpu.make_async_remote_copy(
            src_ref=src, dst_ref=dst, send_sem=core_s.at[stage], recv_sem=core_r.at[stage],
            device_id=(me_s, me_z + 1 - 2 * core), device_id_type=MESH,
        )

    def group_copy(d):
        peer = lax.rem(mine + d, n_gz)
        return pltpu.make_async_remote_copy(
            src_ref=part_of(hs, peer), dst_ref=rb.at[mine], send_sem=rs_s.at[0, d], recv_sem=rs_r.at[0, d],
            device_id=in_group(peer), device_id_type=MESH,
        )

    def line_copy(d):
        return pltpu.make_async_remote_copy(
            src_ref=eb.at[last], dst_ref=eb.at[last], send_sem=ex_s.at[0, d], recv_sem=ex_r.at[0, d],
            device_id=in_line(lax.rem(last + d, n_e)), device_id_type=MESH,
        )

    def back_copy(d):
        return pltpu.make_async_remote_copy(
            src_ref=part_of(fh, mine), dst_ref=part_of(fh, mine), send_sem=ag_s.at[0, d], recv_sem=ag_r.at[0, d],
            device_id=in_group(lax.rem(mine + d, n_gz)), device_id_type=MESH,
        )

    def reduce_b0():
        swap = core_copy(0, half_of(sb, 1 - core), cb)
        swap.start()
        return swap

    def reduce_b1(swap):
        swap.wait()
        own = sb[pl.ds(pl.multiple_of(core * HALF_B, 128), HALF_B), :]
        hs[0:HALF_B] = (own.astype(F32) + cb[...].astype(F32)).astype(BF16)
        start_all(group_copy, n_gz)

    def reduce_b2():
        wait_all(group_copy, n_gz)
        rb[mine] = hs[pl.ds(pl.multiple_of(mine * part, 64), part), :]
        total = rb[0].astype(F32)
        for t in range(1, n_gz):
            total = total + rb[t].astype(F32)
        eb[last] = total.astype(BF16)
        start_all(line_copy, n_e)

    def reduce_b3():
        wait_all(line_copy, n_e)
        total = eb[0].astype(F32)
        for t in range(1, n_e):
            total = total + eb[t].astype(F32)
        fh[pl.ds(pl.multiple_of(mine * part, 64), part), :] = (total * (1.0 / (CUBES * n_s))).astype(BF16)
        start_all(back_copy, n_gz)

    def reduce_b4():
        wait_all(back_copy, n_gz)
        swap = core_copy(1, fh.at[0:HALF_B], fo)
        swap.start()
        wb32[pl.ds(pl.multiple_of(core * HALF_B, 128), HALF_B), :] = fh[0:HALF_B].astype(F32)
        return swap

    def reduce_b5(swap):
        swap.wait()
        wb32[pl.ds(pl.multiple_of((1 - core) * HALF_B, 128), HALF_B), :] = fo[...].astype(F32)

    swap = reduce_b0()

    def h_windows(planes):
        return jnp.concatenate([jnp.concatenate([
            hb[:, z, sy, :, 512 * j:512 * j + 768].reshape(32, 768) for z in planes for sy in range(3)
        ], axis=1) for j in range(5)], axis=0)

    window = h_windows((1, 2))
    gp_s[0] = dot_nt(window, tbd[:, 2304:6912])
    gp_s[1] = dot_nt(window, tbd[:, 0:4608])

    reduce_b1(swap)
    for copy in halo_h:
        copy.wait()
    for plane, way, keep in ((0, 0, keep_low), (3, 1, keep_high)):
        v = hh[way].astype(F32).reshape(32, 2048) * keep
        for dy, v in enumerate((rows_before(v), v, rows_after(v))):
            hb[:, plane, dy, :, 256:2304] = v.astype(BF16).reshape(CUBES, 16, 2048)

    for zp in range(2):
        gp_s[zp] = gp_s[zp] + dot_nt(h_windows((3 * zp,)), tbd[:, 4608 * zp:4608 * zp + 2304])

    @pl.loop(0, BLOCKS)
    def _(kk):
        up = gp_s[:, pl.ds(pl.multiple_of((kk // 2) * 32, 32), 32), lanes(128 * (kk % 2), 128)]
        up = jnp.concatenate([up, up], axis=2).reshape(2, CUBES, 16, 256)
        g = []
        for b in range(CUBES):
            for zp in range(2):
                g.append((ds_a[kk, 128 * b + 64 * zp:128 * b + 64 * zp + 64].reshape(4, 16, 256) * up[zp, b][None]).reshape(64, 256))
        g = jnp.concatenate(g, axis=0)
        gt[:, lanes(256 * kk, 256)] = g.astype(BF16).T
        g = g.reshape(CUBES, ZD, 2, 16, 256)
        even = g[:, :, 0].reshape(128, 256)
        odd = g[:, :, 1].reshape(128, 256)
        for group, v in enumerate((rows_before(odd), even, odd, rows_after(even))):
            ga[:, 1:1 + ZD, 16 * group:16 * group + 16, lanes(256 * kk, 256)] = v.astype(BF16).reshape(CUBES, ZD, 16, 256)

    halo_g = halo(3, ga.at[:, 1, 16:48], ga.at[:, ZD, 16:48], gh)

    def terms_a(dz):
        window = jnp.concatenate([jnp.concatenate([
            xa[:, pl.ds(dz, ZD), 16 * dy:16 * dy + 32, 128 * kk:128 * kk + 256].reshape(256, 256)
            for kk in range(BLOCKS)
        ], axis=0) for dy in range(3)], axis=1)
        all_dy = dot(gt[...], window)
        for dy in range(3):
            full = all_dy[:, 256 * dy:256 * dy + 256]
            total = jnp.zeros((64, 256), F32)
            for par in range(2):
                for pair in range(2):
                    t = 2 * pair + par
                    at = 128 * par + 64 * pair
                    total = total + pltpu.roll(full[at:at + 64], 256 - 32 * (t + 1), 1)
            total = total[:, :128]
            da[pl.ds(pl.multiple_of(dz * 288 + dy * 96, 32), 96), :] = jnp.concatenate([total, total], axis=0).T[:96]

    @pl.loop(0, 3)
    def _(dz):
        terms_a(dz)

    half = iota((ROWS_A, 128), 1) < C2
    da[864:1024, :] = jnp.zeros((160, 128), F32)
    sa[...] = jnp.where(half, da[0:512], da[512:1024]).astype(BF16)
    scatter_start(1, sa, ra)
    stores = []

    def store(src, dst):
        copy = pltpu.make_async_copy(src, dst, store_s.at[len(stores)])
        copy.start()
        stores.append(copy)

    def g_windows(jj, planes):
        return jnp.concatenate([jnp.concatenate([
            ga[:, sz:sz + ZD, 16 * sy:16 * sy + 32, 1024 * jj + 512 * i:1024 * jj + 512 * i + 768].reshape(256, 768)
            for sz in planes for sy in range(3)
        ], axis=1) for i in range(2)], axis=0)

    def middle(jj):
        part = dot_nt(g_windows(jj, (1,)), tad[:, 0:2304])
        for i in range(2):
            ds_a[2 * jj + i] = part[256 * i:256 * i + 256]

    def cubes_grad(jj):
        part = dot_nt(g_windows(jj, (0, 2)), tad[:, 2304:6912])
        for i in range(2):
            total = (part[256 * i:256 * i + 256] + ds_a[2 * jj + i]).astype(BF16)
            for b in range(CUBES):
                for z in range(ZD):
                    at = 32 * (ZD * b + z)
                    dx_ref[b, z, :, 512 * jj + 256 * i:512 * jj + 256 * i + 256] = dot(natural, total[at:at + 32]).astype(BF16)

    middle(0)
    reduce_b2()
    middle(1)
    for copy in halo_g:
        copy.wait()
    for plane, way, keep in ((0, 0, keep_low), (ZD + 1, 1, keep_high)):
        even = gh[way, :, 0:16].astype(F32).reshape(32, 2304) * keep
        odd = gh[way, :, 16:32].astype(F32).reshape(32, 2304) * keep
        for group, v in enumerate((rows_before(odd), even, odd, rows_after(even))):
            ga[:, plane, 16 * group:16 * group + 16] = v.astype(BF16).reshape(CUBES, 16, 2304)


    cubes_grad(0)
    scatter_end(1, sa, ra, ea)
    reduce_b3()
    cubes_grad(1)
    store(dx_ref, dx_hbm)
    exchange_end(1, ea, fa)
    reduce_b5(reduce_b4())

    @pl.loop(0, C2)
    def _(i):
        gb_ref[:, lanes(128 * i, 128)] = wb32[pl.ds(i, 27, stride=C2), :]

    store(gb_ref, gb_hbm)
    wait_all(functools.partial(gather_copy, 1, fa), n_gz)
    wa32[0:ROWS_A] = fa[...].astype(F32)
    first = iota((16, 128), 1) < C2

    @pl.loop(0, C1 // 2)
    def _(m):
        v = wa32[pl.ds(2 * m, 16, stride=C1), :]
        w = wa32[pl.ds(2 * m + 1, 16, stride=C1), :]
        ga_ref[0:16, lanes(128 * m, 128)] = jnp.where(first, v, pltpu.roll(w, C2, 1))
        ga_ref[16:27, lanes(128 * m, 128)] = jnp.where(first, pltpu.roll(v, C2, 1), w)[:11]

    store(ga_ref, ga_hbm)
    for copy in stores:
        copy.wait()


def pass_on(dx_in, ga_in, gb_in, dx_out, ga_out, gb_out, dx_ref, ga_ref, gb_ref, in_s, out_s):
    near, far = pl.ds(0, 4096), pl.ds(4096, 4096)
    pieces = [(dx_in.at[b], dx_ref.at[b], dx_out.at[b]) for b in range(CUBES)]
    pieces += [(gb_in.at[:, w], gb_ref.at[:, w], gb_out.at[:, w]) for w in (near, far)]
    pieces.append((ga_in, ga_ref, ga_out))
    taken = [pltpu.make_async_copy(src, via, in_s.at[i]) for i, (src, via, _) in enumerate(pieces)]
    given = [pltpu.make_async_copy(via, dst, out_s.at[i]) for i, (_, via, dst) in enumerate(pieces)]
    for copy in taken:
        copy.start()
    for arrive, leave in zip(taken, given):
        arrive.wait()
        leave.start()
    for copy in given:
        copy.wait()


def shards(n_s, n_gz, cubes, weight_a, weight_b, cotangent):
    dma = pltpu.SemaphoreType.DMA
    anywhere = pl.BlockSpec(memory_space=pl.ANY)
    ins = (cubes, weight_a, weight_b, cotangent)
    outs = (
        jax.ShapeDtypeStruct((CUBES, ZD, SIDE, SIDE * C1), BF16),
        jax.ShapeDtypeStruct((27, C1 * C2), F32),
        jax.ShapeDtypeStruct((27, C2 * C3), F32),
    )
    results = pl.pallas_call(
        functools.partial(kernel, n_s, n_gz),
        out_shape=outs,
        in_specs=[anywhere] * 4,
        out_specs=(anywhere,) * 3,
        scratch_shapes=[pltpu.VMEM(v.shape, v.dtype) for v in ins + outs] + [
            pltpu.VMEM((27 * C1, 128), F32),
            pltpu.VMEM((ROWS_B, 128), F32),
            pltpu.VMEM((CUBES, ZD + 2, 64, 1280), BF16),
            pltpu.VMEM((2304, 256), BF16),
            pltpu.VMEM((2304, 256), BF16),
            pltpu.VMEM((256, 6912), BF16),
            pltpu.VMEM((256, 6912), BF16),
            pltpu.VMEM((BLOCKS, 256, 256), F32),
            pltpu.VMEM((2, 256, 256), F32),
            pltpu.VMEM((2, 160, 256), F32),
            pltpu.VMEM((CUBES, 4, 3, 16, 1152), BF16),
            pltpu.VMEM((CUBES, 4, 3, 16, 2816), BF16),
            pltpu.VMEM((CUBES, ZD + 2, 64, 2304), BF16),
            pltpu.VMEM((256, 512), BF16),
            pltpu.VMEM((256, 2304), BF16),
            pltpu.VMEM((CUBES, 16, 1024), F32),
            pltpu.VMEM((1024, 128), F32),
            pltpu.VMEM((2, CUBES, SIDE, 1024), BF16),
            pltpu.VMEM((2, CUBES, 16, 1152), BF16),
            pltpu.VMEM((2, CUBES, 16, 2048), BF16),
            pltpu.VMEM((2, CUBES, 32, 2304), BF16),
            pltpu.VMEM((ROWS_B, 128), BF16),
            pltpu.VMEM((HALF_B, 128), BF16),
            pltpu.VMEM((WIDE_B, 128), BF16),
            pltpu.VMEM((n_gz, WIDE_B // n_gz, 128), BF16),
            pltpu.VMEM((n_s // 2, WIDE_B // n_gz, 128), BF16),
            pltpu.VMEM((WIDE_B, 128), BF16),
            pltpu.VMEM((HALF_B, 128), BF16),
            pltpu.VMEM((ROWS_A, 128), BF16),
            pltpu.VMEM((n_gz, ROWS_A // n_gz, 128), BF16),
            pltpu.VMEM((n_s, ROWS_A // n_gz, 128), BF16),
            pltpu.VMEM((ROWS_A, 128), BF16),
            dma((4,)), dma((3,)),
            dma((4, 2)), dma((4, 2)), dma((2,)), dma((2,)),
            dma((2, n_gz)), dma((2, n_gz)),
            dma((2, n_s)), dma((2, n_s)),
            dma((2, n_gz)), dma((2, n_gz)),
        ],
        compiler_params=pltpu.CompilerParams(
            collective_id=0, has_side_effects=True, vmem_limit_bytes=60 * 1024 * 1024
        ),
    )(*ins)
    return pl.pallas_call(
        pass_on,
        out_shape=outs,
        in_specs=[anywhere] * 3,
        out_specs=(anywhere,) * 3,
        scratch_shapes=[pltpu.VMEM(v.shape, v.dtype) for v in outs] + [dma((5,)), dma((5,))],
    )(*results)


def solution(mesh):
    in_specs = (P("sample", "gz", None, None), P(), P(), P("sample", "gz", None, None))
    out_specs = (P("sample", "gz", None, None), P(), P())
    body = functools.partial(shards, mesh.shape["sample"], mesh.shape["gz"])
    return jax.shard_map(body, mesh=mesh, in_specs=in_specs, out_specs=out_specs, check_vma=False)
```

```python
import functools

import jax
import jax.numpy as jnp
from jax import lax
from jax.experimental import pallas as pl
from jax.experimental.pallas import tpu as pltpu
from jax.sharding import PartitionSpec as P

C1, C2, C3 = 32, 64, 128
SIDE = 32
ZD = 4
CUBES = 2
BLOCKS = 9
F32, BF16 = jnp.float32, jnp.bfloat16
MESH = pl.DeviceIdType.MESH
ROWS_B = 1792
HALF_B = 896
WIDE_B = 1024
ROWS_A = 512


def iota(shape, dim):
    return lax.broadcasted_iota(jnp.int32, shape, dim)


def dot(a, b):
    return lax.dot_general(a, b, (((1,), (0,)), ((), ())), preferred_element_type=F32)


def dot_nt(a, b):
    return lax.dot_general(a, b, (((1,), (1,)), ((), ())), preferred_element_type=F32)


def rows_before(v):
    return jnp.where(iota(v.shape, 0) % 16 == 0, 0.0, pltpu.roll(v, 1, 0))


def rows_after(v):
    return jnp.where(iota(v.shape, 0) % 16 == 15, 0.0, pltpu.roll(v, v.shape[0] - 1, 0))


def lanes(start, size):
    return pl.ds(pl.multiple_of(start, 128), size)


def kernel(
    n_s, n_gz, x_hbm, wa_hbm, wb_hbm, cot_hbm, dx_hbm, ga_hbm, gb_hbm,
    x_ref, wa_ref, wb_ref, cot_ref, dx_ref, ga_ref, gb_ref,
    wa32, wb32, xa, ta, tb, tad, tbd, ds_a, pre_s, gp_s, pb, hb, ga, ht, gt, cs, da,
    xh, ph, hh, gh, sb, cb, hs, rb, eb, fh, fo, sa, ra, ea, fa,
    load_s, store_s, halo_s, halo_r, core_s, core_r, rs_s, rs_r, ex_s, ex_r, ag_s, ag_r,
):
    me_s = lax.axis_index("sample")
    me_z = lax.axis_index("gz")
    low = lax.rem(me_z + n_gz - 1, n_gz)
    high = lax.rem(me_z + 1, n_gz)
    keep_low = (me_z > 0).astype(F32)
    keep_high = (me_z < n_gz - 1).astype(F32)

    core, y_lo, at_z = me_z % 2, (me_z // 2) % 2, me_z // 4
    at_x, y_hi = me_s // 2, me_s % 2
    n_e = n_s // 2
    mine = (core * at_x + (1 - core) * at_z) * 4 + y_hi * 2 + y_lo
    last = core * at_z + (1 - core) * at_x

    def in_group(t):
        a, y = t // 4, t % 4
        to_x = core * a + (1 - core) * at_x
        to_z = (1 - core) * a + core * at_z
        return (to_x * 2 + y // 2, to_z * 4 + (y % 2) * 2 + core)

    def in_line(e):
        to_x = core * at_x + (1 - core) * e
        to_z = (1 - core) * at_z + core * e
        return (to_x * 2 + y_hi, to_z * 4 + y_lo * 2 + core)

    barrier = pltpu.get_barrier_semaphore()

    @pl.loop(1, n_gz)
    def _(d):
        pl.semaphore_signal(barrier, inc=1, device_id=in_group(lax.rem(mine + d, n_gz)), device_id_type=MESH)

    @pl.loop(1, n_gz)
    def _(d):
        pl.semaphore_signal(barrier, inc=1, device_id=(me_s, lax.rem(me_z + d, n_gz)), device_id_type=MESH)

    @pl.loop(1, n_s)
    def _(d):
        pl.semaphore_signal(barrier, inc=1, device_id=(lax.rem(me_s + d, n_s), me_z), device_id_type=MESH)

    loads = [
        pltpu.make_async_copy(src, dst, load_s.at[i])
        for i, (src, dst) in enumerate(((wa_hbm, wa_ref), (wb_hbm, wb_ref), (x_hbm, x_ref), (cot_hbm, cot_ref)))
    ]
    for load in loads:
        load.start()

    def halo(stage, low_plane, high_plane, landing, start=True):
        pair = []
        for way, (src, peer) in enumerate(((high_plane, high), (low_plane, low))):
            copy = pltpu.make_async_remote_copy(
                src_ref=src, dst_ref=landing(way),
                send_sem=halo_s.at[stage, way], recv_sem=halo_r.at[stage, way],
                device_id=(me_s, peer), device_id_type=MESH,
            )
            if start:
                copy.start()
            pair.append(copy)
        return pair

    def pooled_piece(kt, start):
        w = lanes(384 * kt, 384)
        return halo(2 + kt, pb.at[:, 1, 1, :, w], pb.at[:, 2, 1, :, w], lambda way: ph.at[way, :, :, w], start)

    def grad_piece(kt, start):
        w = lanes(768 * kt, 768)
        return halo(5 + kt, ga.at[:, 1, 16:48, w], ga.at[:, ZD, 16:48, w], lambda way: gh.at[way, :, :, w], start)

    half = iota((27, 128), 1) < C2
    loads[0].wait()

    @pl.loop(0, C1 // 2)
    def _(m):
        v = wa_ref[:, lanes(128 * m, 128)].astype(F32)
        w = pltpu.roll(v, C2, 1)
        wa32[pl.ds(2 * m, 27, stride=C1), :] = jnp.where(half, v, w)
        wa32[pl.ds(2 * m + 1, 27, stride=C1), :] = jnp.where(half, w, v)

    loads[1].wait()

    @pl.loop(0, C2)
    def _(i):
        wb32[pl.ds(i, 27, stride=C2), :] = wb_ref[:, lanes(128 * i, 128)].astype(F32)

    pl.semaphore_wait(barrier, 2 * n_gz + n_s - 3)
    halo_x = halo(0, x_hbm.at[:, 0], x_hbm.at[:, ZD - 1], lambda way: xh.at[way])

    zero_a = jnp.zeros((C1, 128), BF16)
    zero_b = jnp.zeros((C2, 128), BF16)
    left = iota((C1, 128), 1) < C2

    def taps_a(zy):
        at = pl.multiple_of(zy * 3 * C1, C1)
        full = wa32[pl.ds(at, 3 * C1), :].astype(BF16)
        taps = [full[C1 * i:C1 * i + C1] for i in range(3)]

        def two(dx0, dx1):
            first = taps[dx0 + 1] if -1 <= dx0 <= 1 else zero_a
            second = taps[dx1 + 1] if -1 <= dx1 <= 1 else zero_a
            if first is second:
                return zero_a
            return jnp.where(left, first, second)

        return two

    def taps_b(zy):
        at = pl.multiple_of(zy * 3 * C2, C2)
        full = wb32[pl.ds(at, 3 * C2), :].astype(BF16)
        taps = [full[C2 * i:C2 * i + C2] for i in range(3)]
        return lambda dx: taps[dx + 1] if -1 <= dx <= 1 else zero_b

    @pl.loop(0, 9)
    def _(zy):
        dz = zy // 3
        base = (jnp.where(dz == 2, 2, 1 - dz) * 3 + zy % 3) * 256
        two = taps_a(zy)
        for p in range(8):
            for par in range(2):
                ta[pl.ds(pl.multiple_of(base + 32 * p, 32), 32), 128 * par:128 * par + 128] = two(p - 2 - par, p - 4 - par)

    spread_rows = (iota((64, SIDE), 1) == 2 * (iota((64, SIDE), 0) % 16) + iota((64, SIDE), 0) // 16 - 1).astype(BF16)
    spread_cot = (iota((16, 8), 0) // 2 == iota((16, 8), 1)).astype(BF16)
    natural = (iota((SIDE, SIDE), 1) == (iota((SIDE, SIDE), 0) % 2) * 16 + iota((SIDE, SIDE), 0) // 2).astype(BF16)
    edge = jnp.zeros((CUBES, ZD + 2, 64, 128), BF16)
    xa[:, :, :, 0:128] = edge
    xa[:, :, :, 1152:1280] = edge
    loads[2].wait()
    for b in range(CUBES):
        for z in range(ZD):
            xa[b, z + 1, :, 128:1152] = dot(spread_rows, x_ref[b, z]).astype(BF16)

    def x_windows(kt, planes):
        return jnp.concatenate([jnp.concatenate([
            xa[:, dz:dz + ZD, 16 * dy:16 * dy + 32, lanes(384 * kt + 128 * i, 256)].reshape(256, 256)
            for dz in planes for dy in range(3)
        ], axis=1) for i in range(3)], axis=0)

    @pl.loop(0, 3)
    def _(kt):
        part = dot(x_windows(kt, (1,)), ta[0:768])
        for i in range(3):
            ds_a[3 * kt + i] = part[256 * i:256 * i + 256]

    loads[3].wait()
    for b in range(CUBES):
        cs[b] = dot(spread_cot, cot_ref[b, 0]) * 0.125
    hb[:, :, :, :, 0:256] = jnp.zeros((CUBES, 4, 3, 16, 256), BF16)
    hb[:, :, :, :, 2304:2816] = jnp.zeros((CUBES, 4, 3, 16, 512), BF16)
    for copy in halo_x:
        copy.wait()
    for b in range(CUBES):
        xa[b, 0, :, 128:1152] = (dot(spread_rows, xh[0, b]) * keep_low).astype(BF16)
        xa[b, ZD + 1, :, 128:1152] = (dot(spread_rows, xh[1, b]) * keep_high).astype(BF16)

    @pl.loop(0, 3)
    def _(kt):
        part = dot(x_windows(kt, (0, 2)), ta[768:2304])
        for i in range(3):
            kk = 3 * kt + i
            pre = part[256 * i:256 * i + 256] + ds_a[kk]
            place = 2 * kk - 1 + (iota((1, 128), 1) // C2)
            inside = ((place >= 0) & (place < SIDE // 2)).astype(F32) * 0.125
            s = 0.5 * jnp.tanh(0.5 * pre) + 0.5
            act = pre * s
            slope = s + act * (1.0 - s)
            ds_a[kk] = slope * jnp.concatenate([inside, inside], axis=1)
            act = (act[:, :128] + act[:, 128:]).reshape(CUBES, 2, 2, 2, 16, 128)
            pooled = (act[:, :, 0, 0] + act[:, :, 0, 1] + act[:, :, 1, 0] + act[:, :, 1, 1]).reshape(64, 128) * inside
            for dy, v in enumerate((rows_before(pooled), pooled, rows_after(pooled))):
                pb[:, 1:3, dy, :, lanes(128 * kk, 128)] = v.astype(BF16).reshape(CUBES, 2, 16, 128)

        pooled_piece(kt, True)

    halo_p = [copy for kt in range(3) for copy in pooled_piece(kt, False)]

    @pl.loop(0, 9)
    def _(zy):
        base = zy * 256
        tap = taps_b(zy)
        for p in range(4):
            for q in range(2):
                tb[pl.ds(pl.multiple_of(base + 64 * p, 64), 64), 128 * q:128 * q + 128] = tap(p - 1 - q)

    def p_windows(planes):
        return jnp.concatenate([jnp.concatenate([
            pb[:, z, dy, :, 128 * k:128 * k + 256].reshape(32, 256) for z in planes for dy in range(3)
        ], axis=1) for k in range(8)], axis=0)

    window = p_windows((1, 2))
    pre_s[0] = dot(window, tb[768:2304])
    pre_s[1] = dot(window, tb[0:1536])

    @pl.loop(0, 9)
    def _(s):
        tap = taps_b(8 - s)
        for r in range(4):
            for p in range(6):
                tbd[64 * r:64 * r + 64, lanes(s * 768 + 128 * p, 128)] = tap(r + 1 - p)

    @pl.loop(0, 9)
    def _(s):
        two = taps_a(8 - s)
        sz = s // 3
        base = (jnp.where(sz == 2, 2, 1 - sz) * 3 + s % 3) * 768
        for r in range(8):
            for kk in range(3):
                for par in range(2):
                    dx = r + 2 - 4 * kk - par
                    tad[32 * r:32 * r + 32, lanes(base + 256 * kk + 128 * par, 128)] = two(dx, dx - 2)

    for copy in halo_p:
        copy.wait()
    for plane, way, keep in ((0, 0, keep_low), (3, 1, keep_high)):
        v = ph[way].astype(F32).reshape(32, 1152) * keep
        for dy, v in enumerate((rows_before(v), v, rows_after(v))):
            pb[:, plane, dy] = v.astype(BF16).reshape(CUBES, 16, 1152)

    for zp in range(2):
        pre = pre_s[zp] + dot(p_windows((3 * zp,)), tb[1536 * zp:1536 * zp + 768])
        s = 0.5 * jnp.tanh(0.5 * pre) + 0.5
        slope = s + pre * s * (1.0 - s)
        grads = []
        for k in range(8):
            up = cs[:, :, 128 * k:128 * k + 128].reshape(32, 128)
            h = slope[32 * k:32 * k + 32] * jnp.concatenate([up, up], axis=1)
            grads.append(h)
            for dy, v in enumerate((rows_before(h), h, rows_after(h))):
                hb[:, 1 + zp, dy, :, 256 + 256 * k:512 + 256 * k] = v.astype(BF16).reshape(CUBES, 16, 256)
        ht[:, 256 * zp:256 * zp + 256] = jnp.concatenate(grads, axis=0).astype(BF16).T

    halo_h = halo(1, hb.at[:, 1, 1, :, 256:2304], hb.at[:, 2, 1, :, 256:2304], lambda way: hh.at[way])

    @pl.loop(0, 3)
    def _(dz):
        window = jnp.concatenate([jnp.concatenate([
            pb[:, dz + zp, dy, :, 128 * k:128 * k + 256].reshape(32, 256) for zp in range(2) for k in range(8)
        ], axis=0) for dy in range(3)], axis=1)
        all_dy = dot(ht[...], window)
        for dy in range(3):
            full = all_dy[:, 256 * dy:256 * dy + 256]
            diag = full[:128] + pltpu.roll(full[128:], 192, 1)
            sb[pl.ds(pl.multiple_of(dz * 576 + dy * 192, 64), 192), :] = diag.astype(BF16).T[:192]

    sb[1728:ROWS_B, :] = jnp.zeros((ROWS_B - 1728, 128), BF16)
    hs[HALF_B:, :] = jnp.zeros((WIDE_B - HALF_B, 128), BF16)

    def shard(ref, n, index):
        rows = ref.shape[0] // n
        return ref.at[pl.ds(pl.multiple_of(index * rows, 16), rows), :]

    def scatter_copy(which, send, land, d):
        peer = lax.rem(me_z + d, n_gz)
        return pltpu.make_async_remote_copy(
            src_ref=shard(send, n_gz, peer), dst_ref=land.at[me_z],
            send_sem=rs_s.at[which, d], recv_sem=rs_r.at[which, d],
            device_id=(me_s, peer), device_id_type=MESH,
        )

    def sample_copy(which, land, d):
        peer = lax.rem(me_s + d, n_s)
        return pltpu.make_async_remote_copy(
            src_ref=land.at[me_s], dst_ref=land.at[me_s],
            send_sem=ex_s.at[which, d], recv_sem=ex_r.at[which, d],
            device_id=(peer, me_z), device_id_type=MESH,
        )

    def gather_copy(which, full, d):
        peer = lax.rem(me_z + d, n_gz)
        return pltpu.make_async_remote_copy(
            src_ref=shard(full, n_gz, me_z), dst_ref=shard(full, n_gz, me_z),
            send_sem=ag_s.at[which, d], recv_sem=ag_r.at[which, d],
            device_id=(me_s, peer), device_id_type=MESH,
        )

    def start_all(make, n):
        @pl.loop(1, n)
        def _(d):
            make(d).start()

    def wait_all(make, n):
        @pl.loop(1, n)
        def _(d):
            make(d).wait()

    def scatter_start(which, send, land):
        start_all(functools.partial(scatter_copy, which, send, land), n_gz)

    def scatter_end(which, send, land, exchange):
        wait_all(functools.partial(scatter_copy, which, send, land), n_gz)
        rows = send.shape[0] // n_gz
        own = send[pl.ds(pl.multiple_of(me_z * rows, 16), rows), :]
        land[me_z] = own
        total = land[0].astype(F32)
        for t in range(1, n_gz):
            total = total + land[t].astype(F32)
        exchange[me_s] = total.astype(BF16)
        start_all(functools.partial(sample_copy, which, exchange), n_s)

    def exchange_end(which, exchange, full):
        wait_all(functools.partial(sample_copy, which, exchange), n_s)
        total = exchange[0].astype(F32)
        for t in range(1, n_s):
            total = total + exchange[t].astype(F32)
        rows = full.shape[0] // n_gz
        full[pl.ds(pl.multiple_of(me_z * rows, 16), rows), :] = (total * (1.0 / (CUBES * n_s))).astype(BF16)
        start_all(functools.partial(gather_copy, which, full), n_gz)

    def half_of(ref, which):
        return ref.at[pl.ds(pl.multiple_of(which * HALF_B, 128), HALF_B), :]

    part = WIDE_B // n_gz

    def part_of(ref, t):
        return ref.at[pl.ds(pl.multiple_of(t * part, 64), part), :]

    def core_copy(stage, src, dst):
        return pltpu.make_async_remote_copy(
            src_ref=src, dst_ref=dst, send_sem=core_s.at[stage], recv_sem=core_r.at[stage],
            device_id=(me_s, me_z + 1 - 2 * core), device_id_type=MESH,
        )

    def group_copy(d):
        peer = lax.rem(mine + d, n_gz)
        return pltpu.make_async_remote_copy(
            src_ref=part_of(hs, peer), dst_ref=rb.at[mine], send_sem=rs_s.at[0, d], recv_sem=rs_r.at[0, d],
            device_id=in_group(peer), device_id_type=MESH,
        )

    def line_copy(d):
        return pltpu.make_async_remote_copy(
            src_ref=eb.at[last], dst_ref=eb.at[last], send_sem=ex_s.at[0, d], recv_sem=ex_r.at[0, d],
            device_id=in_line(lax.rem(last + d, n_e)), device_id_type=MESH,
        )

    def back_copy(d):
        return pltpu.make_async_remote_copy(
            src_ref=part_of(fh, mine), dst_ref=part_of(fh, mine), send_sem=ag_s.at[0, d], recv_sem=ag_r.at[0, d],
            device_id=in_group(lax.rem(mine + d, n_gz)), device_id_type=MESH,
        )

    def reduce_b0():
        swap = core_copy(0, half_of(sb, 1 - core), cb)
        swap.start()
        return swap

    def reduce_b1(swap):
        swap.wait()
        own = sb[pl.ds(pl.multiple_of(core * HALF_B, 128), HALF_B), :]
        hs[0:HALF_B] = (own.astype(F32) + cb[...].astype(F32)).astype(BF16)
        start_all(group_copy, n_gz)

    def reduce_b2():
        wait_all(group_copy, n_gz)
        rb[mine] = hs[pl.ds(pl.multiple_of(mine * part, 64), part), :]
        total = rb[0].astype(F32)
        for t in range(1, n_gz):
            total = total + rb[t].astype(F32)
        eb[last] = total.astype(BF16)
        start_all(line_copy, n_e)

    def reduce_b3():
        wait_all(line_copy, n_e)
        total = eb[0].astype(F32)
        for t in range(1, n_e):
            total = total + eb[t].astype(F32)
        fh[pl.ds(pl.multiple_of(mine * part, 64), part), :] = (total * (1.0 / (CUBES * n_s))).astype(BF16)
        start_all(back_copy, n_gz)

    def reduce_b4():
        wait_all(back_copy, n_gz)
        swap = core_copy(1, fh.at[0:HALF_B], fo)
        swap.start()
        wb32[pl.ds(pl.multiple_of(core * HALF_B, 128), HALF_B), :] = fh[0:HALF_B].astype(F32)
        return swap

    def reduce_b5(swap):
        swap.wait()
        wb32[pl.ds(pl.multiple_of((1 - core) * HALF_B, 128), HALF_B), :] = fo[...].astype(F32)

    swap = reduce_b0()

    def h_windows(planes):
        return jnp.concatenate([jnp.concatenate([
            hb[:, z, sy, :, 512 * j:512 * j + 768].reshape(32, 768) for z in planes for sy in range(3)
        ], axis=1) for j in range(5)], axis=0)

    window = h_windows((1, 2))
    gp_s[0] = dot_nt(window, tbd[:, 2304:6912])
    gp_s[1] = dot_nt(window, tbd[:, 0:4608])

    reduce_b1(swap)
    for copy in halo_h:
        copy.wait()
    for plane, way, keep in ((0, 0, keep_low), (3, 1, keep_high)):
        v = hh[way].astype(F32).reshape(32, 2048) * keep
        for dy, v in enumerate((rows_before(v), v, rows_after(v))):
            hb[:, plane, dy, :, 256:2304] = v.astype(BF16).reshape(CUBES, 16, 2048)

    for zp in range(2):
        gp_s[zp] = gp_s[zp] + dot_nt(h_windows((3 * zp,)), tbd[:, 4608 * zp:4608 * zp + 2304])

    def first_grad(kk):
        up = gp_s[:, pl.ds(pl.multiple_of((kk // 2) * 32, 32), 32), lanes(128 * (kk % 2), 128)]
        up = jnp.concatenate([up, up], axis=2).reshape(2, CUBES, 16, 256)
        g = []
        for b in range(CUBES):
            for zp in range(2):
                g.append((ds_a[kk, 128 * b + 64 * zp:128 * b + 64 * zp + 64].reshape(4, 16, 256) * up[zp, b][None]).reshape(64, 256))
        g = jnp.concatenate(g, axis=0)
        gt[:, lanes(256 * kk, 256)] = g.astype(BF16).T
        g = g.reshape(CUBES, ZD, 2, 16, 256)
        even = g[:, :, 0].reshape(128, 256)
        odd = g[:, :, 1].reshape(128, 256)
        for group, v in enumerate((rows_before(odd), even, odd, rows_after(even))):
            ga[:, 1:1 + ZD, 16 * group:16 * group + 16, lanes(256 * kk, 256)] = v.astype(BF16).reshape(CUBES, ZD, 16, 256)

    @pl.loop(0, 3)
    def _(kt):
        @pl.loop(0, 3)
        def _(i):
            first_grad(3 * kt + i)

        grad_piece(kt, True)

    halo_g = [copy for kt in range(3) for copy in grad_piece(kt, False)]

    def terms_a(dz):
        window = jnp.concatenate([jnp.concatenate([
            xa[:, pl.ds(dz, ZD), 16 * dy:16 * dy + 32, 128 * kk:128 * kk + 256].reshape(256, 256)
            for kk in range(BLOCKS)
        ], axis=0) for dy in range(3)], axis=1)
        all_dy = dot(gt[...], window)
        for dy in range(3):
            full = all_dy[:, 256 * dy:256 * dy + 256]
            total = jnp.zeros((64, 256), F32)
            for par in range(2):
                for pair in range(2):
                    t = 2 * pair + par
                    at = 128 * par + 64 * pair
                    total = total + pltpu.roll(full[at:at + 64], 256 - 32 * (t + 1), 1)
            total = total[:, :128]
            da[pl.ds(pl.multiple_of(dz * 288 + dy * 96, 32), 96), :] = jnp.concatenate([total, total], axis=0).T[:96]

    @pl.loop(0, 3)
    def _(dz):
        terms_a(dz)

    half = iota((ROWS_A, 128), 1) < C2
    da[864:1024, :] = jnp.zeros((160, 128), F32)
    sa[...] = jnp.where(half, da[0:512], da[512:1024]).astype(BF16)
    scatter_start(1, sa, ra)
    stores = []

    def store(src, dst):
        copy = pltpu.make_async_copy(src, dst, store_s.at[len(stores)])
        copy.start()
        stores.append(copy)

    def g_windows(jj, planes):
        return jnp.concatenate([jnp.concatenate([
            ga[:, sz:sz + ZD, 16 * sy:16 * sy + 32, 1024 * jj + 512 * i:1024 * jj + 512 * i + 768].reshape(256, 768)
            for sz in planes for sy in range(3)
        ], axis=1) for i in range(2)], axis=0)

    def middle(jj):
        part = dot_nt(g_windows(jj, (1,)), tad[:, 0:2304])
        for i in range(2):
            ds_a[2 * jj + i] = part[256 * i:256 * i + 256]

    def cubes_grad(jj):
        part = dot_nt(g_windows(jj, (0, 2)), tad[:, 2304:6912])
        for i in range(2):
            total = (part[256 * i:256 * i + 256] + ds_a[2 * jj + i]).astype(BF16)
            for b in range(CUBES):
                for z in range(ZD):
                    at = 32 * (ZD * b + z)
                    dx_ref[b, z, :, 512 * jj + 256 * i:512 * jj + 256 * i + 256] = dot(natural, total[at:at + 32]).astype(BF16)

    middle(0)
    reduce_b2()
    middle(1)
    for copy in halo_g:
        copy.wait()
    for plane, way, keep in ((0, 0, keep_low), (ZD + 1, 1, keep_high)):
        even = gh[way, :, 0:16].astype(F32).reshape(32, 2304) * keep
        odd = gh[way, :, 16:32].astype(F32).reshape(32, 2304) * keep
        for group, v in enumerate((rows_before(odd), even, odd, rows_after(even))):
            ga[:, plane, 16 * group:16 * group + 16] = v.astype(BF16).reshape(CUBES, 16, 2304)


    cubes_grad(0)
    scatter_end(1, sa, ra, ea)
    reduce_b3()
    cubes_grad(1)
    store(dx_ref, dx_hbm)
    exchange_end(1, ea, fa)
    reduce_b5(reduce_b4())

    @pl.loop(0, C2)
    def _(i):
        gb_ref[:, lanes(128 * i, 128)] = wb32[pl.ds(i, 27, stride=C2), :]

    store(gb_ref, gb_hbm)
    wait_all(functools.partial(gather_copy, 1, fa), n_gz)
    wa32[0:ROWS_A] = fa[...].astype(F32)
    first = iota((16, 128), 1) < C2

    @pl.loop(0, C1 // 2)
    def _(m):
        v = wa32[pl.ds(2 * m, 16, stride=C1), :]
        w = wa32[pl.ds(2 * m + 1, 16, stride=C1), :]
        ga_ref[0:16, lanes(128 * m, 128)] = jnp.where(first, v, pltpu.roll(w, C2, 1))
        ga_ref[16:27, lanes(128 * m, 128)] = jnp.where(first, pltpu.roll(v, C2, 1), w)[:11]

    store(ga_ref, ga_hbm)
    for copy in stores:
        copy.wait()


def pass_on(dx_in, ga_in, gb_in, dx_out, ga_out, gb_out, dx_ref, ga_ref, gb_ref, in_s, out_s):
    near, far = pl.ds(0, 4096), pl.ds(4096, 4096)
    pieces = [(dx_in.at[b], dx_ref.at[b], dx_out.at[b]) for b in range(CUBES)]
    pieces += [(gb_in.at[:, w], gb_ref.at[:, w], gb_out.at[:, w]) for w in (near, far)]
    pieces.append((ga_in, ga_ref, ga_out))
    taken = [pltpu.make_async_copy(src, via, in_s.at[i]) for i, (src, via, _) in enumerate(pieces)]
    given = [pltpu.make_async_copy(via, dst, out_s.at[i]) for i, (_, via, dst) in enumerate(pieces)]
    for copy in taken:
        copy.start()
    for arrive, leave in zip(taken, given):
        arrive.wait()
        leave.start()
    for copy in given:
        copy.wait()


def shards(n_s, n_gz, cubes, weight_a, weight_b, cotangent):
    dma = pltpu.SemaphoreType.DMA
    anywhere = pl.BlockSpec(memory_space=pl.ANY)
    ins = (cubes, weight_a, weight_b, cotangent)
    outs = (
        jax.ShapeDtypeStruct((CUBES, ZD, SIDE, SIDE * C1), BF16),
        jax.ShapeDtypeStruct((27, C1 * C2), F32),
        jax.ShapeDtypeStruct((27, C2 * C3), F32),
    )
    results = pl.pallas_call(
        functools.partial(kernel, n_s, n_gz),
        out_shape=outs,
        in_specs=[anywhere] * 4,
        out_specs=(anywhere,) * 3,
        scratch_shapes=[pltpu.VMEM(v.shape, v.dtype) for v in ins + outs] + [
            pltpu.VMEM((27 * C1, 128), F32),
            pltpu.VMEM((ROWS_B, 128), F32),
            pltpu.VMEM((CUBES, ZD + 2, 64, 1280), BF16),
            pltpu.VMEM((2304, 256), BF16),
            pltpu.VMEM((2304, 256), BF16),
            pltpu.VMEM((256, 6912), BF16),
            pltpu.VMEM((256, 6912), BF16),
            pltpu.VMEM((BLOCKS, 256, 256), F32),
            pltpu.VMEM((2, 256, 256), F32),
            pltpu.VMEM((2, 160, 256), F32),
            pltpu.VMEM((CUBES, 4, 3, 16, 1152), BF16),
            pltpu.VMEM((CUBES, 4, 3, 16, 2816), BF16),
            pltpu.VMEM((CUBES, ZD + 2, 64, 2304), BF16),
            pltpu.VMEM((256, 512), BF16),
            pltpu.VMEM((256, 2304), BF16),
            pltpu.VMEM((CUBES, 16, 1024), F32),
            pltpu.VMEM((1024, 128), F32),
            pltpu.VMEM((2, CUBES, SIDE, 1024), BF16),
            pltpu.VMEM((2, CUBES, 16, 1152), BF16),
            pltpu.VMEM((2, CUBES, 16, 2048), BF16),
            pltpu.VMEM((2, CUBES, 32, 2304), BF16),
            pltpu.VMEM((ROWS_B, 128), BF16),
            pltpu.VMEM((HALF_B, 128), BF16),
            pltpu.VMEM((WIDE_B, 128), BF16),
            pltpu.VMEM((n_gz, WIDE_B // n_gz, 128), BF16),
            pltpu.VMEM((n_s // 2, WIDE_B // n_gz, 128), BF16),
            pltpu.VMEM((WIDE_B, 128), BF16),
            pltpu.VMEM((HALF_B, 128), BF16),
            pltpu.VMEM((ROWS_A, 128), BF16),
            pltpu.VMEM((n_gz, ROWS_A // n_gz, 128), BF16),
            pltpu.VMEM((n_s, ROWS_A // n_gz, 128), BF16),
            pltpu.VMEM((ROWS_A, 128), BF16),
            dma((4,)), dma((3,)),
            dma((8, 2)), dma((8, 2)), dma((2,)), dma((2,)),
            dma((2, n_gz)), dma((2, n_gz)),
            dma((2, n_s)), dma((2, n_s)),
            dma((2, n_gz)), dma((2, n_gz)),
        ],
        compiler_params=pltpu.CompilerParams(
            collective_id=0, has_side_effects=True, vmem_limit_bytes=60 * 1024 * 1024
        ),
    )(*ins)
    return pl.pallas_call(
        pass_on,
        out_shape=outs,
        in_specs=[anywhere] * 3,
        out_specs=(anywhere,) * 3,
        scratch_shapes=[pltpu.VMEM(v.shape, v.dtype) for v in outs] + [dma((5,)), dma((5,))],
    )(*results)


def solution(mesh):
    in_specs = (P("sample", "gz", None, None), P(), P(), P("sample", "gz", None, None))
    out_specs = (P("sample", "gz", None, None), P(), P())
    body = functools.partial(shards, mesh.shape["sample"], mesh.shape["gz"])
    return jax.shard_map(body, mesh=mesh, in_specs=in_specs, out_specs=out_specs, check_vma=False)
```

```python
import functools

import jax
import jax.numpy as jnp
from jax import lax
from jax.experimental import pallas as pl
from jax.experimental.pallas import tpu as pltpu
from jax.sharding import PartitionSpec as P

C1, C2, C3 = 32, 64, 128
SIDE = 32
ZD = 4
CUBES = 2
BLOCKS = 9
F32, BF16 = jnp.float32, jnp.bfloat16
MESH = pl.DeviceIdType.MESH
ROWS_B = 1792
HALF_B = 896
WIDE_B = 1024
ROWS_A = 512


def iota(shape, dim):
    return lax.broadcasted_iota(jnp.int32, shape, dim)


def dot(a, b):
    return lax.dot_general(a, b, (((1,), (0,)), ((), ())), preferred_element_type=F32)


def dot_nt(a, b):
    return lax.dot_general(a, b, (((1,), (1,)), ((), ())), preferred_element_type=F32)


def rows_before(v):
    return jnp.where(iota(v.shape, 0) % 16 == 0, 0.0, pltpu.roll(v, 1, 0))


def rows_after(v):
    return jnp.where(iota(v.shape, 0) % 16 == 15, 0.0, pltpu.roll(v, v.shape[0] - 1, 0))


def lanes(start, size):
    return pl.ds(pl.multiple_of(start, 128), size)


def kernel(
    n_s, n_gz, x_hbm, wa_hbm, wb_hbm, cot_hbm, dx_hbm, ga_hbm, gb_hbm,
    x_ref, wa_ref, wb_ref, cot_ref, dx_ref, ga_ref, gb_ref,
    wa32, wb32, xa, ta, tb, tad, tbd, ds_a, pre_s, gp_s, pb, hb, ga, ht, gt, cs, da,
    xh, ph, hh, gh, sb, cb, hs, rb, eb, fh, fo, sa, ra, ea, fa,
    load_s, store_s, halo_s, halo_r, core_s, core_r, rs_s, rs_r, ex_s, ex_r, ag_s, ag_r,
):
    me_s = lax.axis_index("sample")
    me_z = lax.axis_index("gz")
    low = lax.rem(me_z + n_gz - 1, n_gz)
    high = lax.rem(me_z + 1, n_gz)
    keep_low = (me_z > 0).astype(F32)
    keep_high = (me_z < n_gz - 1).astype(F32)

    core, y_lo, at_z = me_z % 2, (me_z // 2) % 2, me_z // 4
    at_x, y_hi = me_s // 2, me_s % 2
    n_e = n_s // 2
    mine = (core * at_x + (1 - core) * at_z) * 4 + y_hi * 2 + y_lo
    last = core * at_z + (1 - core) * at_x

    def in_group(t):
        a, y = t // 4, t % 4
        to_x = core * a + (1 - core) * at_x
        to_z = (1 - core) * a + core * at_z
        return (to_x * 2 + y // 2, to_z * 4 + (y % 2) * 2 + core)

    def in_line(e):
        to_x = core * at_x + (1 - core) * e
        to_z = (1 - core) * at_z + core * e
        return (to_x * 2 + y_hi, to_z * 4 + y_lo * 2 + core)

    barrier = pltpu.get_barrier_semaphore()

    @pl.loop(1, n_gz)
    def _(d):
        pl.semaphore_signal(barrier, inc=1, device_id=in_group(lax.rem(mine + d, n_gz)), device_id_type=MESH)

    @pl.loop(1, n_gz)
    def _(d):
        pl.semaphore_signal(barrier, inc=1, device_id=(me_s, lax.rem(me_z + d, n_gz)), device_id_type=MESH)

    @pl.loop(1, n_s)
    def _(d):
        pl.semaphore_signal(barrier, inc=1, device_id=(lax.rem(me_s + d, n_s), me_z), device_id_type=MESH)

    loads = [
        pltpu.make_async_copy(src, dst, load_s.at[i])
        for i, (src, dst) in enumerate(((wa_hbm, wa_ref), (wb_hbm, wb_ref), (x_hbm, x_ref), (cot_hbm, cot_ref)))
    ]
    for load in loads:
        load.start()

    def halo(stage, low_plane, high_plane, landing, start=True):
        pair = []
        for way, (src, peer) in enumerate(((high_plane, high), (low_plane, low))):
            copy = pltpu.make_async_remote_copy(
                src_ref=src, dst_ref=landing(way),
                send_sem=halo_s.at[stage, way], recv_sem=halo_r.at[stage, way],
                device_id=(me_s, peer), device_id_type=MESH,
            )
            if start:
                copy.start()
            pair.append(copy)
        return pair

    def pooled_piece(kt, start):
        w = lanes(384 * kt, 384)
        return halo(2 + kt, pb.at[:, 1, 1, :, w], pb.at[:, 2, 1, :, w], lambda way: ph.at[way, :, :, w], start)

    def grad_piece(kt, start):
        w = lanes(768 * kt, 768)
        return halo(5 + kt, ga.at[:, 1, 16:48, w], ga.at[:, ZD, 16:48, w], lambda way: gh.at[way, :, :, w], start)

    half = iota((27, 128), 1) < C2
    loads[0].wait()

    @pl.loop(0, C1 // 2)
    def _(m):
        v = wa_ref[:, lanes(128 * m, 128)].astype(F32)
        w = pltpu.roll(v, C2, 1)
        wa32[pl.ds(2 * m, 27, stride=C1), :] = jnp.where(half, v, w)
        wa32[pl.ds(2 * m + 1, 27, stride=C1), :] = jnp.where(half, w, v)

    loads[1].wait()

    @pl.loop(0, C2)
    def _(i):
        wb32[pl.ds(i, 27, stride=C2), :] = wb_ref[:, lanes(128 * i, 128)].astype(F32)

    pl.semaphore_wait(barrier, 2 * n_gz + n_s - 3)
    halo_x = halo(0, x_hbm.at[:, 0], x_hbm.at[:, ZD - 1], lambda way: xh.at[way])

    zero_a = jnp.zeros((C1, 128), BF16)
    zero_b = jnp.zeros((C2, 128), BF16)
    left = iota((C1, 128), 1) < C2

    def taps_a(zy):
        at = pl.multiple_of(zy * 3 * C1, C1)
        full = wa32[pl.ds(at, 3 * C1), :].astype(BF16)
        taps = [full[C1 * i:C1 * i + C1] for i in range(3)]

        def two(dx0, dx1):
            first = taps[dx0 + 1] if -1 <= dx0 <= 1 else zero_a
            second = taps[dx1 + 1] if -1 <= dx1 <= 1 else zero_a
            if first is second:
                return zero_a
            return jnp.where(left, first, second)

        return two

    def taps_b(zy):
        at = pl.multiple_of(zy * 3 * C2, C2)
        full = wb32[pl.ds(at, 3 * C2), :].astype(BF16)
        taps = [full[C2 * i:C2 * i + C2] for i in range(3)]
        return lambda dx: taps[dx + 1] if -1 <= dx <= 1 else zero_b

    @pl.loop(0, 9)
    def _(zy):
        dz = zy // 3
        base = (jnp.where(dz == 2, 2, 1 - dz) * 3 + zy % 3) * 256
        two = taps_a(zy)
        for p in range(8):
            for par in range(2):
                ta[pl.ds(pl.multiple_of(base + 32 * p, 32), 32), 128 * par:128 * par + 128] = two(p - 2 - par, p - 4 - par)

    spread_rows = (iota((64, SIDE), 1) == 2 * (iota((64, SIDE), 0) % 16) + iota((64, SIDE), 0) // 16 - 1).astype(BF16)
    spread_cot = (iota((16, 8), 0) // 2 == iota((16, 8), 1)).astype(BF16)
    natural = (iota((SIDE, SIDE), 1) == (iota((SIDE, SIDE), 0) % 2) * 16 + iota((SIDE, SIDE), 0) // 2).astype(BF16)
    edge = jnp.zeros((CUBES, ZD + 2, 64, 128), BF16)
    xa[:, :, :, 0:128] = edge
    xa[:, :, :, 1152:1280] = edge
    loads[2].wait()
    for b in range(CUBES):
        for z in range(ZD):
            xa[b, z + 1, :, 128:1152] = dot(spread_rows, x_ref[b, z]).astype(BF16)

    def x_windows(kt, planes):
        return jnp.concatenate([jnp.concatenate([
            xa[:, dz:dz + ZD, 16 * dy:16 * dy + 32, lanes(384 * kt + 128 * i, 256)].reshape(256, 256)
            for dz in planes for dy in range(3)
        ], axis=1) for i in range(3)], axis=0)

    @pl.loop(0, 3)
    def _(kt):
        part = dot(x_windows(kt, (1,)), ta[0:768])
        for i in range(3):
            ds_a[3 * kt + i] = part[256 * i:256 * i + 256]

    loads[3].wait()
    for b in range(CUBES):
        cs[b] = dot(spread_cot, cot_ref[b, 0]) * 0.125
    hb[:, :, :, :, 0:256] = jnp.zeros((CUBES, 4, 3, 16, 256), BF16)
    hb[:, :, :, :, 2304:2816] = jnp.zeros((CUBES, 4, 3, 16, 512), BF16)
    for copy in halo_x:
        copy.wait()
    for b in range(CUBES):
        xa[b, 0, :, 128:1152] = (dot(spread_rows, xh[0, b]) * keep_low).astype(BF16)
        xa[b, ZD + 1, :, 128:1152] = (dot(spread_rows, xh[1, b]) * keep_high).astype(BF16)

    @pl.loop(0, 3)
    def _(kt):
        part = dot(x_windows(kt, (0, 2)), ta[768:2304])
        for i in range(3):
            kk = 3 * kt + i
            pre = part[256 * i:256 * i + 256] + ds_a[kk]
            place = 2 * kk - 1 + (iota((1, 128), 1) // C2)
            inside = ((place >= 0) & (place < SIDE // 2)).astype(F32) * 0.125
            s = 0.5 * jnp.tanh(0.5 * pre) + 0.5
            act = pre * s
            slope = s + act * (1.0 - s)
            ds_a[kk] = slope * jnp.concatenate([inside, inside], axis=1)
            act = (act[:, :128] + act[:, 128:]).reshape(CUBES, 2, 2, 2, 16, 128)
            pooled = (act[:, :, 0, 0] + act[:, :, 0, 1] + act[:, :, 1, 0] + act[:, :, 1, 1]).reshape(64, 128) * inside
            for dy, v in enumerate((rows_before(pooled), pooled, rows_after(pooled))):
                pb[:, 1:3, dy, :, lanes(128 * kk, 128)] = v.astype(BF16).reshape(CUBES, 2, 16, 128)

        pooled_piece(kt, True)

    halo_p = [copy for kt in range(3) for copy in pooled_piece(kt, False)]

    @pl.loop(0, 9)
    def _(zy):
        base = zy * 256
        tap = taps_b(zy)
        for p in range(4):
            for q in range(2):
                tb[pl.ds(pl.multiple_of(base + 64 * p, 64), 64), 128 * q:128 * q + 128] = tap(p - 1 - q)

    def p_windows(planes):
        return jnp.concatenate([jnp.concatenate([
            pb[:, z, dy, :, 128 * k:128 * k + 256].reshape(32, 256) for z in planes for dy in range(3)
        ], axis=1) for k in range(8)], axis=0)

    window = p_windows((1, 2))
    pre_s[0] = dot(window, tb[768:2304])
    pre_s[1] = dot(window, tb[0:1536])

    @pl.loop(0, 9)
    def _(s):
        tap = taps_b(8 - s)
        for r in range(4):
            for p in range(6):
                tbd[64 * r:64 * r + 64, lanes(s * 768 + 128 * p, 128)] = tap(r + 1 - p)

    @pl.loop(0, 9)
    def _(s):
        two = taps_a(8 - s)
        sz = s // 3
        base = (jnp.where(sz == 2, 2, 1 - sz) * 3 + s % 3) * 768
        for r in range(8):
            for kk in range(3):
                for par in range(2):
                    dx = r + 2 - 4 * kk - par
                    tad[32 * r:32 * r + 32, lanes(base + 256 * kk + 128 * par, 128)] = two(dx, dx - 2)

    for copy in halo_p:
        copy.wait()
    for plane, way, keep in ((0, 0, keep_low), (3, 1, keep_high)):
        v = ph[way].astype(F32).reshape(32, 1152) * keep
        for dy, v in enumerate((rows_before(v), v, rows_after(v))):
            pb[:, plane, dy] = v.astype(BF16).reshape(CUBES, 16, 1152)

    for zp in range(2):
        pre = pre_s[zp] + dot(p_windows((3 * zp,)), tb[1536 * zp:1536 * zp + 768])
        s = 0.5 * jnp.tanh(0.5 * pre) + 0.5
        slope = s + pre * s * (1.0 - s)
        grads = []
        for k in range(8):
            up = cs[:, :, 128 * k:128 * k + 128].reshape(32, 128)
            h = slope[32 * k:32 * k + 32] * jnp.concatenate([up, up], axis=1)
            grads.append(h)
            for dy, v in enumerate((rows_before(h), h, rows_after(h))):
                hb[:, 1 + zp, dy, :, 256 + 256 * k:512 + 256 * k] = v.astype(BF16).reshape(CUBES, 16, 256)
        ht[:, 256 * zp:256 * zp + 256] = jnp.concatenate(grads, axis=0).astype(BF16).T

    halo_h = halo(1, hb.at[:, 1, 1, :, 256:2304], hb.at[:, 2, 1, :, 256:2304], lambda way: hh.at[way])

    for dz in range(3):
        window = jnp.concatenate([jnp.concatenate([
            pb[:, dz + zp, dy, :, 128 * k:128 * k + 256].reshape(32, 256) for zp in range(2) for k in range(8)
        ], axis=0) for dy in range(3)], axis=1)
        all_dy = dot(ht[...], window)
        for dy in range(3):
            full = all_dy[:, 256 * dy:256 * dy + 256]
            diag = full[:128] + pltpu.roll(full[128:], 192, 1)
            sb[dz * 576 + dy * 192:dz * 576 + dy * 192 + 192, :] = diag.astype(BF16).T[:192]

    sb[1728:ROWS_B, :] = jnp.zeros((ROWS_B - 1728, 128), BF16)
    hs[HALF_B:, :] = jnp.zeros((WIDE_B - HALF_B, 128), BF16)

    def shard(ref, n, index):
        rows = ref.shape[0] // n
        return ref.at[pl.ds(pl.multiple_of(index * rows, 16), rows), :]

    def scatter_copy(which, send, land, d):
        peer = lax.rem(me_z + d, n_gz)
        return pltpu.make_async_remote_copy(
            src_ref=shard(send, n_gz, peer), dst_ref=land.at[me_z],
            send_sem=rs_s.at[which, d], recv_sem=rs_r.at[which, d],
            device_id=(me_s, peer), device_id_type=MESH,
        )

    def sample_copy(which, land, d):
        peer = lax.rem(me_s + d, n_s)
        return pltpu.make_async_remote_copy(
            src_ref=land.at[me_s], dst_ref=land.at[me_s],
            send_sem=ex_s.at[which, d], recv_sem=ex_r.at[which, d],
            device_id=(peer, me_z), device_id_type=MESH,
        )

    def gather_copy(which, full, d):
        peer = lax.rem(me_z + d, n_gz)
        return pltpu.make_async_remote_copy(
            src_ref=shard(full, n_gz, me_z), dst_ref=shard(full, n_gz, me_z),
            send_sem=ag_s.at[which, d], recv_sem=ag_r.at[which, d],
            device_id=(me_s, peer), device_id_type=MESH,
        )

    def start_all(make, n):
        @pl.loop(1, n)
        def _(d):
            make(d).start()

    def wait_all(make, n):
        @pl.loop(1, n)
        def _(d):
            make(d).wait()

    def scatter_start(which, send, land):
        start_all(functools.partial(scatter_copy, which, send, land), n_gz)

    def scatter_end(which, send, land, exchange):
        wait_all(functools.partial(scatter_copy, which, send, land), n_gz)
        rows = send.shape[0] // n_gz
        own = send[pl.ds(pl.multiple_of(me_z * rows, 16), rows), :]
        land[me_z] = own
        total = land[0].astype(F32)
        for t in range(1, n_gz):
            total = total + land[t].astype(F32)
        exchange[me_s] = total.astype(BF16)
        start_all(functools.partial(sample_copy, which, exchange), n_s)

    def exchange_end(which, exchange, full):
        wait_all(functools.partial(sample_copy, which, exchange), n_s)
        total = exchange[0].astype(F32)
        for t in range(1, n_s):
            total = total + exchange[t].astype(F32)
        rows = full.shape[0] // n_gz
        full[pl.ds(pl.multiple_of(me_z * rows, 16), rows), :] = (total * (1.0 / (CUBES * n_s))).astype(BF16)
        start_all(functools.partial(gather_copy, which, full), n_gz)

    def half_of(ref, which):
        return ref.at[pl.ds(pl.multiple_of(which * HALF_B, 128), HALF_B), :]

    part = WIDE_B // n_gz

    def part_of(ref, t):
        return ref.at[pl.ds(pl.multiple_of(t * part, 64), part), :]

    def core_copy(stage, src, dst):
        return pltpu.make_async_remote_copy(
            src_ref=src, dst_ref=dst, send_sem=core_s.at[stage], recv_sem=core_r.at[stage],
            device_id=(me_s, me_z + 1 - 2 * core), device_id_type=MESH,
        )

    def group_copy(d):
        peer = lax.rem(mine + d, n_gz)
        return pltpu.make_async_remote_copy(
            src_ref=part_of(hs, peer), dst_ref=rb.at[mine], send_sem=rs_s.at[0, d], recv_sem=rs_r.at[0, d],
            device_id=in_group(peer), device_id_type=MESH,
        )

    def line_copy(d):
        return pltpu.make_async_remote_copy(
            src_ref=eb.at[last], dst_ref=eb.at[last], send_sem=ex_s.at[0, d], recv_sem=ex_r.at[0, d],
            device_id=in_line(lax.rem(last + d, n_e)), device_id_type=MESH,
        )

    def back_copy(d):
        return pltpu.make_async_remote_copy(
            src_ref=part_of(fh, mine), dst_ref=part_of(fh, mine), send_sem=ag_s.at[0, d], recv_sem=ag_r.at[0, d],
            device_id=in_group(lax.rem(mine + d, n_gz)), device_id_type=MESH,
        )

    def reduce_b0():
        swap = core_copy(0, half_of(sb, 1 - core), cb)
        swap.start()
        return swap

    def reduce_b1(swap):
        swap.wait()
        own = sb[pl.ds(pl.multiple_of(core * HALF_B, 128), HALF_B), :]
        hs[0:HALF_B] = (own.astype(F32) + cb[...].astype(F32)).astype(BF16)
        start_all(group_copy, n_gz)

    def reduce_b2():
        wait_all(group_copy, n_gz)
        rb[mine] = hs[pl.ds(pl.multiple_of(mine * part, 64), part), :]
        total = rb[0].astype(F32)
        for t in range(1, n_gz):
            total = total + rb[t].astype(F32)
        eb[last] = total.astype(BF16)
        start_all(line_copy, n_e)

    def reduce_b3():
        wait_all(line_copy, n_e)
        total = eb[0].astype(F32)
        for t in range(1, n_e):
            total = total + eb[t].astype(F32)
        fh[pl.ds(pl.multiple_of(mine * part, 64), part), :] = (total * (1.0 / (CUBES * n_s))).astype(BF16)
        start_all(back_copy, n_gz)

    def reduce_b4():
        wait_all(back_copy, n_gz)
        swap = core_copy(1, fh.at[0:HALF_B], fo)
        swap.start()
        wb32[pl.ds(pl.multiple_of(core * HALF_B, 128), HALF_B), :] = fh[0:HALF_B].astype(F32)
        return swap

    def reduce_b5(swap):
        swap.wait()
        wb32[pl.ds(pl.multiple_of((1 - core) * HALF_B, 128), HALF_B), :] = fo[...].astype(F32)

    swap = reduce_b0()

    def h_windows(planes):
        return jnp.concatenate([jnp.concatenate([
            hb[:, z, sy, :, 512 * j:512 * j + 768].reshape(32, 768) for z in planes for sy in range(3)
        ], axis=1) for j in range(5)], axis=0)

    window = h_windows((1, 2))
    gp_s[0] = dot_nt(window, tbd[:, 2304:6912])
    gp_s[1] = dot_nt(window, tbd[:, 0:4608])

    reduce_b1(swap)
    for copy in halo_h:
        copy.wait()
    for plane, way, keep in ((0, 0, keep_low), (3, 1, keep_high)):
        v = hh[way].astype(F32).reshape(32, 2048) * keep
        for dy, v in enumerate((rows_before(v), v, rows_after(v))):
            hb[:, plane, dy, :, 256:2304] = v.astype(BF16).reshape(CUBES, 16, 2048)

    for zp in range(2):
        gp_s[zp] = gp_s[zp] + dot_nt(h_windows((3 * zp,)), tbd[:, 4608 * zp:4608 * zp + 2304])

    def first_grad(kk):
        up = gp_s[:, pl.ds(pl.multiple_of((kk // 2) * 32, 32), 32), lanes(128 * (kk % 2), 128)]
        up = jnp.concatenate([up, up], axis=2).reshape(2, CUBES, 16, 256)
        g = []
        for b in range(CUBES):
            for zp in range(2):
                g.append((ds_a[kk, 128 * b + 64 * zp:128 * b + 64 * zp + 64].reshape(4, 16, 256) * up[zp, b][None]).reshape(64, 256))
        g = jnp.concatenate(g, axis=0)
        gt[:, lanes(256 * kk, 256)] = g.astype(BF16).T
        g = g.reshape(CUBES, ZD, 2, 16, 256)
        even = g[:, :, 0].reshape(128, 256)
        odd = g[:, :, 1].reshape(128, 256)
        for group, v in enumerate((rows_before(odd), even, odd, rows_after(even))):
            ga[:, 1:1 + ZD, 16 * group:16 * group + 16, lanes(256 * kk, 256)] = v.astype(BF16).reshape(CUBES, ZD, 16, 256)

    @pl.loop(0, 3)
    def _(kt):
        @pl.loop(0, 3)
        def _(i):
            first_grad(3 * kt + i)

        grad_piece(kt, True)

    halo_g = [copy for kt in range(3) for copy in grad_piece(kt, False)]

    def terms_a(dz):
        window = jnp.concatenate([jnp.concatenate([
            xa[:, dz:dz + ZD, 16 * dy:16 * dy + 32, 128 * kk:128 * kk + 256].reshape(256, 256)
            for kk in range(BLOCKS)
        ], axis=0) for dy in range(3)], axis=1)
        all_dy = dot(gt[...], window)
        for dy in range(3):
            full = all_dy[:, 256 * dy:256 * dy + 256]
            total = jnp.zeros((64, 256), F32)
            for par in range(2):
                for pair in range(2):
                    t = 2 * pair + par
                    at = 128 * par + 64 * pair
                    total = total + pltpu.roll(full[at:at + 64], 256 - 32 * (t + 1), 1)
            total = total[:, :128]
            da[dz * 288 + dy * 96:dz * 288 + dy * 96 + 96, :] = jnp.concatenate([total, total], axis=0).T[:96]

    for dz in range(3):
        terms_a(dz)

    half = iota((ROWS_A, 128), 1) < C2
    da[864:1024, :] = jnp.zeros((160, 128), F32)
    sa[...] = jnp.where(half, da[0:512], da[512:1024]).astype(BF16)
    scatter_start(1, sa, ra)
    stores = []

    def store(src, dst):
        copy = pltpu.make_async_copy(src, dst, store_s.at[len(stores)])
        copy.start()
        stores.append(copy)

    def g_windows(jj, planes):
        return jnp.concatenate([jnp.concatenate([
            ga[:, sz:sz + ZD, 16 * sy:16 * sy + 32, 1024 * jj + 512 * i:1024 * jj + 512 * i + 768].reshape(256, 768)
            for sz in planes for sy in range(3)
        ], axis=1) for i in range(2)], axis=0)

    def middle(jj):
        part = dot_nt(g_windows(jj, (1,)), tad[:, 0:2304])
        for i in range(2):
            ds_a[2 * jj + i] = part[256 * i:256 * i + 256]

    def cubes_grad(jj):
        part = dot_nt(g_windows(jj, (0, 2)), tad[:, 2304:6912])
        for i in range(2):
            total = (part[256 * i:256 * i + 256] + ds_a[2 * jj + i]).astype(BF16)
            for b in range(CUBES):
                for z in range(ZD):
                    at = 32 * (ZD * b + z)
                    dx_ref[b, z, :, 512 * jj + 256 * i:512 * jj + 256 * i + 256] = dot(natural, total[at:at + 32]).astype(BF16)

    middle(0)
    reduce_b2()
    middle(1)
    for copy in halo_g:
        copy.wait()
    for plane, way, keep in ((0, 0, keep_low), (ZD + 1, 1, keep_high)):
        even = gh[way, :, 0:16].astype(F32).reshape(32, 2304) * keep
        odd = gh[way, :, 16:32].astype(F32).reshape(32, 2304) * keep
        for group, v in enumerate((rows_before(odd), even, odd, rows_after(even))):
            ga[:, plane, 16 * group:16 * group + 16] = v.astype(BF16).reshape(CUBES, 16, 2304)


    cubes_grad(0)
    scatter_end(1, sa, ra, ea)
    reduce_b3()
    cubes_grad(1)
    store(dx_ref, dx_hbm)
    exchange_end(1, ea, fa)
    reduce_b5(reduce_b4())

    @pl.loop(0, C2)
    def _(i):
        gb_ref[:, lanes(128 * i, 128)] = wb32[pl.ds(i, 27, stride=C2), :].astype(BF16)

    store(gb_ref, gb_hbm)
    wait_all(functools.partial(gather_copy, 1, fa), n_gz)
    wa32[0:ROWS_A] = fa[...].astype(F32)
    first = iota((16, 128), 1) < C2

    @pl.loop(0, C1 // 2)
    def _(m):
        v = wa32[pl.ds(2 * m, 16, stride=C1), :]
        w = wa32[pl.ds(2 * m + 1, 16, stride=C1), :]
        ga_ref[0:16, lanes(128 * m, 128)] = jnp.where(first, v, pltpu.roll(w, C2, 1))
        ga_ref[16:27, lanes(128 * m, 128)] = jnp.where(first, pltpu.roll(v, C2, 1), w)[:11]

    store(ga_ref, ga_hbm)
    for copy in stores:
        copy.wait()


def pass_on(dx_in, ga_in, gb_in, dx_out, ga_out, gb_out, dx_ref, ga_ref, gb_ref, wide_ref, in_s, out_s):
    near, far = pl.ds(0, 4096), pl.ds(4096, 4096)
    pieces = [(dx_in.at[b], dx_ref.at[b], dx_out.at[b]) for b in range(CUBES)]
    pieces += [(gb_in.at[:, w], wide_ref.at[:, w], gb_out.at[:, w]) for w in (near, far)]
    pieces.append((ga_in, ga_ref, ga_out))
    given = [pltpu.make_async_copy(via, dst, out_s.at[i]) for i, (_, via, dst) in enumerate(pieces)]
    narrow = {2: near, 3: far}
    taken = [
        pltpu.make_async_copy(src, gb_ref.at[:, narrow[i]] if i in narrow else via, in_s.at[i])
        for i, (src, via, _) in enumerate(pieces)
    ]
    for copy in taken:
        copy.start()
    for i, (arrive, leave) in enumerate(zip(taken, given)):
        arrive.wait()
        if i in narrow:
            wide_ref[:, narrow[i]] = gb_ref[:, narrow[i]].astype(F32)
        leave.start()
    for copy in given:
        copy.wait()


def shards(n_s, n_gz, cubes, weight_a, weight_b, cotangent):
    dma = pltpu.SemaphoreType.DMA
    anywhere = pl.BlockSpec(memory_space=pl.ANY)
    ins = (cubes, weight_a, weight_b, cotangent)
    outs = (
        jax.ShapeDtypeStruct((CUBES, ZD, SIDE, SIDE * C1), BF16),
        jax.ShapeDtypeStruct((27, C1 * C2), F32),
        jax.ShapeDtypeStruct((27, C2 * C3), F32),
    )
    parts = outs[:2] + (jax.ShapeDtypeStruct((27, C2 * C3), BF16),)
    results = pl.pallas_call(
        functools.partial(kernel, n_s, n_gz),
        out_shape=parts,
        in_specs=[anywhere] * 4,
        out_specs=(anywhere,) * 3,
        scratch_shapes=[pltpu.VMEM(v.shape, v.dtype) for v in ins + parts] + [
            pltpu.VMEM((27 * C1, 128), F32),
            pltpu.VMEM((ROWS_B, 128), F32),
            pltpu.VMEM((CUBES, ZD + 2, 64, 1280), BF16),
            pltpu.VMEM((2304, 256), BF16),
            pltpu.VMEM((2304, 256), BF16),
            pltpu.VMEM((256, 6912), BF16),
            pltpu.VMEM((256, 6912), BF16),
            pltpu.VMEM((BLOCKS, 256, 256), F32),
            pltpu.VMEM((2, 256, 256), F32),
            pltpu.VMEM((2, 160, 256), F32),
            pltpu.VMEM((CUBES, 4, 3, 16, 1152), BF16),
            pltpu.VMEM((CUBES, 4, 3, 16, 2816), BF16),
            pltpu.VMEM((CUBES, ZD + 2, 64, 2304), BF16),
            pltpu.VMEM((256, 512), BF16),
            pltpu.VMEM((256, 2304), BF16),
            pltpu.VMEM((CUBES, 16, 1024), F32),
            pltpu.VMEM((1024, 128), F32),
            pltpu.VMEM((2, CUBES, SIDE, 1024), BF16),
            pltpu.VMEM((2, CUBES, 16, 1152), BF16),
            pltpu.VMEM((2, CUBES, 16, 2048), BF16),
            pltpu.VMEM((2, CUBES, 32, 2304), BF16),
            pltpu.VMEM((ROWS_B, 128), BF16),
            pltpu.VMEM((HALF_B, 128), BF16),
            pltpu.VMEM((WIDE_B, 128), BF16),
            pltpu.VMEM((n_gz, WIDE_B // n_gz, 128), BF16),
            pltpu.VMEM((n_s // 2, WIDE_B // n_gz, 128), BF16),
            pltpu.VMEM((WIDE_B, 128), BF16),
            pltpu.VMEM((HALF_B, 128), BF16),
            pltpu.VMEM((ROWS_A, 128), BF16),
            pltpu.VMEM((n_gz, ROWS_A // n_gz, 128), BF16),
            pltpu.VMEM((n_s, ROWS_A // n_gz, 128), BF16),
            pltpu.VMEM((ROWS_A, 128), BF16),
            dma((4,)), dma((3,)),
            dma((8, 2)), dma((8, 2)), dma((2,)), dma((2,)),
            dma((2, n_gz)), dma((2, n_gz)),
            dma((2, n_s)), dma((2, n_s)),
            dma((2, n_gz)), dma((2, n_gz)),
        ],
        compiler_params=pltpu.CompilerParams(
            collective_id=0, has_side_effects=True, vmem_limit_bytes=60 * 1024 * 1024
        ),
    )(*ins)
    return pl.pallas_call(
        pass_on,
        out_shape=outs,
        in_specs=[anywhere] * 3,
        out_specs=(anywhere,) * 3,
        scratch_shapes=[pltpu.VMEM(v.shape, v.dtype) for v in parts + outs[2:]] + [dma((5,)), dma((5,))],
    )(*results)


def solution(mesh):
    in_specs = (P("sample", "gz", None, None), P(), P(), P("sample", "gz", None, None))
    out_specs = (P("sample", "gz", None, None), P(), P())
    body = functools.partial(shards, mesh.shape["sample"], mesh.shape["gz"])
    return jax.shard_map(body, mesh=mesh, in_specs=in_specs, out_specs=out_specs, check_vma=False)
```

```python
import functools

import jax
import jax.numpy as jnp
from jax import lax
from jax.experimental import pallas as pl
from jax.experimental.pallas import tpu as pltpu
from jax.sharding import PartitionSpec as P

C1, C2, C3 = 32, 64, 128
SIDE = 32
ZD = 4
CUBES = 2
BLOCKS = 9
F32, BF16 = jnp.float32, jnp.bfloat16
MESH = pl.DeviceIdType.MESH
ROWS_B = 1792
HALF_B = 896
WIDE_B = 1024
ROWS_A = 512


def iota(shape, dim):
    return lax.broadcasted_iota(jnp.int32, shape, dim)


def dot(a, b):
    return lax.dot_general(a, b, (((1,), (0,)), ((), ())), preferred_element_type=F32)


def dot_nt(a, b):
    return lax.dot_general(a, b, (((1,), (1,)), ((), ())), preferred_element_type=F32)


def rows_before(v):
    return jnp.where(iota(v.shape, 0) % 16 == 0, 0.0, pltpu.roll(v, 1, 0))


def rows_after(v):
    return jnp.where(iota(v.shape, 0) % 16 == 15, 0.0, pltpu.roll(v, v.shape[0] - 1, 0))


def lanes(start, size):
    return pl.ds(pl.multiple_of(start, 128), size)


def kernel(
    n_s, n_gz, x_hbm, wa_hbm, wb_hbm, cot_hbm, dx_hbm, ga_hbm, gb_hbm,
    x_ref, wa_ref, wb_ref, cot_ref, dx_ref, ga_ref, gb_ref,
    wa32, wb32, xa, ta, tb, tad, tbd, ds_a, pre_s, gp_s, pb, hb, ga, ht, gt, cs, da,
    xh, ph, hh, gh, sb, cb, hs, rb, eb, fh, fo, sa, ra, ea, fa,
    load_s, store_s, halo_s, halo_r, core_s, core_r, rs_s, rs_r, ex_s, ex_r, ag_s, ag_r,
):
    me_s = lax.axis_index("sample")
    me_z = lax.axis_index("gz")
    low = lax.rem(me_z + n_gz - 1, n_gz)
    high = lax.rem(me_z + 1, n_gz)
    keep_low = (me_z > 0).astype(F32)
    keep_high = (me_z < n_gz - 1).astype(F32)

    core, y_lo, at_z = me_z % 2, (me_z // 2) % 2, me_z // 4
    at_x, y_hi = me_s // 2, me_s % 2
    n_e = n_s // 2
    mine = (core * at_x + (1 - core) * at_z) * 4 + y_hi * 2 + y_lo
    last = core * at_z + (1 - core) * at_x

    def in_group(t):
        a, y = t // 4, t % 4
        to_x = core * a + (1 - core) * at_x
        to_z = (1 - core) * a + core * at_z
        return (to_x * 2 + y // 2, to_z * 4 + (y % 2) * 2 + core)

    def in_line(e):
        to_x = core * at_x + (1 - core) * e
        to_z = (1 - core) * at_z + core * e
        return (to_x * 2 + y_hi, to_z * 4 + y_lo * 2 + core)

    barrier = pltpu.get_barrier_semaphore()

    @pl.loop(1, n_gz)
    def _(d):
        pl.semaphore_signal(barrier, inc=1, device_id=in_group(lax.rem(mine + d, n_gz)), device_id_type=MESH)

    @pl.loop(1, n_gz)
    def _(d):
        pl.semaphore_signal(barrier, inc=1, device_id=(me_s, lax.rem(me_z + d, n_gz)), device_id_type=MESH)

    @pl.loop(1, n_s)
    def _(d):
        pl.semaphore_signal(barrier, inc=1, device_id=(lax.rem(me_s + d, n_s), me_z), device_id_type=MESH)

    loads = [
        pltpu.make_async_copy(src, dst, load_s.at[i])
        for i, (src, dst) in enumerate(((wa_hbm, wa_ref), (wb_hbm, wb_ref), (x_hbm, x_ref), (cot_hbm, cot_ref)))
    ]
    for load in loads:
        load.start()

    def halo(stage, low_plane, high_plane, landing, start=True):
        pair = []
        for way, (src, peer) in enumerate(((high_plane, high), (low_plane, low))):
            copy = pltpu.make_async_remote_copy(
                src_ref=src, dst_ref=landing(way),
                send_sem=halo_s.at[stage, way], recv_sem=halo_r.at[stage, way],
                device_id=(me_s, peer), device_id_type=MESH,
            )
            if start:
                copy.start()
            pair.append(copy)
        return pair

    def pooled_piece(kt, start):
        w = lanes(384 * kt, 384)
        return halo(2 + kt, pb.at[:, 1, 1, :, w], pb.at[:, 2, 1, :, w], lambda way: ph.at[way, :, :, w], start)

    def grad_piece(kt, start):
        w = lanes(768 * kt, 768)
        return halo(5 + kt, ga.at[:, 1, 16:48, w], ga.at[:, ZD, 16:48, w], lambda way: gh.at[way, :, :, w], start)

    half = iota((27, 128), 1) < C2
    loads[0].wait()

    @pl.loop(0, C1 // 2)
    def _(m):
        v = wa_ref[:, lanes(128 * m, 128)].astype(F32)
        w = pltpu.roll(v, C2, 1)
        wa32[pl.ds(2 * m, 27, stride=C1), :] = jnp.where(half, v, w)
        wa32[pl.ds(2 * m + 1, 27, stride=C1), :] = jnp.where(half, w, v)

    loads[1].wait()

    @pl.loop(0, C2)
    def _(i):
        wb32[pl.ds(i, 27, stride=C2), :] = wb_ref[:, lanes(128 * i, 128)].astype(F32)

    pl.semaphore_wait(barrier, 2 * n_gz + n_s - 3)
    halo_x = halo(0, x_hbm.at[:, 0], x_hbm.at[:, ZD - 1], lambda way: xh.at[way])

    zero_a = jnp.zeros((C1, 128), BF16)
    zero_b = jnp.zeros((C2, 128), BF16)
    left = iota((C1, 128), 1) < C2

    def taps_a(zy):
        at = pl.multiple_of(zy * 3 * C1, C1)
        full = wa32[pl.ds(at, 3 * C1), :].astype(BF16)
        taps = [full[C1 * i:C1 * i + C1] for i in range(3)]

        def two(dx0, dx1):
            first = taps[dx0 + 1] if -1 <= dx0 <= 1 else zero_a
            second = taps[dx1 + 1] if -1 <= dx1 <= 1 else zero_a
            if first is second:
                return zero_a
            return jnp.where(left, first, second)

        return two

    def taps_b(zy):
        at = pl.multiple_of(zy * 3 * C2, C2)
        full = wb32[pl.ds(at, 3 * C2), :].astype(BF16)
        taps = [full[C2 * i:C2 * i + C2] for i in range(3)]
        return lambda dx: taps[dx + 1] if -1 <= dx <= 1 else zero_b

    @pl.loop(0, 9)
    def _(zy):
        dz = zy // 3
        base = (jnp.where(dz == 2, 2, 1 - dz) * 3 + zy % 3) * 256
        two = taps_a(zy)
        for p in range(8):
            for par in range(2):
                ta[pl.ds(pl.multiple_of(base + 32 * p, 32), 32), 128 * par:128 * par + 128] = two(p - 2 - par, p - 4 - par)

    spread_rows = (iota((64, SIDE), 1) == 2 * (iota((64, SIDE), 0) % 16) + iota((64, SIDE), 0) // 16 - 1).astype(BF16)
    spread_cot = (iota((16, 8), 0) // 2 == iota((16, 8), 1)).astype(BF16)
    natural = (iota((SIDE, SIDE), 1) == (iota((SIDE, SIDE), 0) % 2) * 16 + iota((SIDE, SIDE), 0) // 2).astype(BF16)
    edge = jnp.zeros((CUBES, ZD + 2, 64, 128), BF16)
    xa[:, :, :, 0:128] = edge
    xa[:, :, :, 1152:1280] = edge
    loads[2].wait()
    for b in range(CUBES):
        for z in range(ZD):
            xa[b, z + 1, :, 128:1152] = dot(spread_rows, x_ref[b, z]).astype(BF16)

    def x_windows(kt, planes):
        return jnp.concatenate([jnp.concatenate([
            xa[:, dz:dz + ZD, 16 * dy:16 * dy + 32, lanes(384 * kt + 128 * i, 256)].reshape(256, 256)
            for dz in planes for dy in range(3)
        ], axis=1) for i in range(3)], axis=0)

    @pl.loop(0, 3)
    def _(kt):
        part = dot(x_windows(kt, (1,)), ta[0:768])
        for i in range(3):
            ds_a[3 * kt + i] = part[256 * i:256 * i + 256]

    loads[3].wait()
    for b in range(CUBES):
        cs[b] = dot(spread_cot, cot_ref[b, 0]) * 0.125
    hb[:, :, :, :, 0:256] = jnp.zeros((CUBES, 4, 3, 16, 256), BF16)
    hb[:, :, :, :, 2304:2816] = jnp.zeros((CUBES, 4, 3, 16, 512), BF16)
    for copy in halo_x:
        copy.wait()
    for b in range(CUBES):
        xa[b, 0, :, 128:1152] = (dot(spread_rows, xh[0, b]) * keep_low).astype(BF16)
        xa[b, ZD + 1, :, 128:1152] = (dot(spread_rows, xh[1, b]) * keep_high).astype(BF16)

    @pl.loop(0, 3)
    def _(kt):
        part = dot(x_windows(kt, (0, 2)), ta[768:2304])
        for i in range(3):
            kk = 3 * kt + i
            pre = part[256 * i:256 * i + 256] + ds_a[kk]
            place = 2 * kk - 1 + (iota((1, 128), 1) // C2)
            inside = ((place >= 0) & (place < SIDE // 2)).astype(F32) * 0.125
            s = 0.5 * jnp.tanh(0.5 * pre) + 0.5
            act = pre * s
            slope = s + act * (1.0 - s)
            ds_a[kk] = slope * jnp.concatenate([inside, inside], axis=1)
            act = (act[:, :128] + act[:, 128:]).reshape(CUBES, 2, 2, 2, 16, 128)
            pooled = (act[:, :, 0, 0] + act[:, :, 0, 1] + act[:, :, 1, 0] + act[:, :, 1, 1]).reshape(64, 128) * inside
            for dy, v in enumerate((rows_before(pooled), pooled, rows_after(pooled))):
                pb[:, 1:3, dy, :, lanes(128 * kk, 128)] = v.astype(BF16).reshape(CUBES, 2, 16, 128)

        pooled_piece(kt, True)

    halo_p = [copy for kt in range(3) for copy in pooled_piece(kt, False)]

    @pl.loop(0, 9)
    def _(zy):
        base = zy * 256
        tap = taps_b(zy)
        for p in range(4):
            for q in range(2):
                tb[pl.ds(pl.multiple_of(base + 64 * p, 64), 64), 128 * q:128 * q + 128] = tap(p - 1 - q)

    def p_windows(planes):
        return jnp.concatenate([jnp.concatenate([
            pb[:, z, dy, :, 128 * k:128 * k + 256].reshape(32, 256) for z in planes for dy in range(3)
        ], axis=1) for k in range(8)], axis=0)

    window = p_windows((1, 2))
    pre_s[0] = dot(window, tb[768:2304])
    pre_s[1] = dot(window, tb[0:1536])

    @pl.loop(0, 9)
    def _(s):
        tap = taps_b(8 - s)
        for r in range(4):
            for p in range(6):
                tbd[64 * r:64 * r + 64, lanes(s * 768 + 128 * p, 128)] = tap(r + 1 - p)

    @pl.loop(0, 9)
    def _(s):
        two = taps_a(8 - s)
        sz = s // 3
        base = (jnp.where(sz == 2, 2, 1 - sz) * 3 + s % 3) * 768
        for r in range(8):
            for kk in range(3):
                for par in range(2):
                    dx = r + 2 - 4 * kk - par
                    tad[32 * r:32 * r + 32, lanes(base + 256 * kk + 128 * par, 128)] = two(dx, dx - 2)

    for copy in halo_p:
        copy.wait()
    for plane, way, keep in ((0, 0, keep_low), (3, 1, keep_high)):
        v = ph[way].astype(F32).reshape(32, 1152) * keep
        for dy, v in enumerate((rows_before(v), v, rows_after(v))):
            pb[:, plane, dy] = v.astype(BF16).reshape(CUBES, 16, 1152)

    for zp in range(2):
        pre = pre_s[zp] + dot(p_windows((3 * zp,)), tb[1536 * zp:1536 * zp + 768])
        s = 0.5 * jnp.tanh(0.5 * pre) + 0.5
        slope = s + pre * s * (1.0 - s)
        grads = []
        for k in range(8):
            up = cs[:, :, 128 * k:128 * k + 128].reshape(32, 128)
            h = slope[32 * k:32 * k + 32] * jnp.concatenate([up, up], axis=1)
            grads.append(h)
            for dy, v in enumerate((rows_before(h), h, rows_after(h))):
                hb[:, 1 + zp, dy, :, 256 + 256 * k:512 + 256 * k] = v.astype(BF16).reshape(CUBES, 16, 256)
        ht[:, 256 * zp:256 * zp + 256] = jnp.concatenate(grads, axis=0).astype(BF16).T

    halo_h = halo(1, hb.at[:, 1, 1, :, 256:2304], hb.at[:, 2, 1, :, 256:2304], lambda way: hh.at[way])

    for dz in range(3):
        window = jnp.concatenate([jnp.concatenate([
            pb[:, dz + zp, dy, :, 128 * k:128 * k + 256].reshape(32, 256) for zp in range(2) for k in range(8)
        ], axis=0) for dy in range(3)], axis=1)
        all_dy = dot(ht[...], window)
        for dy in range(3):
            full = all_dy[:, 256 * dy:256 * dy + 256]
            diag = full[:128] + pltpu.roll(full[128:], 192, 1)
            sb[dz * 576 + dy * 192:dz * 576 + dy * 192 + 192, :] = diag.astype(BF16).T[:192]

    sb[1728:ROWS_B, :] = jnp.zeros((ROWS_B - 1728, 128), BF16)
    hs[HALF_B:, :] = jnp.zeros((WIDE_B - HALF_B, 128), BF16)

    def shard(ref, n, index):
        rows = ref.shape[0] // n
        return ref.at[pl.ds(pl.multiple_of(index * rows, 16), rows), :]

    def scatter_copy(which, send, land, d):
        peer = lax.rem(me_z + d, n_gz)
        return pltpu.make_async_remote_copy(
            src_ref=shard(send, n_gz, peer), dst_ref=land.at[me_z],
            send_sem=rs_s.at[which, d], recv_sem=rs_r.at[which, d],
            device_id=(me_s, peer), device_id_type=MESH,
        )

    def sample_copy(which, land, d):
        peer = lax.rem(me_s + d, n_s)
        return pltpu.make_async_remote_copy(
            src_ref=land.at[me_s], dst_ref=land.at[me_s],
            send_sem=ex_s.at[which, d], recv_sem=ex_r.at[which, d],
            device_id=(peer, me_z), device_id_type=MESH,
        )

    def gather_copy(which, full, d):
        peer = lax.rem(me_z + d, n_gz)
        return pltpu.make_async_remote_copy(
            src_ref=shard(full, n_gz, me_z), dst_ref=shard(full, n_gz, me_z),
            send_sem=ag_s.at[which, d], recv_sem=ag_r.at[which, d],
            device_id=(me_s, peer), device_id_type=MESH,
        )

    def start_all(make, n):
        @pl.loop(1, n)
        def _(d):
            make(d).start()

    def wait_all(make, n):
        @pl.loop(1, n)
        def _(d):
            make(d).wait()

    def scatter_start(which, send, land):
        start_all(functools.partial(scatter_copy, which, send, land), n_gz)

    def scatter_end(which, send, land, exchange):
        wait_all(functools.partial(scatter_copy, which, send, land), n_gz)
        rows = send.shape[0] // n_gz
        own = send[pl.ds(pl.multiple_of(me_z * rows, 16), rows), :]
        land[me_z] = own
        total = land[0].astype(F32)
        for t in range(1, n_gz):
            total = total + land[t].astype(F32)
        exchange[me_s] = total.astype(BF16)
        start_all(functools.partial(sample_copy, which, exchange), n_s)

    def exchange_end(which, exchange, full):
        wait_all(functools.partial(sample_copy, which, exchange), n_s)
        total = exchange[0].astype(F32)
        for t in range(1, n_s):
            total = total + exchange[t].astype(F32)
        rows = full.shape[0] // n_gz
        full[pl.ds(pl.multiple_of(me_z * rows, 16), rows), :] = (total * (1.0 / (CUBES * n_s))).astype(BF16)
        start_all(functools.partial(gather_copy, which, full), n_gz)

    def half_of(ref, which):
        return ref.at[pl.ds(pl.multiple_of(which * HALF_B, 128), HALF_B), :]

    part = WIDE_B // n_gz

    def part_of(ref, t):
        return ref.at[pl.ds(pl.multiple_of(t * part, 64), part), :]

    def core_copy(stage, src, dst):
        return pltpu.make_async_remote_copy(
            src_ref=src, dst_ref=dst, send_sem=core_s.at[stage], recv_sem=core_r.at[stage],
            device_id=(me_s, me_z + 1 - 2 * core), device_id_type=MESH,
        )

    def group_copy(d):
        peer = lax.rem(mine + d, n_gz)
        return pltpu.make_async_remote_copy(
            src_ref=part_of(hs, peer), dst_ref=rb.at[mine], send_sem=rs_s.at[0, d], recv_sem=rs_r.at[0, d],
            device_id=in_group(peer), device_id_type=MESH,
        )

    def line_copy(d):
        return pltpu.make_async_remote_copy(
            src_ref=eb.at[last], dst_ref=eb.at[last], send_sem=ex_s.at[0, d], recv_sem=ex_r.at[0, d],
            device_id=in_line(lax.rem(last + d, n_e)), device_id_type=MESH,
        )

    def back_copy(d):
        return pltpu.make_async_remote_copy(
            src_ref=part_of(fh, mine), dst_ref=part_of(fh, mine), send_sem=ag_s.at[0, d], recv_sem=ag_r.at[0, d],
            device_id=in_group(lax.rem(mine + d, n_gz)), device_id_type=MESH,
        )

    def reduce_b0():
        swap = core_copy(0, half_of(sb, 1 - core), cb)
        swap.start()
        return swap

    def reduce_b1(swap):
        swap.wait()
        own = sb[pl.ds(pl.multiple_of(core * HALF_B, 128), HALF_B), :]
        hs[0:HALF_B] = (own.astype(F32) + cb[...].astype(F32)).astype(BF16)
        start_all(group_copy, n_gz)

    def reduce_b2():
        wait_all(group_copy, n_gz)
        rb[mine] = hs[pl.ds(pl.multiple_of(mine * part, 64), part), :]
        total = rb[0].astype(F32)
        for t in range(1, n_gz):
            total = total + rb[t].astype(F32)
        eb[last] = total.astype(BF16)
        start_all(line_copy, n_e)

    def reduce_b3():
        wait_all(line_copy, n_e)
        total = eb[0].astype(F32)
        for t in range(1, n_e):
            total = total + eb[t].astype(F32)
        fh[pl.ds(pl.multiple_of(mine * part, 64), part), :] = (total * (1.0 / (CUBES * n_s))).astype(BF16)
        start_all(back_copy, n_gz)

    def reduce_b4():
        wait_all(back_copy, n_gz)
        swap = core_copy(1, fh.at[0:HALF_B], fo)
        swap.start()
        wb32[pl.ds(pl.multiple_of(core * HALF_B, 128), HALF_B), :] = fh[0:HALF_B].astype(F32)
        return swap

    def reduce_b5(swap):
        swap.wait()
        wb32[pl.ds(pl.multiple_of((1 - core) * HALF_B, 128), HALF_B), :] = fo[...].astype(F32)

    swap = reduce_b0()

    def h_windows(planes):
        return jnp.concatenate([jnp.concatenate([
            hb[:, z, sy, :, 512 * j:512 * j + 768].reshape(32, 768) for z in planes for sy in range(3)
        ], axis=1) for j in range(5)], axis=0)

    window = h_windows((1, 2))
    gp_s[0] = dot_nt(window, tbd[:, 2304:6912])
    gp_s[1] = dot_nt(window, tbd[:, 0:4608])

    reduce_b1(swap)
    for copy in halo_h:
        copy.wait()
    for plane, way, keep in ((0, 0, keep_low), (3, 1, keep_high)):
        v = hh[way].astype(F32).reshape(32, 2048) * keep
        for dy, v in enumerate((rows_before(v), v, rows_after(v))):
            hb[:, plane, dy, :, 256:2304] = v.astype(BF16).reshape(CUBES, 16, 2048)

    for zp in range(2):
        gp_s[zp] = gp_s[zp] + dot_nt(h_windows((3 * zp,)), tbd[:, 4608 * zp:4608 * zp + 2304])

    def first_grad(kk):
        up = gp_s[:, pl.ds(pl.multiple_of((kk // 2) * 32, 32), 32), lanes(128 * (kk % 2), 128)]
        up = jnp.concatenate([up, up], axis=2).reshape(2, CUBES, 16, 256)
        g = []
        for b in range(CUBES):
            for zp in range(2):
                g.append((ds_a[kk, 128 * b + 64 * zp:128 * b + 64 * zp + 64].reshape(4, 16, 256) * up[zp, b][None]).reshape(64, 256))
        g = jnp.concatenate(g, axis=0)
        gt[:, lanes(256 * kk, 256)] = g.astype(BF16).T
        g = g.reshape(CUBES, ZD, 2, 16, 256)
        even = g[:, :, 0].reshape(128, 256)
        odd = g[:, :, 1].reshape(128, 256)
        for group, v in enumerate((rows_before(odd), even, odd, rows_after(even))):
            ga[:, 1:1 + ZD, 16 * group:16 * group + 16, lanes(256 * kk, 256)] = v.astype(BF16).reshape(CUBES, ZD, 16, 256)

    @pl.loop(0, 3)
    def _(kt):
        @pl.loop(0, 3)
        def _(i):
            first_grad(3 * kt + i)

        grad_piece(kt, True)

    halo_g = [copy for kt in range(3) for copy in grad_piece(kt, False)]

    def terms_a(dz):
        window = jnp.concatenate([jnp.concatenate([
            xa[:, dz:dz + ZD, 16 * dy:16 * dy + 32, 128 * kk:128 * kk + 256].reshape(256, 256)
            for kk in range(BLOCKS)
        ], axis=0) for dy in range(3)], axis=1)
        all_dy = dot(gt[...], window)
        for dy in range(3):
            full = all_dy[:, 256 * dy:256 * dy + 256]
            total = jnp.zeros((64, 256), F32)
            for par in range(2):
                for pair in range(2):
                    t = 2 * pair + par
                    at = 128 * par + 64 * pair
                    total = total + pltpu.roll(full[at:at + 64], 256 - 32 * (t + 1), 1)
            total = total[:, :128]
            da[dz * 288 + dy * 96:dz * 288 + dy * 96 + 96, :] = jnp.concatenate([total, total], axis=0).T[:96]

    for dz in range(3):
        terms_a(dz)

    half = iota((ROWS_A, 128), 1) < C2
    da[864:1024, :] = jnp.zeros((160, 128), F32)
    sa[...] = jnp.where(half, da[0:512], da[512:1024]).astype(BF16)
    scatter_start(1, sa, ra)
    stores = []

    def store(src, dst):
        copy = pltpu.make_async_copy(src, dst, store_s.at[len(stores)])
        copy.start()
        stores.append(copy)

    def g_windows(jj, planes):
        return jnp.concatenate([jnp.concatenate([
            ga[:, sz:sz + ZD, 16 * sy:16 * sy + 32, 1024 * jj + 512 * i:1024 * jj + 512 * i + 768].reshape(256, 768)
            for sz in planes for sy in range(3)
        ], axis=1) for i in range(2)], axis=0)

    def middle(jj):
        part = dot_nt(g_windows(jj, (1,)), tad[:, 0:2304])
        for i in range(2):
            ds_a[2 * jj + i] = part[256 * i:256 * i + 256]

    def cubes_grad(jj):
        part = dot_nt(g_windows(jj, (0, 2)), tad[:, 2304:6912])
        for i in range(2):
            total = (part[256 * i:256 * i + 256] + ds_a[2 * jj + i]).astype(BF16)
            for b in range(CUBES):
                for z in range(ZD):
                    at = 32 * (ZD * b + z)
                    dx_ref[b, z, :, 512 * jj + 256 * i:512 * jj + 256 * i + 256] = dot(natural, total[at:at + 32]).astype(BF16)

    middle(0)
    reduce_b2()
    middle(1)
    for copy in halo_g:
        copy.wait()
    for plane, way, keep in ((0, 0, keep_low), (ZD + 1, 1, keep_high)):
        even = gh[way, :, 0:16].astype(F32).reshape(32, 2304) * keep
        odd = gh[way, :, 16:32].astype(F32).reshape(32, 2304) * keep
        for group, v in enumerate((rows_before(odd), even, odd, rows_after(even))):
            ga[:, plane, 16 * group:16 * group + 16] = v.astype(BF16).reshape(CUBES, 16, 2304)


    cubes_grad(0)
    scatter_end(1, sa, ra, ea)
    reduce_b3()
    cubes_grad(1)
    store(dx_ref, dx_hbm)
    exchange_end(1, ea, fa)
    reduce_b5(reduce_b4())

    @pl.loop(0, C2)
    def _(i):
        gb_ref[:, lanes(128 * i, 128)] = wb32[pl.ds(i, 27, stride=C2), :].astype(BF16)

    store(gb_ref, gb_hbm)
    wait_all(functools.partial(gather_copy, 1, fa), n_gz)
    wa32[0:ROWS_A] = fa[...].astype(F32)
    first = iota((16, 128), 1) < C2

    @pl.loop(0, C1 // 2)
    def _(m):
        v = wa32[pl.ds(2 * m, 16, stride=C1), :]
        w = wa32[pl.ds(2 * m + 1, 16, stride=C1), :]
        ga_ref[0:16, lanes(128 * m, 128)] = jnp.where(first, v, pltpu.roll(w, C2, 1))
        ga_ref[16:27, lanes(128 * m, 128)] = jnp.where(first, pltpu.roll(v, C2, 1), w)[:11]

    store(ga_ref, ga_hbm)
    for copy in stores:
        copy.wait()


def pass_on(dx_in, ga_in, gb_in, dx_out, ga_out, gb_out, dx_ref, ga_ref, gb_ref, wide_ref, in_s, out_s):
    near, far = pl.ds(0, 4096), pl.ds(4096, 4096)
    pieces = [(dx_in.at[b], dx_ref.at[b], dx_out.at[b]) for b in range(CUBES)]
    pieces += [(gb_in.at[:, w], wide_ref.at[:, w], gb_out.at[:, w]) for w in (near, far)]
    pieces.append((ga_in, ga_ref, ga_out))
    given = [pltpu.make_async_copy(via, dst, out_s.at[i]) for i, (_, via, dst) in enumerate(pieces)]
    narrow = {2: near, 3: far}
    taken = [
        pltpu.make_async_copy(src, gb_ref.at[:, narrow[i]] if i in narrow else via, in_s.at[i])
        for i, (src, via, _) in enumerate(pieces)
    ]
    for copy in taken:
        copy.start()
    for i, (arrive, leave) in enumerate(zip(taken, given)):
        arrive.wait()
        if i in narrow:
            wide_ref[:, narrow[i]] = gb_ref[:, narrow[i]].astype(F32)
        leave.start()
    for copy in given:
        copy.wait()


def shards(n_s, n_gz, cubes, weight_a, weight_b, cotangent):
    dma = pltpu.SemaphoreType.DMA
    anywhere = pl.BlockSpec(memory_space=pl.ANY)
    ins = (cubes, weight_a, weight_b, cotangent)
    outs = (
        jax.ShapeDtypeStruct((CUBES, ZD, SIDE, SIDE * C1), BF16),
        jax.ShapeDtypeStruct((27, C1 * C2), F32),
        jax.ShapeDtypeStruct((27, C2 * C3), F32),
    )
    parts = outs[:2] + (jax.ShapeDtypeStruct((27, C2 * C3), BF16),)
    results = pl.pallas_call(
        functools.partial(kernel, n_s, n_gz),
        out_shape=parts,
        in_specs=[anywhere] * 4,
        out_specs=(anywhere,) * 3,
        scratch_shapes=[pltpu.VMEM(v.shape, v.dtype) for v in ins + parts] + [
            pltpu.VMEM((32 * C1, 128), F32),
            pltpu.VMEM((32 * C2, 128), F32),
            pltpu.VMEM((CUBES, ZD + 2, 64, 1280), BF16),
            pltpu.VMEM((2304, 256), BF16),
            pltpu.VMEM((2304, 256), BF16),
            pltpu.VMEM((256, 6912), BF16),
            pltpu.VMEM((256, 6912), BF16),
            pltpu.VMEM((BLOCKS, 256, 256), F32),
            pltpu.VMEM((2, 256, 256), F32),
            pltpu.VMEM((2, 160, 256), F32),
            pltpu.VMEM((CUBES, 4, 3, 16, 1152), BF16),
            pltpu.VMEM((CUBES, 4, 3, 16, 2816), BF16),
            pltpu.VMEM((CUBES, ZD + 2, 64, 2304), BF16),
            pltpu.VMEM((256, 512), BF16),
            pltpu.VMEM((256, 2304), BF16),
            pltpu.VMEM((CUBES, 16, 1024), F32),
            pltpu.VMEM((1024, 128), F32),
            pltpu.VMEM((2, CUBES, SIDE, 1024), BF16),
            pltpu.VMEM((2, CUBES, 16, 1152), BF16),
            pltpu.VMEM((2, CUBES, 16, 2048), BF16),
            pltpu.VMEM((2, CUBES, 32, 2304), BF16),
            pltpu.VMEM((ROWS_B, 128), BF16),
            pltpu.VMEM((HALF_B, 128), BF16),
            pltpu.VMEM((WIDE_B, 128), BF16),
            pltpu.VMEM((n_gz, WIDE_B // n_gz, 128), BF16),
            pltpu.VMEM((n_s // 2, WIDE_B // n_gz, 128), BF16),
            pltpu.VMEM((WIDE_B, 128), BF16),
            pltpu.VMEM((HALF_B, 128), BF16),
            pltpu.VMEM((ROWS_A, 128), BF16),
            pltpu.VMEM((n_gz, ROWS_A // n_gz, 128), BF16),
            pltpu.VMEM((n_s, ROWS_A // n_gz, 128), BF16),
            pltpu.VMEM((ROWS_A, 128), BF16),
            dma((4,)), dma((3,)),
            dma((8, 2)), dma((8, 2)), dma((2,)), dma((2,)),
            dma((2, n_gz)), dma((2, n_gz)),
            dma((2, n_s)), dma((2, n_s)),
            dma((2, n_gz)), dma((2, n_gz)),
        ],
        compiler_params=pltpu.CompilerParams(
            collective_id=0, has_side_effects=True, vmem_limit_bytes=60 * 1024 * 1024
        ),
    )(*ins)
    return pl.pallas_call(
        pass_on,
        out_shape=outs,
        in_specs=[anywhere] * 3,
        out_specs=(anywhere,) * 3,
        scratch_shapes=[pltpu.VMEM(v.shape, v.dtype) for v in parts + outs[2:]] + [dma((5,)), dma((5,))],
    )(*results)


def solution(mesh):
    in_specs = (P("sample", "gz", None, None), P(), P(), P("sample", "gz", None, None))
    out_specs = (P("sample", "gz", None, None), P(), P())
    body = functools.partial(shards, mesh.shape["sample"], mesh.shape["gz"])
    return jax.shard_map(body, mesh=mesh, in_specs=in_specs, out_specs=out_specs, check_vma=False)
```
